256 devices in a mesh: seq: 8 (over x, core), head: 8 (over z), dp: 4 (over y).
Axes of the slice: x: 4, y: 4, z: 8, core: 2. Of those that a mesh axis runs over, the one named last changes fastest.
Arguments:
- layer_input: bfloat16 [4, 4096, 2048], P('dp', 'seq'), may hold values from -6 to 6
- w_query: bfloat16 [2048, 2048], P(None, 'head'), may hold values from -0.125 to 0.125
- w_key: bfloat16 [2048, 2048], P(None, 'head'), may hold values from -0.125 to 0.125
- w_value: bfloat16 [2048, 2048], P(None, 'head'), may hold values from -0.125 to 0.125
- w_out: bfloat16 [2048, 2048], P('head'), may hold values from -0.125 to 0.125
- out_grad: bfloat16 [4, 4096, 2048], P('dp', 'seq'), may hold values from -6 to 6
Outputs:
- input_grad: bfloat16 [4, 4096, 2048], P('dp', 'seq', 'head')
- grad_query: float32 [2048, 2048], P(('seq', 'dp'), 'head')
- grad_key: float32 [2048, 2048], P(('seq', 'dp'), 'head')
- grad_value: float32 [2048, 2048], P(('seq', 'dp'), 'head')
- grad_out: float32 [2048, 2048], P('head', ('seq', 'dp'))
The draws below stay inside these ranges and needn't reach their ends.
All inputs are finite; a program needn't handle non-finite values.
Results may differ from the reference program's by a relative error of at most 0.0073.
Values sent between devices are 32-bit elements; how exact they have to be, the bound alone decides.
A program may use at most 64 MiB of HBM per device.

```python
import jax
import jax.numpy as jnp
from jax import lax

D = 2048
HEADS = 16
HEAD_DIM = 128
TOK_DEV = 512
SEQS = 4
LENGTH = 4096
HD = 2048
N_SEQ = 8


def raised(entries, rng, source, target, shards_of, factor):
    def block_of(axis_at):
        return (jnp.arange(entries.shape[axis_at]) // (entries.shape[axis_at] // shards_of)).reshape((-1,) + (1,) * (entries.ndim - 1 - axis_at))

    near = jax.random.permutation(rng, shards_of)[block_of(target)]
    other_side = (block_of(target) + shards_of // 2) % shards_of
    return jnp.where((block_of(source) == near) | (block_of(source) == other_side), factor * entries, entries)


def block_levels(key, dims, cuts, low, high):
    def one(axis_at, parts):
        draws = jax.random.uniform(jax.random.fold_in(jax.random.fold_in(key, 6), axis_at), (parts,), jnp.float32, low / len(cuts), high / len(cuts))
        return jnp.repeat(jnp.exp(draws), dims[axis_at] // parts).reshape((-1,) + (1,) * (len(dims) - axis_at - 1))

    factor_of = one(*cuts[0])
    for cut in cuts[1:]:
        factor_of = factor_of * one(*cut)
    return factor_of


def gaussian(key, extent, width, bound, pieces=(), held_as=jnp.bfloat16):
    factor_of = block_levels(key, extent, pieces, -0.22, 0.18) if pieces else 1.0
    drawn = jax.random.normal(key, extent, jnp.float32) * width * factor_of
    return jnp.minimum(jnp.maximum(drawn, -bound), bound).astype(held_as)


def noise_with(key, shape, width, reach, shards, heavy, kind=jnp.bfloat16):
    drawn = width * jax.random.normal(key, shape, jnp.float32)
    if shards:
        drawn = drawn * block_levels(key, shape, shards, -0.22, 0.18)
    return jnp.clip(raised(drawn, jax.random.fold_in(key, 3), *heavy), -reach, reach).astype(kind)


def setup_inputs(seed: int = 0) -> dict:
    key_of = jax.random.split(jax.random.key(seed), 7)
    layer_input = noise_with(key_of[0], (SEQS, LENGTH, D), 1.0, 6.0, ((0, 4), (1, 8)), (1, 2, 8, 2.0))
    w_query = gaussian(key_of[1], (D, HD), D ** -0.5, 0.125, ((1, 8),))
    w_key = gaussian(key_of[2], (D, HD), D ** -0.5, 0.125, ((1, 8),))
    w_value = gaussian(key_of[3], (D, HD), D ** -0.5, 0.125, ((1, 8),))
    w_out = gaussian(key_of[4], (HD, D), HD ** -0.5, 0.125, ((0, 8),))
    out_grad = noise_with(key_of[5], (SEQS, LENGTH, D), 1.0, 6.0, ((0, 4), (1, 8)), (1, 2, 8, 2.0))
    return dict(layer_input=layer_input, w_query=w_query, w_key=w_key, w_value=w_value, w_out=w_out, out_grad=out_grad)


def widen_float(array_in):
    return array_in.astype(jnp.float32)

def reference(layer_input, w_query, w_key, w_value, w_out, out_grad):
    precise = lax.Precision.HIGHEST
    num_blocks = N_SEQ
    block_len = TOK_DEV
    in_rows = layer_input.reshape(-1, D)
    grad_rows = out_grad.reshape(-1, D)

    def project(weight):
        result = jnp.dot(in_rows, weight, preferred_element_type=jnp.float32).astype(jnp.bfloat16)
        return result.reshape(SEQS, num_blocks, block_len, HEADS, HEAD_DIM)
    queries = project(w_query)
    key_rows = project(w_key)
    value_rows = project(w_value)
    positions = jnp.arange(LENGTH, dtype=jnp.float32)
    pos_scale = (1.0 / jnp.sqrt(HEAD_DIM * (positions + 1.0))).reshape(num_blocks, block_len)
    backward = jnp.dot(grad_rows, w_out.T, preferred_element_type=jnp.float32).reshape(SEQS, num_blocks, block_len, HEADS, HEAD_DIM)
    grad_in = (backward * pos_scale[None, :, :, None, None]).astype(jnp.bfloat16)
    kv_state = jnp.einsum('bntkd,bntke->bnkde', widen_float(key_rows), widen_float(value_rows), precision=precise)
    qg_state = jnp.einsum('bntkd,bntke->bnkde', widen_float(queries), widen_float(grad_in), precision=precise)
    prefix = (jnp.cumsum(kv_state, axis=1) - kv_state).astype(jnp.bfloat16)
    suffix = (lax.optimization_barrier(jnp.sum(qg_state, axis=1, keepdims=True)) - jnp.cumsum(qg_state, axis=1)).astype(jnp.bfloat16)
    causal = jnp.arange(block_len)[:, None] >= jnp.arange(block_len)[None, :]

    def one_block(block_item):
        q_block, k_block, v_block, g_block, p_block, r_block, s_block = block_item
        scores = jnp.einsum('thd,shd->hts', widen_float(q_block), widen_float(k_block), precision=precise)
        scores_qk = jnp.where(causal[None], scores, 0.0).astype(jnp.bfloat16)
        scores_g = jnp.einsum('thd,shd->hts', widen_float(g_block), widen_float(v_block), precision=precise)
        scores_gv = jnp.where(causal[None], scores_g, 0.0).astype(jnp.bfloat16)
        inner_sum = jnp.einsum('hts,she->the', widen_float(scores_qk), widen_float(v_block), precision=precise)
        cross_sum = jnp.einsum('thd,hde->the', widen_float(q_block), widen_float(p_block), precision=precise)
        attention = ((inner_sum + cross_sum) * s_block[:, None, None]).astype(jnp.bfloat16)
        d_query = jnp.einsum('hts,shd->thd', widen_float(scores_gv), widen_float(k_block), precision=precise) + jnp.einsum('the,hde->thd', widen_float(g_block), widen_float(p_block), precision=precise)
        d_keys = jnp.einsum('hts,thd->shd', widen_float(scores_gv), widen_float(q_block), precision=precise) + jnp.einsum('she,hde->shd', widen_float(v_block), widen_float(r_block), precision=precise)
        d_values = jnp.einsum('hts,the->she', widen_float(scores_qk), widen_float(g_block), precision=precise) + jnp.einsum('shd,hde->she', widen_float(k_block), widen_float(r_block), precision=precise)
        return (attention, d_query.astype(jnp.bfloat16), d_keys.astype(jnp.bfloat16), d_values.astype(jnp.bfloat16))
    item_count = SEQS * num_blocks
    all_scales = jnp.broadcast_to(pos_scale[None], (SEQS, num_blocks, block_len)).reshape(item_count, block_len)
    block_items = (queries.reshape(item_count, block_len, HEADS, HEAD_DIM), key_rows.reshape(item_count, block_len, HEADS, HEAD_DIM), value_rows.reshape(item_count, block_len, HEADS, HEAD_DIM), grad_in.reshape(item_count, block_len, HEADS, HEAD_DIM), prefix.reshape(item_count, HEADS, HEAD_DIM, HEAD_DIM), suffix.reshape(item_count, HEADS, HEAD_DIM, HEAD_DIM), all_scales)
    attention, d_query, d_keys, d_values = lax.map(one_block, block_items)
    attention = attention.reshape(-1, HD)
    d_query = d_query.reshape(-1, HD)
    d_keys = d_keys.reshape(-1, HD)
    d_values = d_values.reshape(-1, HD)
    summed_in = jnp.dot(d_query, w_query.T, preferred_element_type=jnp.float32)
    summed_in = summed_in + jnp.dot(d_keys, w_key.T, preferred_element_type=jnp.float32)
    summed_in = summed_in + jnp.dot(d_values, w_value.T, preferred_element_type=jnp.float32)
    input_grad = summed_in.astype(jnp.bfloat16).reshape(SEQS, LENGTH, D)
    grad_scale = jnp.float32(1.0) / jnp.sqrt(jnp.float32(SEQS * LENGTH))
    in_rows_t = in_rows.T
    grad_query = jnp.dot(in_rows_t, d_query, preferred_element_type=jnp.float32) * grad_scale
    grad_key = jnp.dot(in_rows_t, d_keys, preferred_element_type=jnp.float32) * grad_scale
    grad_value = jnp.dot(in_rows_t, d_values, preferred_element_type=jnp.float32) * grad_scale
    grad_out = jnp.dot(attention.T, grad_rows, preferred_element_type=jnp.float32) * grad_scale
    return (input_grad, grad_query, grad_key, grad_value, grad_out)
```

```python
import jax
import jax.numpy as jnp
from jax import lax
from jax.sharding import PartitionSpec as P

HEAD_DIM = 128


def local(layer_input, w_query, w_key, w_value, w_out, out_grad):
    num_rows = layer_input.shape[1]
    local_heads = w_query.shape[1] // HEAD_DIM
    width = local_heads * HEAD_DIM
    in_rows = layer_input[0]
    grad_rows = out_grad[0]

    def project(weight):
        result = jnp.dot(in_rows, weight, preferred_element_type=jnp.float32).astype(jnp.bfloat16)
        return result.reshape(num_rows, local_heads, HEAD_DIM)

    queries = project(w_query)
    key_rows = project(w_key)
    value_rows = project(w_value)
    here = lax.axis_index("seq")
    peers = lax.axis_size("seq")
    row_start = here * num_rows
    positions = (row_start + jnp.arange(num_rows, dtype=jnp.int32)).astype(jnp.float32)
    pos_scale = 1.0 / jnp.sqrt(HEAD_DIM * (positions + 1.0))
    backward = jnp.einsum("td,kd->tk", grad_rows, w_out, preferred_element_type=jnp.float32)
    grad_in = (
        (backward * pos_scale[:, None])
        .astype(jnp.bfloat16)
        .reshape(num_rows, local_heads, HEAD_DIM)
    )
    kv_state = jnp.einsum("thd,the->hde", key_rows, value_rows, preferred_element_type=jnp.float32)
    qg_state = jnp.einsum("thd,the->hde", queries, grad_in, preferred_element_type=jnp.float32)
    states = lax.all_gather(jnp.stack([kv_state, qg_state]), "seq")
    blocks = jnp.arange(peers)[:, None, None, None]
    prefix = jnp.sum(jnp.where(blocks < here, states[:, 0], 0.0), axis=0).astype(jnp.bfloat16)
    suffix = jnp.sum(jnp.where(blocks > here, states[:, 1], 0.0), axis=0).astype(jnp.bfloat16)
    causal = (jnp.arange(num_rows)[:, None] >= jnp.arange(num_rows)[None, :])[None]
    scores = jnp.einsum("thd,shd->hts", queries, key_rows, preferred_element_type=jnp.float32)
    scores_qk = jnp.where(causal, scores, 0.0).astype(jnp.bfloat16)
    scores_g = jnp.einsum("thd,shd->hts", grad_in, value_rows, preferred_element_type=jnp.float32)
    scores_gv = jnp.where(causal, scores_g, 0.0).astype(jnp.bfloat16)
    inner_sum = jnp.einsum(
        "hts,she->the", scores_qk, value_rows, preferred_element_type=jnp.float32
    )
    cross_sum = jnp.einsum("thd,hde->the", queries, prefix, preferred_element_type=jnp.float32)
    attention = (
        ((inner_sum + cross_sum) * pos_scale[:, None, None])
        .astype(jnp.bfloat16)
        .reshape(num_rows, width)
    )
    d_query = jnp.einsum("hts,shd->thd", scores_gv, key_rows, preferred_element_type=jnp.float32)
    d_query = d_query + jnp.einsum(
        "the,hde->thd", grad_in, prefix, preferred_element_type=jnp.float32
    )
    d_keys = jnp.einsum("hts,thd->shd", scores_gv, queries, preferred_element_type=jnp.float32)
    d_keys = d_keys + jnp.einsum(
        "she,hde->shd", value_rows, suffix, preferred_element_type=jnp.float32
    )
    d_values = jnp.einsum("hts,the->she", scores_qk, grad_in, preferred_element_type=jnp.float32)
    d_values = d_values + jnp.einsum(
        "shd,hde->she", key_rows, suffix, preferred_element_type=jnp.float32
    )
    d_query = d_query.astype(jnp.bfloat16).reshape(num_rows, width)
    d_keys = d_keys.astype(jnp.bfloat16).reshape(num_rows, width)
    d_values = d_values.astype(jnp.bfloat16).reshape(num_rows, width)
    head_terms = jnp.einsum("tk,dk->td", d_query, w_query, preferred_element_type=jnp.float32)
    head_terms = head_terms + jnp.einsum(
        "tk,dk->td", d_keys, w_key, preferred_element_type=jnp.float32
    )
    head_terms = head_terms + jnp.einsum(
        "tk,dk->td", d_values, w_value, preferred_element_type=jnp.float32
    )
    input_grad = lax.psum_scatter(head_terms, "head", scatter_dimension=1, tiled=True).astype(
        jnp.bfloat16
    )[None]
    total_rows = lax.axis_size("seq") * lax.axis_size("dp") * num_rows
    grad_scale = jnp.float32(1.0) / jnp.sqrt(jnp.float32(total_rows))
    grads = jnp.concatenate([d_query, d_keys, d_values], axis=1)
    term_qkv = jnp.einsum("td,tk->dk", in_rows, grads, preferred_element_type=jnp.float32)
    term_out = jnp.einsum("td,tk->dk", grad_rows, attention, preferred_element_type=jnp.float32)
    terms = jnp.concatenate([term_qkv, term_out], axis=1) * grad_scale
    summed = lax.psum_scatter(terms, "seq", scatter_dimension=0, tiled=True)
    summed = lax.psum_scatter(summed, "dp", scatter_dimension=0, tiled=True)
    grad_query = summed[:, :width]
    grad_key = summed[:, width:2 * width]
    grad_value = summed[:, 2 * width:3 * width]
    grad_out = summed[:, 3 * width:].T
    return (input_grad, grad_query, grad_key, grad_value, grad_out)


def solution(mesh):
    return jax.shard_map(
        local,
        mesh=mesh,
        in_specs=(
            P("dp", "seq", None),
            P(None, "head"),
            P(None, "head"),
            P(None, "head"),
            P("head", None),
            P("dp", "seq", None),
        ),
        out_specs=(
            P("dp", "seq", "head"),
            P(("seq", "dp"), "head"),
            P(("seq", "dp"), "head"),
            P(("seq", "dp"), "head"),
            P("head", ("seq", "dp")),
        ),
        check_vma=False,
    )
```

```python
import functools

import jax
import jax.numpy as jnp
from jax import lax
from jax.experimental import pallas as pl
from jax.experimental.pallas import tpu as pltpu
from jax.sharding import PartitionSpec as P

HEAD_DIM = 128
MESH = pl.DeviceIdType.MESH


def ring_scatter_kernel(n, term_ref, out_ref, recv, sendbuf, send_sem, recv_sem):
    me = lax.axis_index("head")
    right, left = lax.rem(me + 1, n), lax.rem(me + n - 1, n)
    half = out_ref.shape[1] // 2
    barrier = pltpu.get_barrier_semaphore()
    for neighbour in (left, right):
        pl.semaphore_signal(barrier, inc=1, device_id={"head": neighbour}, device_id_type=MESH)
    pl.semaphore_wait(barrier, 2)
    routes = ((right, -1), (left, 1))
    copies = [[], []]
    for step in range(n - 1):
        for way, (dest, sign) in enumerate(routes):
            block = lax.rem(me + n + sign * (step + 1), n)
            cols = pl.ds(way * half, half)
            if step == 0:
                src = term_ref.at[block, :, cols]
            else:
                copies[way][step - 1].wait_recv()
                sendbuf[way, step] = recv[way, step - 1] + term_ref[block, :, cols]
                src = sendbuf.at[way, step]
            copy = pltpu.make_async_remote_copy(
                src_ref=src,
                dst_ref=recv.at[way, step],
                send_sem=send_sem.at[way, step],
                recv_sem=recv_sem.at[way, step],
                device_id={"head": dest},
                device_id_type=MESH,
            )
            copy.start()
            copies[way].append(copy)
    for way in range(2):
        cols = pl.ds(way * half, half)
        copies[way][n - 2].wait_recv()
        out_ref[:, cols] = (recv[way, n - 2] + term_ref[me, :, cols]).astype(out_ref.dtype)
    for way in range(2):
        for copy in copies[way]:
            copy.wait_send()


def ring_scatter(terms):
    n, rows, width = terms.shape
    half = width // 2
    return pl.pallas_call(
        functools.partial(ring_scatter_kernel, n),
        out_shape=jax.ShapeDtypeStruct((rows, width), jnp.bfloat16),
        in_specs=[pl.BlockSpec(memory_space=pltpu.VMEM)],
        out_specs=pl.BlockSpec(memory_space=pltpu.VMEM),
        scratch_shapes=[
            pltpu.VMEM((2, n - 1, rows, half), jnp.float32),
            pltpu.VMEM((2, n - 1, rows, half), jnp.float32),
            pltpu.SemaphoreType.DMA((2, n - 1)),
            pltpu.SemaphoreType.DMA((2, n - 1)),
        ],
        compiler_params=pltpu.CompilerParams(
            collective_id=0, has_side_effects=True, vmem_limit_bytes=48 * 1024 * 1024
        ),
        cost_estimate=pl.CostEstimate(
            flops=2 * n * rows * width, bytes_accessed=8 * n * rows * width, transcendentals=0
        ),
    )(terms)


def local(layer_input, w_query, w_key, w_value, w_out, out_grad):
    num_rows = layer_input.shape[1]
    local_heads = w_query.shape[1] // HEAD_DIM
    width = local_heads * HEAD_DIM
    in_rows = layer_input[0]
    grad_rows = out_grad[0]

    def project(weight):
        result = jnp.dot(in_rows, weight, preferred_element_type=jnp.float32).astype(jnp.bfloat16)
        return result.reshape(num_rows, local_heads, HEAD_DIM)

    queries = project(w_query)
    key_rows = project(w_key)
    value_rows = project(w_value)
    here = lax.axis_index("seq")
    peers = lax.axis_size("seq")
    row_start = here * num_rows
    positions = (row_start + jnp.arange(num_rows, dtype=jnp.int32)).astype(jnp.float32)
    pos_scale = 1.0 / jnp.sqrt(HEAD_DIM * (positions + 1.0))
    backward = jnp.einsum("td,kd->tk", grad_rows, w_out, preferred_element_type=jnp.float32)
    grad_in = (
        (backward * pos_scale[:, None])
        .astype(jnp.bfloat16)
        .reshape(num_rows, local_heads, HEAD_DIM)
    )
    kv_state = jnp.einsum("thd,the->hde", key_rows, value_rows, preferred_element_type=jnp.float32)
    qg_state = jnp.einsum("thd,the->hde", queries, grad_in, preferred_element_type=jnp.float32)
    states = lax.all_gather(jnp.stack([kv_state, qg_state]), "seq")
    blocks = jnp.arange(peers)[:, None, None, None]
    prefix = jnp.sum(jnp.where(blocks < here, states[:, 0], 0.0), axis=0).astype(jnp.bfloat16)
    suffix = jnp.sum(jnp.where(blocks > here, states[:, 1], 0.0), axis=0).astype(jnp.bfloat16)
    causal = (jnp.arange(num_rows)[:, None] >= jnp.arange(num_rows)[None, :])[None]
    scores = jnp.einsum("thd,shd->hts", queries, key_rows, preferred_element_type=jnp.float32)
    scores_qk = jnp.where(causal, scores, 0.0).astype(jnp.bfloat16)
    scores_g = jnp.einsum("thd,shd->hts", grad_in, value_rows, preferred_element_type=jnp.float32)
    scores_gv = jnp.where(causal, scores_g, 0.0).astype(jnp.bfloat16)
    inner_sum = jnp.einsum(
        "hts,she->the", scores_qk, value_rows, preferred_element_type=jnp.float32
    )
    cross_sum = jnp.einsum("thd,hde->the", queries, prefix, preferred_element_type=jnp.float32)
    attention = (
        ((inner_sum + cross_sum) * pos_scale[:, None, None])
        .astype(jnp.bfloat16)
        .reshape(num_rows, width)
    )
    d_query = jnp.einsum("hts,shd->thd", scores_gv, key_rows, preferred_element_type=jnp.float32)
    d_query = d_query + jnp.einsum(
        "the,hde->thd", grad_in, prefix, preferred_element_type=jnp.float32
    )
    d_keys = jnp.einsum("hts,thd->shd", scores_gv, queries, preferred_element_type=jnp.float32)
    d_keys = d_keys + jnp.einsum(
        "she,hde->shd", value_rows, suffix, preferred_element_type=jnp.float32
    )
    d_values = jnp.einsum("hts,the->she", scores_qk, grad_in, preferred_element_type=jnp.float32)
    d_values = d_values + jnp.einsum(
        "shd,hde->she", key_rows, suffix, preferred_element_type=jnp.float32
    )
    d_query = d_query.astype(jnp.bfloat16).reshape(num_rows, width)
    d_keys = d_keys.astype(jnp.bfloat16).reshape(num_rows, width)
    d_values = d_values.astype(jnp.bfloat16).reshape(num_rows, width)
    groups = lax.axis_size("head")

    def by_block(weight):
        return weight.reshape(groups, weight.shape[0] // groups, width)

    head_terms = jnp.einsum("tk,bdk->btd", d_query, by_block(w_query), preferred_element_type=jnp.float32)
    head_terms = head_terms + jnp.einsum(
        "tk,bdk->btd", d_keys, by_block(w_key), preferred_element_type=jnp.float32
    )
    head_terms = head_terms + jnp.einsum(
        "tk,bdk->btd", d_values, by_block(w_value), preferred_element_type=jnp.float32
    )
    total_rows = lax.axis_size("seq") * lax.axis_size("dp") * num_rows
    grad_scale = jnp.float32(1.0) / jnp.sqrt(jnp.float32(total_rows))
    grads = jnp.concatenate([d_query, d_keys, d_values], axis=1)
    term_qkv = jnp.einsum("td,tk->dk", in_rows, grads, preferred_element_type=jnp.float32)
    term_out = jnp.einsum("td,tk->dk", grad_rows, attention, preferred_element_type=jnp.float32)
    terms = jnp.concatenate([term_qkv, term_out], axis=1) * grad_scale
    terms, head_terms = lax.optimization_barrier((terms, head_terms))
    summed = lax.psum_scatter(terms, "seq", scatter_dimension=0, tiled=True)
    input_grad = ring_scatter(head_terms)[None]
    summed, input_grad = lax.optimization_barrier((summed, input_grad))
    summed = lax.psum_scatter(summed, "dp", scatter_dimension=0, tiled=True)
    grad_query = summed[:, :width]
    grad_key = summed[:, width:2 * width]
    grad_value = summed[:, 2 * width:3 * width]
    grad_out = summed[:, 3 * width:].T
    return (input_grad, grad_query, grad_key, grad_value, grad_out)


def solution(mesh):
    return jax.shard_map(
        local,
        mesh=mesh,
        in_specs=(
            P("dp", "seq", None),
            P(None, "head"),
            P(None, "head"),
            P(None, "head"),
            P("head", None),
            P("dp", "seq", None),
        ),
        out_specs=(
            P("dp", "seq", "head"),
            P(("seq", "dp"), "head"),
            P(("seq", "dp"), "head"),
            P(("seq", "dp"), "head"),
            P("head", ("seq", "dp")),
        ),
        check_vma=False,
    )
```

```python
import functools

import jax
import jax.numpy as jnp
from jax import lax
from jax.experimental import pallas as pl
from jax.experimental.pallas import tpu as pltpu
from jax.sharding import PartitionSpec as P

HEAD_DIM = 128
MESH = pl.DeviceIdType.MESH


def ring_scatter_kernel(n, term_ref, out_ref, recv, sendbuf, send_sem, recv_sem):
    me = lax.axis_index("head")
    right, left = lax.rem(me + 1, n), lax.rem(me + n - 1, n)
    half = out_ref.shape[1] // 2
    barrier = pltpu.get_barrier_semaphore()
    for neighbour in (left, right):
        pl.semaphore_signal(barrier, inc=1, device_id={"head": neighbour}, device_id_type=MESH)
    pl.semaphore_wait(barrier, 2)
    routes = ((right, -1), (left, 1))
    copies = [[], []]
    for step in range(n - 1):
        for way, (dest, sign) in enumerate(routes):
            block = lax.rem(me + n + sign * (step + 1), n)
            cols = pl.ds(way * half, half)
            if step == 0:
                src = term_ref.at[block, :, cols]
            else:
                copies[way][step - 1].wait_recv()
                sendbuf[way, step] = recv[way, step - 1] + term_ref[block, :, cols]
                src = sendbuf.at[way, step]
            copy = pltpu.make_async_remote_copy(
                src_ref=src,
                dst_ref=recv.at[way, step],
                send_sem=send_sem.at[way, step],
                recv_sem=recv_sem.at[way, step],
                device_id={"head": dest},
                device_id_type=MESH,
            )
            copy.start()
            copies[way].append(copy)
    for way in range(2):
        cols = pl.ds(way * half, half)
        copies[way][n - 2].wait_recv()
        out_ref[:, cols] = (recv[way, n - 2] + term_ref[me, :, cols]).astype(out_ref.dtype)
    for way in range(2):
        for copy in copies[way]:
            copy.wait_send()


def ring_scatter(terms):
    n, rows, width = terms.shape
    half = width // 2
    return pl.pallas_call(
        functools.partial(ring_scatter_kernel, n),
        out_shape=jax.ShapeDtypeStruct((rows, width), jnp.bfloat16),
        in_specs=[pl.BlockSpec(memory_space=pltpu.VMEM)],
        out_specs=pl.BlockSpec(memory_space=pltpu.VMEM),
        scratch_shapes=[
            pltpu.VMEM((2, n - 1, rows, half), jnp.float32),
            pltpu.VMEM((2, n - 1, rows, half), jnp.float32),
            pltpu.SemaphoreType.DMA((2, n - 1)),
            pltpu.SemaphoreType.DMA((2, n - 1)),
        ],
        compiler_params=pltpu.CompilerParams(
            collective_id=0, has_side_effects=True, vmem_limit_bytes=48 * 1024 * 1024
        ),
        cost_estimate=pl.CostEstimate(
            flops=2 * n * rows * width, bytes_accessed=8 * n * rows * width, transcendentals=0
        ),
    )(terms)


def exclusive_scan(x, axis, reverse):
    peers = lax.axis_size(axis)
    span = x
    total = None
    reach = 1
    while reach < peers:
        if reverse:
            pairs = [(j, j - reach) for j in range(reach, peers)]
        else:
            pairs = [(j, j + reach) for j in range(peers - reach)]
        arrived = lax.ppermute(span, axis, pairs)
        total = arrived if total is None else total + arrived
        if reach * 2 < peers:
            span = span + arrived
        reach *= 2
    return total


def local(layer_input, w_query, w_key, w_value, w_out, out_grad):
    num_rows = layer_input.shape[1]
    local_heads = w_query.shape[1] // HEAD_DIM
    width = local_heads * HEAD_DIM
    in_rows = layer_input[0]
    grad_rows = out_grad[0]

    def project(weight):
        result = jnp.dot(in_rows, weight, preferred_element_type=jnp.float32).astype(jnp.bfloat16)
        return result.reshape(num_rows, local_heads, HEAD_DIM)

    queries = project(w_query)
    key_rows = project(w_key)
    value_rows = project(w_value)
    row_start = lax.axis_index("seq") * num_rows
    positions = (row_start + jnp.arange(num_rows, dtype=jnp.int32)).astype(jnp.float32)
    pos_scale = 1.0 / jnp.sqrt(HEAD_DIM * (positions + 1.0))
    backward = jnp.einsum("td,kd->tk", grad_rows, w_out, preferred_element_type=jnp.float32)
    grad_in = (
        (backward * pos_scale[:, None])
        .astype(jnp.bfloat16)
        .reshape(num_rows, local_heads, HEAD_DIM)
    )
    kv_state = jnp.einsum("thd,the->hde", key_rows, value_rows, preferred_element_type=jnp.float32)
    qg_state = jnp.einsum("thd,the->hde", queries, grad_in, preferred_element_type=jnp.float32)
    prefix = exclusive_scan(kv_state, "seq", False).astype(jnp.bfloat16)
    suffix = exclusive_scan(qg_state, "seq", True).astype(jnp.bfloat16)
    causal = (jnp.arange(num_rows)[:, None] >= jnp.arange(num_rows)[None, :])[None]
    scores = jnp.einsum("thd,shd->hts", queries, key_rows, preferred_element_type=jnp.float32)
    scores_qk = jnp.where(causal, scores, 0.0).astype(jnp.bfloat16)
    scores_g = jnp.einsum("thd,shd->hts", grad_in, value_rows, preferred_element_type=jnp.float32)
    scores_gv = jnp.where(causal, scores_g, 0.0).astype(jnp.bfloat16)
    inner_sum = jnp.einsum(
        "hts,she->the", scores_qk, value_rows, preferred_element_type=jnp.float32
    )
    cross_sum = jnp.einsum("thd,hde->the", queries, prefix, preferred_element_type=jnp.float32)
    attention = (
        ((inner_sum + cross_sum) * pos_scale[:, None, None])
        .astype(jnp.bfloat16)
        .reshape(num_rows, width)
    )
    d_query = jnp.einsum("hts,shd->thd", scores_gv, key_rows, preferred_element_type=jnp.float32)
    d_query = d_query + jnp.einsum(
        "the,hde->thd", grad_in, prefix, preferred_element_type=jnp.float32
    )
    d_keys = jnp.einsum("hts,thd->shd", scores_gv, queries, preferred_element_type=jnp.float32)
    d_keys = d_keys + jnp.einsum(
        "she,hde->shd", value_rows, suffix, preferred_element_type=jnp.float32
    )
    d_values = jnp.einsum("hts,the->she", scores_qk, grad_in, preferred_element_type=jnp.float32)
    d_values = d_values + jnp.einsum(
        "shd,hde->she", key_rows, suffix, preferred_element_type=jnp.float32
    )
    d_query = d_query.astype(jnp.bfloat16).reshape(num_rows, width)
    d_keys = d_keys.astype(jnp.bfloat16).reshape(num_rows, width)
    d_values = d_values.astype(jnp.bfloat16).reshape(num_rows, width)
    groups = lax.axis_size("head")

    def by_block(weight):
        return weight.reshape(groups, weight.shape[0] // groups, width)

    head_terms = jnp.einsum("tk,bdk->btd", d_query, by_block(w_query), preferred_element_type=jnp.float32)
    head_terms = head_terms + jnp.einsum(
        "tk,bdk->btd", d_keys, by_block(w_key), preferred_element_type=jnp.float32
    )
    head_terms = head_terms + jnp.einsum(
        "tk,bdk->btd", d_values, by_block(w_value), preferred_element_type=jnp.float32
    )
    total_rows = lax.axis_size("seq") * lax.axis_size("dp") * num_rows
    grad_scale = jnp.float32(1.0) / jnp.sqrt(jnp.float32(total_rows))
    grads = jnp.concatenate([d_query, d_keys, d_values], axis=1)
    term_qkv = jnp.einsum("td,tk->dk", in_rows, grads, preferred_element_type=jnp.float32)
    term_out = jnp.einsum("td,tk->dk", grad_rows, attention, preferred_element_type=jnp.float32)
    terms = jnp.concatenate([term_qkv, term_out], axis=1) * grad_scale
    terms, head_terms = lax.optimization_barrier((terms, head_terms))
    summed = lax.psum_scatter(terms, "seq", scatter_dimension=0, tiled=True)
    input_grad = ring_scatter(head_terms)[None]
    summed, input_grad = lax.optimization_barrier((summed, input_grad))
    summed = lax.psum_scatter(summed, "dp", scatter_dimension=0, tiled=True)
    grad_query = summed[:, :width]
    grad_key = summed[:, width:2 * width]
    grad_value = summed[:, 2 * width:3 * width]
    grad_out = summed[:, 3 * width:].T
    return (input_grad, grad_query, grad_key, grad_value, grad_out)


def solution(mesh):
    return jax.shard_map(
        local,
        mesh=mesh,
        in_specs=(
            P("dp", "seq", None),
            P(None, "head"),
            P(None, "head"),
            P(None, "head"),
            P("head", None),
            P("dp", "seq", None),
        ),
        out_specs=(
            P("dp", "seq", "head"),
            P(("seq", "dp"), "head"),
            P(("seq", "dp"), "head"),
            P(("seq", "dp"), "head"),
            P("head", ("seq", "dp")),
        ),
        check_vma=False,
    )
```

```python
import functools

import jax
import jax.numpy as jnp
from jax import lax
from jax.experimental import pallas as pl
from jax.experimental.pallas import tpu as pltpu
from jax.sharding import PartitionSpec as P

HEAD_DIM = 128
MESH = pl.DeviceIdType.MESH


def ring_scatter_kernel(n, axis, term_ref, out_ref, recv, sendbuf, send_sem, recv_sem):
    me = lax.axis_index(axis)
    right, left = lax.rem(me + 1, n), lax.rem(me + n - 1, n)
    half = out_ref.shape[1] // 2
    barrier = pltpu.get_barrier_semaphore()
    for neighbour in (left, right):
        pl.semaphore_signal(barrier, inc=1, device_id={axis: neighbour}, device_id_type=MESH)
    pl.semaphore_wait(barrier, 2)
    routes = ((right, -1), (left, 1))
    copies = [[], []]
    for step in range(n - 1):
        for way, (dest, sign) in enumerate(routes):
            block = lax.rem(me + n + sign * (step + 1), n)
            cols = pl.ds(way * half, half)
            if step == 0:
                src = term_ref.at[block, :, cols]
            else:
                copies[way][step - 1].wait_recv()
                sendbuf[way, step] = recv[way, step - 1] + term_ref[block, :, cols]
                src = sendbuf.at[way, step]
            copy = pltpu.make_async_remote_copy(
                src_ref=src,
                dst_ref=recv.at[way, step],
                send_sem=send_sem.at[way, step],
                recv_sem=recv_sem.at[way, step],
                device_id={axis: dest},
                device_id_type=MESH,
            )
            copy.start()
            copies[way].append(copy)
    for way in range(2):
        cols = pl.ds(way * half, half)
        copies[way][n - 2].wait_recv()
        out_ref[:, cols] = (recv[way, n - 2] + term_ref[me, :, cols]).astype(out_ref.dtype)
    for way in range(2):
        for copy in copies[way]:
            copy.wait_send()


def ring_scatter(terms, axis, out_dtype, channel):
    n, rows, width = terms.shape
    half = width // 2
    return pl.pallas_call(
        functools.partial(ring_scatter_kernel, n, axis),
        out_shape=jax.ShapeDtypeStruct((rows, width), out_dtype),
        in_specs=[pl.BlockSpec(memory_space=pltpu.VMEM)],
        out_specs=pl.BlockSpec(memory_space=pltpu.VMEM),
        scratch_shapes=[
            pltpu.VMEM((2, n - 1, rows, half), jnp.float32),
            pltpu.VMEM((2, n - 1, rows, half), jnp.float32),
            pltpu.SemaphoreType.DMA((2, n - 1)),
            pltpu.SemaphoreType.DMA((2, n - 1)),
        ],
        compiler_params=pltpu.CompilerParams(
            collective_id=channel, has_side_effects=True, vmem_limit_bytes=48 * 1024 * 1024
        ),
        cost_estimate=pl.CostEstimate(
            flops=2 * n * rows * width, bytes_accessed=8 * n * rows * width, transcendentals=0
        ),
    )(terms)


def exclusive_scan(x, axis, reverse):
    peers = lax.axis_size(axis)
    span = x
    total = None
    reach = 1
    while reach < peers:
        if reverse:
            pairs = [(j, j - reach) for j in range(reach, peers)]
        else:
            pairs = [(j, j + reach) for j in range(peers - reach)]
        arrived = lax.ppermute(span, axis, pairs)
        total = arrived if total is None else total + arrived
        if reach * 2 < peers:
            span = span + arrived
        reach *= 2
    return total


def local(layer_input, w_query, w_key, w_value, w_out, out_grad):
    num_rows = layer_input.shape[1]
    local_heads = w_query.shape[1] // HEAD_DIM
    width = local_heads * HEAD_DIM
    in_rows = layer_input[0]
    grad_rows = out_grad[0]

    def project(weight):
        result = jnp.dot(in_rows, weight, preferred_element_type=jnp.float32).astype(jnp.bfloat16)
        return result.reshape(num_rows, local_heads, HEAD_DIM)

    queries = project(w_query)
    key_rows = project(w_key)
    value_rows = project(w_value)
    row_start = lax.axis_index("seq") * num_rows
    positions = (row_start + jnp.arange(num_rows, dtype=jnp.int32)).astype(jnp.float32)
    pos_scale = 1.0 / jnp.sqrt(HEAD_DIM * (positions + 1.0))
    backward = jnp.einsum("td,kd->tk", grad_rows, w_out, preferred_element_type=jnp.float32)
    grad_in = (
        (backward * pos_scale[:, None])
        .astype(jnp.bfloat16)
        .reshape(num_rows, local_heads, HEAD_DIM)
    )
    kv_state = jnp.einsum("thd,the->hde", key_rows, value_rows, preferred_element_type=jnp.float32)
    qg_state = jnp.einsum("thd,the->hde", queries, grad_in, preferred_element_type=jnp.float32)
    prefix = exclusive_scan(kv_state, "seq", False).astype(jnp.bfloat16)
    suffix = exclusive_scan(qg_state, "seq", True).astype(jnp.bfloat16)
    causal = (jnp.arange(num_rows)[:, None] >= jnp.arange(num_rows)[None, :])[None]
    scores = jnp.einsum("thd,shd->hts", queries, key_rows, preferred_element_type=jnp.float32)
    scores_qk = jnp.where(causal, scores, 0.0).astype(jnp.bfloat16)
    scores_g = jnp.einsum("thd,shd->hts", grad_in, value_rows, preferred_element_type=jnp.float32)
    scores_gv = jnp.where(causal, scores_g, 0.0).astype(jnp.bfloat16)
    inner_sum = jnp.einsum(
        "hts,she->the", scores_qk, value_rows, preferred_element_type=jnp.float32
    )
    cross_sum = jnp.einsum("thd,hde->the", queries, prefix, preferred_element_type=jnp.float32)
    attention = (
        ((inner_sum + cross_sum) * pos_scale[:, None, None])
        .astype(jnp.bfloat16)
        .reshape(num_rows, width)
    )
    d_query = jnp.einsum("hts,shd->thd", scores_gv, key_rows, preferred_element_type=jnp.float32)
    d_query = d_query + jnp.einsum(
        "the,hde->thd", grad_in, prefix, preferred_element_type=jnp.float32
    )
    d_keys = jnp.einsum("hts,thd->shd", scores_gv, queries, preferred_element_type=jnp.float32)
    d_keys = d_keys + jnp.einsum(
        "she,hde->shd", value_rows, suffix, preferred_element_type=jnp.float32
    )
    d_values = jnp.einsum("hts,the->she", scores_qk, grad_in, preferred_element_type=jnp.float32)
    d_values = d_values + jnp.einsum(
        "shd,hde->she", key_rows, suffix, preferred_element_type=jnp.float32
    )
    d_query = d_query.astype(jnp.bfloat16).reshape(num_rows, width)
    d_keys = d_keys.astype(jnp.bfloat16).reshape(num_rows, width)
    d_values = d_values.astype(jnp.bfloat16).reshape(num_rows, width)
    groups = lax.axis_size("head")

    def by_block(weight):
        return weight.reshape(groups, weight.shape[0] // groups, width)

    head_terms = jnp.einsum("tk,bdk->btd", d_query, by_block(w_query), preferred_element_type=jnp.float32)
    head_terms = head_terms + jnp.einsum(
        "tk,bdk->btd", d_keys, by_block(w_key), preferred_element_type=jnp.float32
    )
    head_terms = head_terms + jnp.einsum(
        "tk,bdk->btd", d_values, by_block(w_value), preferred_element_type=jnp.float32
    )
    total_rows = lax.axis_size("seq") * lax.axis_size("dp") * num_rows
    grad_scale = jnp.float32(1.0) / jnp.sqrt(jnp.float32(total_rows))
    grads = jnp.concatenate([d_query, d_keys, d_values], axis=1)
    term_qkv = jnp.einsum("td,tk->dk", in_rows, grads, preferred_element_type=jnp.float32)
    term_out = jnp.einsum("td,tk->dk", grad_rows, attention, preferred_element_type=jnp.float32)
    terms = jnp.concatenate([term_qkv, term_out], axis=1) * grad_scale
    terms, head_terms = lax.optimization_barrier((terms, head_terms))
    summed = lax.psum_scatter(terms, "seq", scatter_dimension=0, tiled=True)
    input_grad = ring_scatter(head_terms, "head", jnp.bfloat16, 0)[None]
    summed, input_grad = lax.optimization_barrier((summed, input_grad))
    shares = lax.axis_size("dp")
    summed = ring_scatter(
        summed.reshape(shares, summed.shape[0] // shares, summed.shape[1]), "dp", jnp.float32, 1
    )
    grad_query = summed[:, :width]
    grad_key = summed[:, width:2 * width]
    grad_value = summed[:, 2 * width:3 * width]
    grad_out = summed[:, 3 * width:].T
    return (input_grad, grad_query, grad_key, grad_value, grad_out)


def solution(mesh):
    return jax.shard_map(
        local,
        mesh=mesh,
        in_specs=(
            P("dp", "seq", None),
            P(None, "head"),
            P(None, "head"),
            P(None, "head"),
            P("head", None),
            P("dp", "seq", None),
        ),
        out_specs=(
            P("dp", "seq", "head"),
            P(("seq", "dp"), "head"),
            P(("seq", "dp"), "head"),
            P(("seq", "dp"), "head"),
            P("head", ("seq", "dp")),
        ),
        check_vma=False,
    )
```

```python
import functools

import jax
import jax.numpy as jnp
from jax import lax
from jax.experimental import pallas as pl
from jax.experimental.pallas import tpu as pltpu
from jax.sharding import PartitionSpec as P

HEAD_DIM = 128
MESH = pl.DeviceIdType.MESH


def ring_scatter_kernel(n, axis, term_ref, out_ref, recv, sendbuf, send_sem, recv_sem):
    me = lax.axis_index(axis)
    right, left = lax.rem(me + 1, n), lax.rem(me + n - 1, n)
    half = out_ref.shape[1] // 2
    barrier = pltpu.get_barrier_semaphore()
    for neighbour in (left, right):
        pl.semaphore_signal(barrier, inc=1, device_id={axis: neighbour}, device_id_type=MESH)
    pl.semaphore_wait(barrier, 2)
    routes = ((right, -1), (left, 1))
    copies = [[], []]
    for step in range(n - 1):
        for way, (dest, sign) in enumerate(routes):
            block = lax.rem(me + n + sign * (step + 1), n)
            cols = pl.ds(way * half, half)
            if step == 0:
                src = term_ref.at[block, :, cols]
            else:
                copies[way][step - 1].wait_recv()
                sendbuf[way, step] = recv[way, step - 1] + term_ref[block, :, cols]
                src = sendbuf.at[way, step]
            copy = pltpu.make_async_remote_copy(
                src_ref=src,
                dst_ref=recv.at[way, step],
                send_sem=send_sem.at[way, step],
                recv_sem=recv_sem.at[way, step],
                device_id={axis: dest},
                device_id_type=MESH,
            )
            copy.start()
            copies[way].append(copy)
    for way in range(2):
        cols = pl.ds(way * half, half)
        copies[way][n - 2].wait_recv()
        out_ref[:, cols] = (recv[way, n - 2] + term_ref[me, :, cols]).astype(out_ref.dtype)
    for way in range(2):
        for copy in copies[way]:
            copy.wait_send()


def ring_scatter(terms, axis, out_dtype, channel):
    n, rows, width = terms.shape
    half = width // 2
    return pl.pallas_call(
        functools.partial(ring_scatter_kernel, n, axis),
        out_shape=jax.ShapeDtypeStruct((rows, width), out_dtype),
        in_specs=[pl.BlockSpec(memory_space=pltpu.VMEM)],
        out_specs=pl.BlockSpec(memory_space=pltpu.VMEM),
        scratch_shapes=[
            pltpu.VMEM((2, n - 1, rows, half), jnp.float32),
            pltpu.VMEM((2, n - 1, rows, half), jnp.float32),
            pltpu.SemaphoreType.DMA((2, n - 1)),
            pltpu.SemaphoreType.DMA((2, n - 1)),
        ],
        compiler_params=pltpu.CompilerParams(
            collective_id=channel, has_side_effects=True, vmem_limit_bytes=48 * 1024 * 1024
        ),
        cost_estimate=pl.CostEstimate(
            flops=2 * n * rows * width, bytes_accessed=8 * n * rows * width, transcendentals=0
        ),
    )(terms)


def exclusive_scan(x, axis, reverse):
    peers = lax.axis_size(axis)
    span = x
    total = None
    reach = 1
    while reach < peers:
        if reverse:
            pairs = [(j, j - reach) for j in range(reach, peers)]
        else:
            pairs = [(j, j + reach) for j in range(peers - reach)]
        arrived = lax.ppermute(span, axis, pairs)
        total = arrived if total is None else total + arrived
        if reach * 2 < peers:
            span = span + arrived
        reach *= 2
    return total


def local(layer_input, w_query, w_key, w_value, w_out, out_grad):
    num_rows = layer_input.shape[1]
    local_heads = w_query.shape[1] // HEAD_DIM
    width = local_heads * HEAD_DIM
    in_rows = layer_input[0]
    grad_rows = out_grad[0]

    def project(weight):
        result = jnp.dot(in_rows, weight, preferred_element_type=jnp.float32).astype(jnp.bfloat16)
        return result.reshape(num_rows, local_heads, HEAD_DIM)

    queries = project(w_query)
    key_rows = project(w_key)
    value_rows = project(w_value)
    row_start = lax.axis_index("seq") * num_rows
    positions = (row_start + jnp.arange(num_rows, dtype=jnp.int32)).astype(jnp.float32)
    pos_scale = 1.0 / jnp.sqrt(HEAD_DIM * (positions + 1.0))
    backward = jnp.einsum("td,kd->tk", grad_rows, w_out, preferred_element_type=jnp.float32)
    grad_in = (
        (backward * pos_scale[:, None])
        .astype(jnp.bfloat16)
        .reshape(num_rows, local_heads, HEAD_DIM)
    )
    kv_state = jnp.einsum("thd,the->hde", key_rows, value_rows, preferred_element_type=jnp.float32)
    qg_state = jnp.einsum("thd,the->hde", queries, grad_in, preferred_element_type=jnp.float32)
    prefix = exclusive_scan(kv_state, "seq", False).astype(jnp.bfloat16)
    suffix = exclusive_scan(qg_state, "seq", True).astype(jnp.bfloat16)
    causal = (jnp.arange(num_rows)[:, None] >= jnp.arange(num_rows)[None, :])[None]
    scores = jnp.einsum("thd,shd->hts", queries, key_rows, preferred_element_type=jnp.float32)
    scores_qk = jnp.where(causal, scores, 0.0).astype(jnp.bfloat16)
    scores_g = jnp.einsum("thd,shd->hts", grad_in, value_rows, preferred_element_type=jnp.float32)
    scores_gv = jnp.where(causal, scores_g, 0.0).astype(jnp.bfloat16)
    inner_sum = jnp.einsum(
        "hts,she->the", scores_qk, value_rows, preferred_element_type=jnp.float32
    )
    cross_sum = jnp.einsum("thd,hde->the", queries, prefix, preferred_element_type=jnp.float32)
    attention = (
        ((inner_sum + cross_sum) * pos_scale[:, None, None])
        .astype(jnp.bfloat16)
        .reshape(num_rows, width)
    )
    d_query = jnp.einsum("hts,shd->thd", scores_gv, key_rows, preferred_element_type=jnp.float32)
    d_query = d_query + jnp.einsum(
        "the,hde->thd", grad_in, prefix, preferred_element_type=jnp.float32
    )
    d_keys = jnp.einsum("hts,thd->shd", scores_gv, queries, preferred_element_type=jnp.float32)
    d_keys = d_keys + jnp.einsum(
        "she,hde->shd", value_rows, suffix, preferred_element_type=jnp.float32
    )
    d_values = jnp.einsum("hts,the->she", scores_qk, grad_in, preferred_element_type=jnp.float32)
    d_values = d_values + jnp.einsum(
        "shd,hde->she", key_rows, suffix, preferred_element_type=jnp.float32
    )
    d_query = d_query.astype(jnp.bfloat16).reshape(num_rows, width)
    d_keys = d_keys.astype(jnp.bfloat16).reshape(num_rows, width)
    d_values = d_values.astype(jnp.bfloat16).reshape(num_rows, width)
    groups = lax.axis_size("head")

    grads = jnp.concatenate([d_query, d_keys, d_values], axis=1)
    w_all = jnp.concatenate([w_query, w_key, w_value], axis=1)
    total_rows = lax.axis_size("seq") * lax.axis_size("dp") * num_rows
    grad_scale = jnp.float32(1.0) / jnp.sqrt(jnp.float32(total_rows))
    term_qkv = jnp.einsum("td,tk->dk", in_rows, grads, preferred_element_type=jnp.float32)
    term_out = jnp.einsum("td,tk->dk", grad_rows, attention, preferred_element_type=jnp.float32)
    terms = jnp.concatenate([term_qkv, term_out], axis=1) * grad_scale
    terms, grads, w_all = lax.optimization_barrier((terms, grads, w_all))
    summed = lax.psum_scatter(terms, "seq", scatter_dimension=0, tiled=True)
    head_terms = jnp.einsum(
        "tk,bdk->btd", grads, w_all.reshape(groups, w_all.shape[0] // groups, 3 * width),
        preferred_element_type=jnp.float32,
    )
    input_grad = ring_scatter(head_terms, "head", jnp.bfloat16, 0)[None]
    summed, input_grad = lax.optimization_barrier((summed, input_grad))
    shares = lax.axis_size("dp")
    summed = ring_scatter(
        summed.reshape(shares, summed.shape[0] // shares, summed.shape[1]), "dp", jnp.float32, 1
    )
    grad_query = summed[:, :width]
    grad_key = summed[:, width:2 * width]
    grad_value = summed[:, 2 * width:3 * width]
    grad_out = summed[:, 3 * width:].T
    return (input_grad, grad_query, grad_key, grad_value, grad_out)


def solution(mesh):
    return jax.shard_map(
        local,
        mesh=mesh,
        in_specs=(
            P("dp", "seq", None),
            P(None, "head"),
            P(None, "head"),
            P(None, "head"),
            P("head", None),
            P("dp", "seq", None),
        ),
        out_specs=(
            P("dp", "seq", "head"),
            P(("seq", "dp"), "head"),
            P(("seq", "dp"), "head"),
            P(("seq", "dp"), "head"),
            P("head", ("seq", "dp")),
        ),
        check_vma=False,
    )
```

```python
import functools

import jax
import jax.numpy as jnp
from jax import lax
from jax.experimental import pallas as pl
from jax.experimental.pallas import tpu as pltpu
from jax.sharding import PartitionSpec as P

HEAD_DIM = 128
MESH = pl.DeviceIdType.MESH


def ring_scatter_kernel(n, axis, term_ref, out_ref, recv, sendbuf, send_sem, recv_sem):
    me = lax.axis_index(axis)
    right, left = lax.rem(me + 1, n), lax.rem(me + n - 1, n)
    half = out_ref.shape[1] // 2
    barrier = pltpu.get_barrier_semaphore()
    for neighbour in (left, right):
        pl.semaphore_signal(barrier, inc=1, device_id={axis: neighbour}, device_id_type=MESH)
    pl.semaphore_wait(barrier, 2)
    routes = ((right, -1), (left, 1))
    copies = [[], []]
    for step in range(n - 1):
        for way, (dest, sign) in enumerate(routes):
            block = lax.rem(me + n + sign * (step + 1), n)
            cols = pl.ds(way * half, half)
            if step == 0:
                src = term_ref.at[block, :, cols]
            else:
                copies[way][step - 1].wait_recv()
                sendbuf[way, step] = recv[way, step - 1] + term_ref[block, :, cols]
                src = sendbuf.at[way, step]
            copy = pltpu.make_async_remote_copy(
                src_ref=src,
                dst_ref=recv.at[way, step],
                send_sem=send_sem.at[way, step],
                recv_sem=recv_sem.at[way, step],
                device_id={axis: dest},
                device_id_type=MESH,
            )
            copy.start()
            copies[way].append(copy)
    for way in range(2):
        cols = pl.ds(way * half, half)
        copies[way][n - 2].wait_recv()
        out_ref[:, cols] = (recv[way, n - 2] + term_ref[me, :, cols]).astype(out_ref.dtype)
    for way in range(2):
        for copy in copies[way]:
            copy.wait_send()


def ring_scatter(terms, axis, out_dtype, channel):
    n, rows, width = terms.shape
    half = width // 2
    return pl.pallas_call(
        functools.partial(ring_scatter_kernel, n, axis),
        out_shape=jax.ShapeDtypeStruct((rows, width), out_dtype),
        in_specs=[pl.BlockSpec(memory_space=pltpu.VMEM)],
        out_specs=pl.BlockSpec(memory_space=pltpu.VMEM),
        scratch_shapes=[
            pltpu.VMEM((2, n - 1, rows, half), jnp.float32),
            pltpu.VMEM((2, n - 1, rows, half), jnp.float32),
            pltpu.SemaphoreType.DMA((2, n - 1)),
            pltpu.SemaphoreType.DMA((2, n - 1)),
        ],
        compiler_params=pltpu.CompilerParams(
            collective_id=channel, has_side_effects=True, vmem_limit_bytes=48 * 1024 * 1024
        ),
        cost_estimate=pl.CostEstimate(
            flops=2 * n * rows * width, bytes_accessed=8 * n * rows * width, transcendentals=0
        ),
    )(terms)


def exchange_kernel(n, axis, kv_ref, qg_ref, prefix_ref, suffix_ref, kv_in, qg_in, send_sem, recv_sem):
    me = lax.axis_index(axis)
    barrier = pltpu.get_barrier_semaphore()
    for offset in range(1, n):
        pl.semaphore_signal(
            barrier, inc=1, device_id={axis: lax.rem(me + offset, n)}, device_id_type=MESH
        )
    pl.semaphore_wait(barrier, n - 1)

    def route(offset, later):
        peer = lax.rem(me + offset, n)
        kind = 0 if later else 1
        return pltpu.make_async_remote_copy(
            src_ref=kv_ref if later else qg_ref,
            dst_ref=(kv_in if later else qg_in).at[me],
            send_sem=send_sem.at[kind, offset],
            recv_sem=recv_sem.at[kind, me],
            device_id={axis: peer},
            device_id_type=MESH,
        )

    for offset in range(1, n):
        for later in (True, False):
            @pl.when((me + offset < n) == later)
            def _():
                route(offset, later).start()

    prefix_ref[...] = jnp.zeros_like(prefix_ref)
    suffix_ref[...] = jnp.zeros_like(suffix_ref)
    for peer in range(n):
        @pl.when(peer < me)
        def _():
            pltpu.make_async_remote_copy(
                src_ref=kv_ref, dst_ref=kv_in.at[peer], send_sem=send_sem.at[0, 0],
                recv_sem=recv_sem.at[0, peer], device_id={axis: peer}, device_id_type=MESH,
            ).wait_recv()
            prefix_ref[...] += kv_in[peer]

        @pl.when(peer > me)
        def _():
            pltpu.make_async_remote_copy(
                src_ref=qg_ref, dst_ref=qg_in.at[peer], send_sem=send_sem.at[1, 0],
                recv_sem=recv_sem.at[1, peer], device_id={axis: peer}, device_id_type=MESH,
            ).wait_recv()
            suffix_ref[...] += qg_in[peer]

    for offset in range(1, n):
        for later in (True, False):
            @pl.when((me + offset < n) == later)
            def _():
                route(offset, later).wait_send()


def exchange_states(kv_state, qg_state, axis):
    n = lax.axis_size(axis)
    shape = kv_state.shape
    return pl.pallas_call(
        functools.partial(exchange_kernel, n, axis),
        out_shape=(jax.ShapeDtypeStruct(shape, jnp.float32),) * 2,
        in_specs=[pl.BlockSpec(memory_space=pltpu.VMEM)] * 2,
        out_specs=(pl.BlockSpec(memory_space=pltpu.VMEM),) * 2,
        scratch_shapes=[
            pltpu.VMEM((n,) + shape, jnp.float32),
            pltpu.VMEM((n,) + shape, jnp.float32),
            pltpu.SemaphoreType.DMA((2, n)),
            pltpu.SemaphoreType.DMA((2, n)),
        ],
        compiler_params=pltpu.CompilerParams(collective_id=2, has_side_effects=True),
    )(kv_state, qg_state)


def local(layer_input, w_query, w_key, w_value, w_out, out_grad):
    num_rows = layer_input.shape[1]
    local_heads = w_query.shape[1] // HEAD_DIM
    width = local_heads * HEAD_DIM
    in_rows = layer_input[0]
    grad_rows = out_grad[0]

    def project(weight):
        result = jnp.dot(in_rows, weight, preferred_element_type=jnp.float32).astype(jnp.bfloat16)
        return result.reshape(num_rows, local_heads, HEAD_DIM)

    queries = project(w_query)
    key_rows = project(w_key)
    value_rows = project(w_value)
    row_start = lax.axis_index("seq") * num_rows
    positions = (row_start + jnp.arange(num_rows, dtype=jnp.int32)).astype(jnp.float32)
    pos_scale = 1.0 / jnp.sqrt(HEAD_DIM * (positions + 1.0))
    backward = jnp.einsum("td,kd->tk", grad_rows, w_out, preferred_element_type=jnp.float32)
    grad_in = (
        (backward * pos_scale[:, None])
        .astype(jnp.bfloat16)
        .reshape(num_rows, local_heads, HEAD_DIM)
    )
    kv_state = jnp.einsum("thd,the->hde", key_rows, value_rows, preferred_element_type=jnp.float32)
    qg_state = jnp.einsum("thd,the->hde", queries, grad_in, preferred_element_type=jnp.float32)
    prefix, suffix = exchange_states(kv_state, qg_state, "seq")
    prefix = prefix.astype(jnp.bfloat16)
    suffix = suffix.astype(jnp.bfloat16)
    causal = (jnp.arange(num_rows)[:, None] >= jnp.arange(num_rows)[None, :])[None]
    scores = jnp.einsum("thd,shd->hts", queries, key_rows, preferred_element_type=jnp.float32)
    scores_qk = jnp.where(causal, scores, 0.0).astype(jnp.bfloat16)
    scores_g = jnp.einsum("thd,shd->hts", grad_in, value_rows, preferred_element_type=jnp.float32)
    scores_gv = jnp.where(causal, scores_g, 0.0).astype(jnp.bfloat16)
    inner_sum = jnp.einsum(
        "hts,she->the", scores_qk, value_rows, preferred_element_type=jnp.float32
    )
    cross_sum = jnp.einsum("thd,hde->the", queries, prefix, preferred_element_type=jnp.float32)
    attention = (
        ((inner_sum + cross_sum) * pos_scale[:, None, None])
        .astype(jnp.bfloat16)
        .reshape(num_rows, width)
    )
    d_query = jnp.einsum("hts,shd->thd", scores_gv, key_rows, preferred_element_type=jnp.float32)
    d_query = d_query + jnp.einsum(
        "the,hde->thd", grad_in, prefix, preferred_element_type=jnp.float32
    )
    d_keys = jnp.einsum("hts,thd->shd", scores_gv, queries, preferred_element_type=jnp.float32)
    d_keys = d_keys + jnp.einsum(
        "she,hde->shd", value_rows, suffix, preferred_element_type=jnp.float32
    )
    d_values = jnp.einsum("hts,the->she", scores_qk, grad_in, preferred_element_type=jnp.float32)
    d_values = d_values + jnp.einsum(
        "shd,hde->she", key_rows, suffix, preferred_element_type=jnp.float32
    )
    d_query = d_query.astype(jnp.bfloat16).reshape(num_rows, width)
    d_keys = d_keys.astype(jnp.bfloat16).reshape(num_rows, width)
    d_values = d_values.astype(jnp.bfloat16).reshape(num_rows, width)
    groups = lax.axis_size("head")

    def by_block(weight):
        return weight.reshape(groups, weight.shape[0] // groups, width)

    head_terms = jnp.einsum("tk,bdk->btd", d_query, by_block(w_query), preferred_element_type=jnp.float32)
    head_terms = head_terms + jnp.einsum(
        "tk,bdk->btd", d_keys, by_block(w_key), preferred_element_type=jnp.float32
    )
    head_terms = head_terms + jnp.einsum(
        "tk,bdk->btd", d_values, by_block(w_value), preferred_element_type=jnp.float32
    )
    total_rows = lax.axis_size("seq") * lax.axis_size("dp") * num_rows
    grad_scale = jnp.float32(1.0) / jnp.sqrt(jnp.float32(total_rows))
    grads = jnp.concatenate([d_query, d_keys, d_values], axis=1)
    term_qkv = jnp.einsum("td,tk->dk", in_rows, grads, preferred_element_type=jnp.float32)
    term_out = jnp.einsum("td,tk->dk", grad_rows, attention, preferred_element_type=jnp.float32)
    terms = jnp.concatenate([term_qkv, term_out], axis=1) * grad_scale
    terms, head_terms = lax.optimization_barrier((terms, head_terms))
    summed = lax.psum_scatter(terms, "seq", scatter_dimension=0, tiled=True)
    input_grad = ring_scatter(head_terms, "head", jnp.bfloat16, 0)[None]
    summed, input_grad = lax.optimization_barrier((summed, input_grad))
    shares = lax.axis_size("dp")
    summed = ring_scatter(
        summed.reshape(shares, summed.shape[0] // shares, summed.shape[1]), "dp", jnp.float32, 1
    )
    grad_query = summed[:, :width]
    grad_key = summed[:, width:2 * width]
    grad_value = summed[:, 2 * width:3 * width]
    grad_out = summed[:, 3 * width:].T
    return (input_grad, grad_query, grad_key, grad_value, grad_out)


def solution(mesh):
    return jax.shard_map(
        local,
        mesh=mesh,
        in_specs=(
            P("dp", "seq", None),
            P(None, "head"),
            P(None, "head"),
            P(None, "head"),
            P("head", None),
            P("dp", "seq", None),
        ),
        out_specs=(
            P("dp", "seq", "head"),
            P(("seq", "dp"), "head"),
            P(("seq", "dp"), "head"),
            P(("seq", "dp"), "head"),
            P("head", ("seq", "dp")),
        ),
        check_vma=False,
    )
```

```python
import functools

import jax
import jax.numpy as jnp
from jax import lax
from jax.experimental import pallas as pl
from jax.experimental.pallas import tpu as pltpu
from jax.sharding import PartitionSpec as P

HEAD_DIM = 128
MESH = pl.DeviceIdType.MESH


def ring_scatter_kernel(jobs, *refs):
    count = len(jobs)
    terms, outs, scratch = refs[:count], refs[count:2 * count], refs[2 * count:]
    barrier = pltpu.get_barrier_semaphore()
    places = []
    for axis, n in jobs:
        me = lax.axis_index(axis)
        right, left = lax.rem(me + 1, n), lax.rem(me + n - 1, n)
        places.append((me, right, left))
        for neighbour in (left, right):
            pl.semaphore_signal(barrier, inc=1, device_id={axis: neighbour}, device_id_type=MESH)
    pl.semaphore_wait(barrier, 2 * count)
    copies = [[[], []] for _ in jobs]
    for step in range(max(n for _, n in jobs) - 1):
        for job, (axis, n) in enumerate(jobs):
            if step >= n - 1:
                continue
            me, right, left = places[job]
            recv, sendbuf, send_sem, recv_sem = scratch[4 * job:4 * job + 4]
            term_ref = terms[job]
            half = outs[job].shape[1] // 2
            for way, (dest, sign) in enumerate(((right, -1), (left, 1))):
                block = lax.rem(me + n + sign * (step + 1), n)
                cols = pl.ds(way * half, half)
                if step == 0:
                    src = term_ref.at[block, :, cols]
                else:
                    copies[job][way][step - 1].wait_recv()
                    sendbuf[way, step] = recv[way, step - 1] + term_ref[block, :, cols]
                    src = sendbuf.at[way, step]
                copy = pltpu.make_async_remote_copy(
                    src_ref=src,
                    dst_ref=recv.at[way, step],
                    send_sem=send_sem.at[way, step],
                    recv_sem=recv_sem.at[way, step],
                    device_id={axis: dest},
                    device_id_type=MESH,
                )
                copy.start()
                copies[job][way].append(copy)
    for job, (axis, n) in enumerate(jobs):
        me = places[job][0]
        recv = scratch[4 * job]
        half = outs[job].shape[1] // 2
        for way in range(2):
            cols = pl.ds(way * half, half)
            copies[job][way][n - 2].wait_recv()
            outs[job][:, cols] = (recv[way, n - 2] + terms[job][me, :, cols]).astype(outs[job].dtype)
    for job in range(count):
        for way in range(2):
            for copy in copies[job][way]:
                copy.wait_send()


def ring_scatter(parts, channel):
    jobs = tuple((axis, terms.shape[0]) for terms, axis, _ in parts)
    scratch = []
    for terms, _, _ in parts:
        n, rows, width = terms.shape
        scratch += [
            pltpu.VMEM((2, n - 1, rows, width // 2), jnp.float32),
            pltpu.VMEM((2, n - 1, rows, width // 2), jnp.float32),
            pltpu.SemaphoreType.DMA((2, n - 1)),
            pltpu.SemaphoreType.DMA((2, n - 1)),
        ]
    size = sum(terms.size for terms, _, _ in parts)
    return pl.pallas_call(
        functools.partial(ring_scatter_kernel, jobs),
        out_shape=tuple(
            jax.ShapeDtypeStruct(terms.shape[1:], dtype) for terms, _, dtype in parts
        ),
        in_specs=[pl.BlockSpec(memory_space=pltpu.VMEM)] * len(parts),
        out_specs=tuple(pl.BlockSpec(memory_space=pltpu.VMEM) for _ in parts),
        scratch_shapes=scratch,
        compiler_params=pltpu.CompilerParams(
            collective_id=channel, has_side_effects=True, vmem_limit_bytes=48 * 1024 * 1024
        ),
        cost_estimate=pl.CostEstimate(flops=2 * size, bytes_accessed=8 * size, transcendentals=0),
    )(*(terms for terms, _, _ in parts))


def exchange_kernel(n, axis, kv_ref, qg_ref, prefix_ref, suffix_ref, kv_in, qg_in, send_sem, recv_sem):
    me = lax.axis_index(axis)
    barrier = pltpu.get_barrier_semaphore()
    for offset in range(1, n):
        pl.semaphore_signal(
            barrier, inc=1, device_id={axis: lax.rem(me + offset, n)}, device_id_type=MESH
        )
    pl.semaphore_wait(barrier, n - 1)

    def route(offset, later):
        peer = lax.rem(me + offset, n)
        kind = 0 if later else 1
        return pltpu.make_async_remote_copy(
            src_ref=kv_ref if later else qg_ref,
            dst_ref=(kv_in if later else qg_in).at[me],
            send_sem=send_sem.at[kind, offset],
            recv_sem=recv_sem.at[kind, me],
            device_id={axis: peer},
            device_id_type=MESH,
        )

    for offset in range(1, n):
        for later in (True, False):
            @pl.when((me + offset < n) == later)
            def _():
                route(offset, later).start()

    prefix_ref[...] = jnp.zeros_like(prefix_ref)
    suffix_ref[...] = jnp.zeros_like(suffix_ref)
    for peer in range(n):
        @pl.when(peer < me)
        def _():
            pltpu.make_async_remote_copy(
                src_ref=kv_ref, dst_ref=kv_in.at[peer], send_sem=send_sem.at[0, 0],
                recv_sem=recv_sem.at[0, peer], device_id={axis: peer}, device_id_type=MESH,
            ).wait_recv()
            prefix_ref[...] += kv_in[peer]

        @pl.when(peer > me)
        def _():
            pltpu.make_async_remote_copy(
                src_ref=qg_ref, dst_ref=qg_in.at[peer], send_sem=send_sem.at[1, 0],
                recv_sem=recv_sem.at[1, peer], device_id={axis: peer}, device_id_type=MESH,
            ).wait_recv()
            suffix_ref[...] += qg_in[peer]

    for offset in range(1, n):
        for later in (True, False):
            @pl.when((me + offset < n) == later)
            def _():
                route(offset, later).wait_send()


def exchange_states(kv_state, qg_state, axis):
    n = lax.axis_size(axis)
    shape = kv_state.shape
    return pl.pallas_call(
        functools.partial(exchange_kernel, n, axis),
        out_shape=(jax.ShapeDtypeStruct(shape, jnp.float32),) * 2,
        in_specs=[pl.BlockSpec(memory_space=pltpu.VMEM)] * 2,
        out_specs=(pl.BlockSpec(memory_space=pltpu.VMEM),) * 2,
        scratch_shapes=[
            pltpu.VMEM((n,) + shape, jnp.float32),
            pltpu.VMEM((n,) + shape, jnp.float32),
            pltpu.SemaphoreType.DMA((2, n)),
            pltpu.SemaphoreType.DMA((2, n)),
        ],
        compiler_params=pltpu.CompilerParams(collective_id=2, has_side_effects=True),
    )(kv_state, qg_state)


def local(layer_input, w_query, w_key, w_value, w_out, out_grad):
    num_rows = layer_input.shape[1]
    local_heads = w_query.shape[1] // HEAD_DIM
    width = local_heads * HEAD_DIM
    in_rows = layer_input[0]
    grad_rows = out_grad[0]

    def project(weight):
        result = jnp.dot(in_rows, weight, preferred_element_type=jnp.float32).astype(jnp.bfloat16)
        return result.reshape(num_rows, local_heads, HEAD_DIM)

    queries = project(w_query)
    key_rows = project(w_key)
    value_rows = project(w_value)
    row_start = lax.axis_index("seq") * num_rows
    positions = (row_start + jnp.arange(num_rows, dtype=jnp.int32)).astype(jnp.float32)
    pos_scale = 1.0 / jnp.sqrt(HEAD_DIM * (positions + 1.0))
    backward = jnp.einsum("td,kd->tk", grad_rows, w_out, preferred_element_type=jnp.float32)
    grad_in = (
        (backward * pos_scale[:, None])
        .astype(jnp.bfloat16)
        .reshape(num_rows, local_heads, HEAD_DIM)
    )
    kv_state = jnp.einsum("thd,the->hde", key_rows, value_rows, preferred_element_type=jnp.float32)
    qg_state = jnp.einsum("thd,the->hde", queries, grad_in, preferred_element_type=jnp.float32)
    prefix, suffix = exchange_states(kv_state, qg_state, "seq")
    prefix = prefix.astype(jnp.bfloat16)
    suffix = suffix.astype(jnp.bfloat16)
    causal = (jnp.arange(num_rows)[:, None] >= jnp.arange(num_rows)[None, :])[None]
    scores = jnp.einsum("thd,shd->hts", queries, key_rows, preferred_element_type=jnp.float32)
    scores_qk = jnp.where(causal, scores, 0.0).astype(jnp.bfloat16)
    scores_g = jnp.einsum("thd,shd->hts", grad_in, value_rows, preferred_element_type=jnp.float32)
    scores_gv = jnp.where(causal, scores_g, 0.0).astype(jnp.bfloat16)
    inner_sum = jnp.einsum(
        "hts,she->the", scores_qk, value_rows, preferred_element_type=jnp.float32
    )
    cross_sum = jnp.einsum("thd,hde->the", queries, prefix, preferred_element_type=jnp.float32)
    attention = (
        ((inner_sum + cross_sum) * pos_scale[:, None, None])
        .astype(jnp.bfloat16)
        .reshape(num_rows, width)
    )
    d_query = jnp.einsum("hts,shd->thd", scores_gv, key_rows, preferred_element_type=jnp.float32)
    d_query = d_query + jnp.einsum(
        "the,hde->thd", grad_in, prefix, preferred_element_type=jnp.float32
    )
    d_keys = jnp.einsum("hts,thd->shd", scores_gv, queries, preferred_element_type=jnp.float32)
    d_keys = d_keys + jnp.einsum(
        "she,hde->shd", value_rows, suffix, preferred_element_type=jnp.float32
    )
    d_values = jnp.einsum("hts,the->she", scores_qk, grad_in, preferred_element_type=jnp.float32)
    d_values = d_values + jnp.einsum(
        "shd,hde->she", key_rows, suffix, preferred_element_type=jnp.float32
    )
    d_query = d_query.astype(jnp.bfloat16).reshape(num_rows, width)
    d_keys = d_keys.astype(jnp.bfloat16).reshape(num_rows, width)
    d_values = d_values.astype(jnp.bfloat16).reshape(num_rows, width)
    groups = lax.axis_size("head")

    def by_block(weight):
        return weight.reshape(groups, weight.shape[0] // groups, width)

    head_terms = jnp.einsum("tk,bdk->btd", d_query, by_block(w_query), preferred_element_type=jnp.float32)
    head_terms = head_terms + jnp.einsum(
        "tk,bdk->btd", d_keys, by_block(w_key), preferred_element_type=jnp.float32
    )
    head_terms = head_terms + jnp.einsum(
        "tk,bdk->btd", d_values, by_block(w_value), preferred_element_type=jnp.float32
    )
    total_rows = lax.axis_size("seq") * lax.axis_size("dp") * num_rows
    grad_scale = jnp.float32(1.0) / jnp.sqrt(jnp.float32(total_rows))
    seqs, shares = lax.axis_size("seq"), lax.axis_size("dp")
    grads = jnp.concatenate([d_query, d_keys, d_values], axis=1)
    term_qkv = jnp.einsum("td,tk->dk", in_rows, grads, preferred_element_type=jnp.float32) * grad_scale
    grad_blocks = grad_rows.reshape(num_rows, seqs, shares, -1)
    term_out = jnp.einsum(
        "tspr,tk->psrk", grad_blocks, attention, preferred_element_type=jnp.float32
    ) * grad_scale
    term_out = term_out.reshape(shares, -1, width)
    term_qkv, head_terms, term_out = lax.optimization_barrier((term_qkv, head_terms, term_out))
    summed = lax.psum_scatter(term_qkv, "seq", scatter_dimension=0, tiled=True)
    input_grad, out_shared = ring_scatter(
        [(head_terms, "head", jnp.bfloat16), (term_out, "dp", jnp.float32)], 0
    )
    input_grad = input_grad[None]
    summed, input_grad, out_shared = lax.optimization_barrier((summed, input_grad, out_shared))
    summed, out_summed = ring_scatter(
        [
            (summed.reshape(shares, -1, summed.shape[1]), "dp", jnp.float32),
            (out_shared.reshape(seqs, -1, width), "seq", jnp.float32),
        ],
        1,
    )
    grad_query = summed[:, :width]
    grad_key = summed[:, width:2 * width]
    grad_value = summed[:, 2 * width:]
    grad_out = out_summed.T
    return (input_grad, grad_query, grad_key, grad_value, grad_out)


def solution(mesh):
    return jax.shard_map(
        local,
        mesh=mesh,
        in_specs=(
            P("dp", "seq", None),
            P(None, "head"),
            P(None, "head"),
            P(None, "head"),
            P("head", None),
            P("dp", "seq", None),
        ),
        out_specs=(
            P("dp", "seq", "head"),
            P(("seq", "dp"), "head"),
            P(("seq", "dp"), "head"),
            P(("seq", "dp"), "head"),
            P("head", ("seq", "dp")),
        ),
        check_vma=False,
    )
```

```python
import functools

import jax
import jax.numpy as jnp
from jax import lax
from jax.experimental import pallas as pl
from jax.experimental.pallas import tpu as pltpu
from jax.sharding import PartitionSpec as P

HEAD_DIM = 128
MESH = pl.DeviceIdType.MESH
PIECES = 2


def ring_scatter_kernel(jobs, *refs):
    count = len(jobs)
    terms, outs, scratch = refs[:count], refs[count:2 * count], refs[2 * count:]
    barrier = pltpu.get_barrier_semaphore()
    places = []
    for axis, n in jobs:
        me = lax.axis_index(axis)
        right, left = lax.rem(me + 1, n), lax.rem(me + n - 1, n)
        places.append((me, right, left))
        for neighbour in (left, right):
            pl.semaphore_signal(barrier, inc=1, device_id={axis: neighbour}, device_id_type=MESH)
    pl.semaphore_wait(barrier, 2 * count)
    ways = [(way, piece) for piece in range(PIECES) for way in range(2)]
    copies = [[[] for _ in ways] for _ in jobs]
    for step in range(max(n for _, n in jobs) - 1):
        for job, (axis, n) in enumerate(jobs):
            if step >= n - 1:
                continue
            me, right, left = places[job]
            recv, sendbuf, send_sem, recv_sem = scratch[4 * job:4 * job + 4]
            term_ref = terms[job]
            rows, half = outs[job].shape[0] // PIECES, outs[job].shape[1] // 2
            for slot, (way, piece) in enumerate(ways):
                dest, sign = ((right, -1), (left, 1))[way]
                block = lax.rem(me + n + sign * (step + 1), n)
                span = (pl.ds(piece * rows, rows), pl.ds(way * half, half))
                if step == 0:
                    src = term_ref.at[block, span[0], span[1]]
                else:
                    copies[job][slot][step - 1].wait_recv()
                    sendbuf[slot, step] = recv[slot, step - 1] + term_ref[block, span[0], span[1]]
                    src = sendbuf.at[slot, step]
                copy = pltpu.make_async_remote_copy(
                    src_ref=src,
                    dst_ref=recv.at[slot, step],
                    send_sem=send_sem.at[slot, step],
                    recv_sem=recv_sem.at[slot, step],
                    device_id={axis: dest},
                    device_id_type=MESH,
                )
                copy.start()
                copies[job][slot].append(copy)
    for job, (axis, n) in enumerate(jobs):
        me = places[job][0]
        recv = scratch[4 * job]
        rows, half = outs[job].shape[0] // PIECES, outs[job].shape[1] // 2
        for slot, (way, piece) in enumerate(ways):
            span = (pl.ds(piece * rows, rows), pl.ds(way * half, half))
            copies[job][slot][n - 2].wait_recv()
            outs[job][span[0], span[1]] = (
                recv[slot, n - 2] + terms[job][me, span[0], span[1]]
            ).astype(outs[job].dtype)
    for job in range(count):
        for slot in range(len(ways)):
            for copy in copies[job][slot]:
                copy.wait_send()


def ring_scatter(parts, channel):
    jobs = tuple((axis, terms.shape[0]) for terms, axis, _ in parts)
    scratch = []
    for terms, _, _ in parts:
        n, rows, width = terms.shape
        scratch += [
            pltpu.VMEM((2 * PIECES, n - 1, rows // PIECES, width // 2), jnp.float32),
            pltpu.VMEM((2 * PIECES, n - 1, rows // PIECES, width // 2), jnp.float32),
            pltpu.SemaphoreType.DMA((2 * PIECES, n - 1)),
            pltpu.SemaphoreType.DMA((2 * PIECES, n - 1)),
        ]
    size = sum(terms.size for terms, _, _ in parts)
    return pl.pallas_call(
        functools.partial(ring_scatter_kernel, jobs),
        out_shape=tuple(
            jax.ShapeDtypeStruct(terms.shape[1:], dtype) for terms, _, dtype in parts
        ),
        in_specs=[pl.BlockSpec(memory_space=pltpu.VMEM)] * len(parts),
        out_specs=tuple(pl.BlockSpec(memory_space=pltpu.VMEM) for _ in parts),
        scratch_shapes=scratch,
        compiler_params=pltpu.CompilerParams(
            collective_id=channel, has_side_effects=True, vmem_limit_bytes=48 * 1024 * 1024
        ),
        cost_estimate=pl.CostEstimate(flops=2 * size, bytes_accessed=8 * size, transcendentals=0),
    )(*(terms for terms, _, _ in parts))


def exchange_kernel(n, axis, kv_ref, qg_ref, prefix_ref, suffix_ref, kv_in, qg_in, send_sem, recv_sem):
    me = lax.axis_index(axis)
    barrier = pltpu.get_barrier_semaphore()
    for offset in range(1, n):
        pl.semaphore_signal(
            barrier, inc=1, device_id={axis: lax.rem(me + offset, n)}, device_id_type=MESH
        )
    pl.semaphore_wait(barrier, n - 1)

    def route(offset, later):
        peer = lax.rem(me + offset, n)
        kind = 0 if later else 1
        return pltpu.make_async_remote_copy(
            src_ref=kv_ref if later else qg_ref,
            dst_ref=(kv_in if later else qg_in).at[me],
            send_sem=send_sem.at[kind, offset],
            recv_sem=recv_sem.at[kind, me],
            device_id={axis: peer},
            device_id_type=MESH,
        )

    for offset in range(1, n):
        for later in (True, False):
            @pl.when((me + offset < n) == later)
            def _():
                route(offset, later).start()

    prefix_ref[...] = jnp.zeros_like(prefix_ref)
    suffix_ref[...] = jnp.zeros_like(suffix_ref)
    for peer in range(n):
        @pl.when(peer < me)
        def _():
            pltpu.make_async_remote_copy(
                src_ref=kv_ref, dst_ref=kv_in.at[peer], send_sem=send_sem.at[0, 0],
                recv_sem=recv_sem.at[0, peer], device_id={axis: peer}, device_id_type=MESH,
            ).wait_recv()
            prefix_ref[...] += kv_in[peer]

        @pl.when(peer > me)
        def _():
            pltpu.make_async_remote_copy(
                src_ref=qg_ref, dst_ref=qg_in.at[peer], send_sem=send_sem.at[1, 0],
                recv_sem=recv_sem.at[1, peer], device_id={axis: peer}, device_id_type=MESH,
            ).wait_recv()
            suffix_ref[...] += qg_in[peer]

    for offset in range(1, n):
        for later in (True, False):
            @pl.when((me + offset < n) == later)
            def _():
                route(offset, later).wait_send()


def exchange_states(kv_state, qg_state, axis):
    n = lax.axis_size(axis)
    shape = kv_state.shape
    return pl.pallas_call(
        functools.partial(exchange_kernel, n, axis),
        out_shape=(jax.ShapeDtypeStruct(shape, jnp.float32),) * 2,
        in_specs=[pl.BlockSpec(memory_space=pltpu.VMEM)] * 2,
        out_specs=(pl.BlockSpec(memory_space=pltpu.VMEM),) * 2,
        scratch_shapes=[
            pltpu.VMEM((n,) + shape, jnp.float32),
            pltpu.VMEM((n,) + shape, jnp.float32),
            pltpu.SemaphoreType.DMA((2, n)),
            pltpu.SemaphoreType.DMA((2, n)),
        ],
        compiler_params=pltpu.CompilerParams(collective_id=2, has_side_effects=True),
    )(kv_state, qg_state)


def local(layer_input, w_query, w_key, w_value, w_out, out_grad):
    num_rows = layer_input.shape[1]
    local_heads = w_query.shape[1] // HEAD_DIM
    width = local_heads * HEAD_DIM
    in_rows = layer_input[0]
    grad_rows = out_grad[0]

    def project(weight):
        result = jnp.dot(in_rows, weight, preferred_element_type=jnp.float32).astype(jnp.bfloat16)
        return result.reshape(num_rows, local_heads, HEAD_DIM)

    queries = project(w_query)
    key_rows = project(w_key)
    value_rows = project(w_value)
    row_start = lax.axis_index("seq") * num_rows
    positions = (row_start + jnp.arange(num_rows, dtype=jnp.int32)).astype(jnp.float32)
    pos_scale = 1.0 / jnp.sqrt(HEAD_DIM * (positions + 1.0))
    backward = jnp.einsum("td,kd->tk", grad_rows, w_out, preferred_element_type=jnp.float32)
    grad_in = (
        (backward * pos_scale[:, None])
        .astype(jnp.bfloat16)
        .reshape(num_rows, local_heads, HEAD_DIM)
    )
    kv_state = jnp.einsum("thd,the->hde", key_rows, value_rows, preferred_element_type=jnp.float32)
    qg_state = jnp.einsum("thd,the->hde", queries, grad_in, preferred_element_type=jnp.float32)
    prefix, suffix = exchange_states(kv_state, qg_state, "seq")
    prefix = prefix.astype(jnp.bfloat16)
    suffix = suffix.astype(jnp.bfloat16)
    causal = (jnp.arange(num_rows)[:, None] >= jnp.arange(num_rows)[None, :])[None]
    scores = jnp.einsum("thd,shd->hts", queries, key_rows, preferred_element_type=jnp.float32)
    scores_qk = jnp.where(causal, scores, 0.0).astype(jnp.bfloat16)
    scores_g = jnp.einsum("thd,shd->hts", grad_in, value_rows, preferred_element_type=jnp.float32)
    scores_gv = jnp.where(causal, scores_g, 0.0).astype(jnp.bfloat16)
    inner_sum = jnp.einsum(
        "hts,she->the", scores_qk, value_rows, preferred_element_type=jnp.float32
    )
    cross_sum = jnp.einsum("thd,hde->the", queries, prefix, preferred_element_type=jnp.float32)
    attention = (
        ((inner_sum + cross_sum) * pos_scale[:, None, None])
        .astype(jnp.bfloat16)
        .reshape(num_rows, width)
    )
    d_query = jnp.einsum("hts,shd->thd", scores_gv, key_rows, preferred_element_type=jnp.float32)
    d_query = d_query + jnp.einsum(
        "the,hde->thd", grad_in, prefix, preferred_element_type=jnp.float32
    )
    d_keys = jnp.einsum("hts,thd->shd", scores_gv, queries, preferred_element_type=jnp.float32)
    d_keys = d_keys + jnp.einsum(
        "she,hde->shd", value_rows, suffix, preferred_element_type=jnp.float32
    )
    d_values = jnp.einsum("hts,the->she", scores_qk, grad_in, preferred_element_type=jnp.float32)
    d_values = d_values + jnp.einsum(
        "shd,hde->she", key_rows, suffix, preferred_element_type=jnp.float32
    )
    d_query = d_query.astype(jnp.bfloat16).reshape(num_rows, width)
    d_keys = d_keys.astype(jnp.bfloat16).reshape(num_rows, width)
    d_values = d_values.astype(jnp.bfloat16).reshape(num_rows, width)
    groups = lax.axis_size("head")

    def by_block(weight):
        return weight.reshape(groups, weight.shape[0] // groups, width)

    head_terms = jnp.einsum("tk,bdk->btd", d_query, by_block(w_query), preferred_element_type=jnp.float32)
    head_terms = head_terms + jnp.einsum(
        "tk,bdk->btd", d_keys, by_block(w_key), preferred_element_type=jnp.float32
    )
    head_terms = head_terms + jnp.einsum(
        "tk,bdk->btd", d_values, by_block(w_value), preferred_element_type=jnp.float32
    )
    total_rows = lax.axis_size("seq") * lax.axis_size("dp") * num_rows
    grad_scale = jnp.float32(1.0) / jnp.sqrt(jnp.float32(total_rows))
    seqs, shares = lax.axis_size("seq"), lax.axis_size("dp")
    grads = jnp.concatenate([d_query, d_keys, d_values], axis=1)
    term_qkv = jnp.einsum("td,tk->dk", in_rows, grads, preferred_element_type=jnp.float32) * grad_scale
    grad_blocks = grad_rows.reshape(num_rows, seqs, shares, -1)
    term_out = jnp.einsum(
        "tspr,tk->psrk", grad_blocks, attention, preferred_element_type=jnp.float32
    ) * grad_scale
    term_out = term_out.reshape(shares, -1, width)
    term_qkv, head_terms, term_out = lax.optimization_barrier((term_qkv, head_terms, term_out))
    summed = lax.psum_scatter(term_qkv, "seq", scatter_dimension=0, tiled=True)
    input_grad, out_shared = ring_scatter(
        [(head_terms, "head", jnp.bfloat16), (term_out, "dp", jnp.float32)], 0
    )
    input_grad = input_grad[None]
    summed, input_grad, out_shared = lax.optimization_barrier((summed, input_grad, out_shared))
    out_summed = lax.psum_scatter(out_shared, "seq", scatter_dimension=0, tiled=True)
    (summed,) = ring_scatter([(summed.reshape(shares, -1, summed.shape[1]), "dp", jnp.float32)], 1)
    grad_query = summed[:, :width]
    grad_key = summed[:, width:2 * width]
    grad_value = summed[:, 2 * width:]
    grad_out = out_summed.T
    return (input_grad, grad_query, grad_key, grad_value, grad_out)


def solution(mesh):
    return jax.shard_map(
        local,
        mesh=mesh,
        in_specs=(
            P("dp", "seq", None),
            P(None, "head"),
            P(None, "head"),
            P(None, "head"),
            P("head", None),
            P("dp", "seq", None),
        ),
        out_specs=(
            P("dp", "seq", "head"),
            P(("seq", "dp"), "head"),
            P(("seq", "dp"), "head"),
            P(("seq", "dp"), "head"),
            P("head", ("seq", "dp")),
        ),
        check_vma=False,
    )
```

```python
import functools

import jax
import jax.numpy as jnp
from jax import lax
from jax.experimental import pallas as pl
from jax.experimental.pallas import tpu as pltpu
from jax.sharding import PartitionSpec as P

HEAD_DIM = 128
MESH = pl.DeviceIdType.MESH


def ring_scatter_kernel(jobs, *refs):
    count = len(jobs)
    terms, outs, scratch = refs[:count], refs[count:2 * count], refs[2 * count:]
    barrier = pltpu.get_barrier_semaphore()
    places, greeted = [], 0
    for axis, n, _, direct in jobs:
        me = lax.axis_index(axis)
        right, left = lax.rem(me + 1, n), lax.rem(me + n - 1, n)
        places.append((me, right, left))
        offsets = range(1, n) if direct else (n - 1, 1)
        for offset in offsets:
            pl.semaphore_signal(
                barrier, inc=1, device_id={axis: lax.rem(me + offset, n)}, device_id_type=MESH
            )
        greeted += len(offsets)
    pl.semaphore_wait(barrier, greeted)

    def direct_copy(job, offset):
        axis, n, _, _ = jobs[job]
        me = places[job][0]
        recv, send_sem, recv_sem = scratch[4 * job], scratch[4 * job + 2], scratch[4 * job + 3]
        peer = lax.rem(me + offset, n)
        return pltpu.make_async_remote_copy(
            src_ref=terms[job].at[peer],
            dst_ref=recv.at[me],
            send_sem=send_sem.at[offset],
            recv_sem=recv_sem.at[me],
            device_id={axis: peer},
            device_id_type=MESH,
        )

    for job, (axis, n, _, direct) in enumerate(jobs):
        if direct:
            for offset in range(1, n):
                direct_copy(job, offset).start()

    copies = [[[] for _ in range(2 * pieces)] for _, _, pieces, _ in jobs]
    for step in range(max(n for _, n, _, _ in jobs) - 1):
        for job, (axis, n, pieces, direct) in enumerate(jobs):
            if direct or step >= n - 1:
                continue
            me, right, left = places[job]
            recv, sendbuf, send_sem, recv_sem = scratch[4 * job:4 * job + 4]
            term_ref = terms[job]
            rows, half = outs[job].shape[0] // pieces, outs[job].shape[1] // 2
            for slot in range(2 * pieces):
                piece, way = divmod(slot, 2)
                dest, sign = ((right, -1), (left, 1))[way]
                block = lax.rem(me + n + sign * (step + 1), n)
                span = (pl.ds(piece * rows, rows), pl.ds(way * half, half))
                if step == 0:
                    src = term_ref.at[block, span[0], span[1]]
                else:
                    copies[job][slot][step - 1].wait_recv()
                    sendbuf[slot, step] = recv[slot, step - 1] + term_ref[block, span[0], span[1]]
                    src = sendbuf.at[slot, step]
                copy = pltpu.make_async_remote_copy(
                    src_ref=src,
                    dst_ref=recv.at[slot, step],
                    send_sem=send_sem.at[slot, step],
                    recv_sem=recv_sem.at[slot, step],
                    device_id={axis: dest},
                    device_id_type=MESH,
                )
                copy.start()
                copies[job][slot].append(copy)
    for job, (axis, n, pieces, direct) in enumerate(jobs):
        me = places[job][0]
        recv = scratch[4 * job]
        if direct:
            outs[job][...] = terms[job][me]
            for sender in range(n):
                @pl.when(sender != me)
                def _():
                    pltpu.make_async_remote_copy(
                        src_ref=terms[job].at[sender],
                        dst_ref=recv.at[sender],
                        send_sem=scratch[4 * job + 2].at[0],
                        recv_sem=scratch[4 * job + 3].at[sender],
                        device_id={axis: sender},
                        device_id_type=MESH,
                    ).wait_recv()
                    outs[job][...] += recv[sender]
            continue
        rows, half = outs[job].shape[0] // pieces, outs[job].shape[1] // 2
        for slot in range(2 * pieces):
            piece, way = divmod(slot, 2)
            span = (pl.ds(piece * rows, rows), pl.ds(way * half, half))
            copies[job][slot][n - 2].wait_recv()
            outs[job][span[0], span[1]] = (
                recv[slot, n - 2] + terms[job][me, span[0], span[1]]
            ).astype(outs[job].dtype)
    for job, (axis, n, pieces, direct) in enumerate(jobs):
        if direct:
            for offset in range(1, n):
                direct_copy(job, offset).wait_send()
        for slot in range(2 * pieces):
            for copy in copies[job][slot]:
                copy.wait_send()


def ring_scatter(parts, channel):
    jobs = tuple((axis, terms.shape[0], pieces, direct) for terms, axis, _, pieces, direct in parts)
    scratch = []
    for terms, _, _, pieces, direct in parts:
        n, rows, width = terms.shape
        if direct:
            scratch += [
                pltpu.VMEM((n, rows, width), jnp.float32),
                pltpu.VMEM((8, 128), jnp.float32),
                pltpu.SemaphoreType.DMA((n,)),
                pltpu.SemaphoreType.DMA((n,)),
            ]
            continue
        scratch += [
            pltpu.VMEM((2 * pieces, n - 1, rows // pieces, width // 2), jnp.float32),
            pltpu.VMEM((2 * pieces, n - 1, rows // pieces, width // 2), jnp.float32),
            pltpu.SemaphoreType.DMA((2 * pieces, n - 1)),
            pltpu.SemaphoreType.DMA((2 * pieces, n - 1)),
        ]
    size = sum(part[0].size for part in parts)
    return pl.pallas_call(
        functools.partial(ring_scatter_kernel, jobs),
        out_shape=tuple(
            jax.ShapeDtypeStruct(part[0].shape[1:], part[2]) for part in parts
        ),
        in_specs=[pl.BlockSpec(memory_space=pltpu.VMEM)] * len(parts),
        out_specs=tuple(pl.BlockSpec(memory_space=pltpu.VMEM) for _ in parts),
        scratch_shapes=scratch,
        compiler_params=pltpu.CompilerParams(
            collective_id=channel, has_side_effects=True, vmem_limit_bytes=48 * 1024 * 1024
        ),
        cost_estimate=pl.CostEstimate(flops=2 * size, bytes_accessed=8 * size, transcendentals=0),
    )(*(part[0] for part in parts))


def exchange_kernel(n, axis, kv_ref, qg_ref, prefix_ref, suffix_ref, kv_in, qg_in, send_sem, recv_sem):
    me = lax.axis_index(axis)
    barrier = pltpu.get_barrier_semaphore()
    for offset in range(1, n):
        pl.semaphore_signal(
            barrier, inc=1, device_id={axis: lax.rem(me + offset, n)}, device_id_type=MESH
        )
    pl.semaphore_wait(barrier, n - 1)

    def route(offset, later):
        peer = lax.rem(me + offset, n)
        kind = 0 if later else 1
        return pltpu.make_async_remote_copy(
            src_ref=kv_ref if later else qg_ref,
            dst_ref=(kv_in if later else qg_in).at[me],
            send_sem=send_sem.at[kind, offset],
            recv_sem=recv_sem.at[kind, me],
            device_id={axis: peer},
            device_id_type=MESH,
        )

    for offset in range(1, n):
        for later in (True, False):
            @pl.when((me + offset < n) == later)
            def _():
                route(offset, later).start()

    prefix_ref[...] = jnp.zeros_like(prefix_ref)
    suffix_ref[...] = jnp.zeros_like(suffix_ref)
    for peer in range(n):
        @pl.when(peer < me)
        def _():
            pltpu.make_async_remote_copy(
                src_ref=kv_ref, dst_ref=kv_in.at[peer], send_sem=send_sem.at[0, 0],
                recv_sem=recv_sem.at[0, peer], device_id={axis: peer}, device_id_type=MESH,
            ).wait_recv()
            prefix_ref[...] += kv_in[peer]

        @pl.when(peer > me)
        def _():
            pltpu.make_async_remote_copy(
                src_ref=qg_ref, dst_ref=qg_in.at[peer], send_sem=send_sem.at[1, 0],
                recv_sem=recv_sem.at[1, peer], device_id={axis: peer}, device_id_type=MESH,
            ).wait_recv()
            suffix_ref[...] += qg_in[peer]

    for offset in range(1, n):
        for later in (True, False):
            @pl.when((me + offset < n) == later)
            def _():
                route(offset, later).wait_send()


def exchange_states(kv_state, qg_state, axis):
    n = lax.axis_size(axis)
    shape = kv_state.shape
    return pl.pallas_call(
        functools.partial(exchange_kernel, n, axis),
        out_shape=(jax.ShapeDtypeStruct(shape, jnp.float32),) * 2,
        in_specs=[pl.BlockSpec(memory_space=pltpu.VMEM)] * 2,
        out_specs=(pl.BlockSpec(memory_space=pltpu.VMEM),) * 2,
        scratch_shapes=[
            pltpu.VMEM((n,) + shape, jnp.float32),
            pltpu.VMEM((n,) + shape, jnp.float32),
            pltpu.SemaphoreType.DMA((2, n)),
            pltpu.SemaphoreType.DMA((2, n)),
        ],
        compiler_params=pltpu.CompilerParams(collective_id=2, has_side_effects=True),
    )(kv_state, qg_state)


def local(layer_input, w_query, w_key, w_value, w_out, out_grad):
    num_rows = layer_input.shape[1]
    local_heads = w_query.shape[1] // HEAD_DIM
    width = local_heads * HEAD_DIM
    in_rows = layer_input[0]
    grad_rows = out_grad[0]

    def project(weight):
        result = jnp.dot(in_rows, weight, preferred_element_type=jnp.float32).astype(jnp.bfloat16)
        return result.reshape(num_rows, local_heads, HEAD_DIM)

    queries = project(w_query)
    key_rows = project(w_key)
    value_rows = project(w_value)
    row_start = lax.axis_index("seq") * num_rows
    positions = (row_start + jnp.arange(num_rows, dtype=jnp.int32)).astype(jnp.float32)
    pos_scale = 1.0 / jnp.sqrt(HEAD_DIM * (positions + 1.0))
    backward = jnp.einsum("td,kd->tk", grad_rows, w_out, preferred_element_type=jnp.float32)
    grad_in = (
        (backward * pos_scale[:, None])
        .astype(jnp.bfloat16)
        .reshape(num_rows, local_heads, HEAD_DIM)
    )
    kv_state = jnp.einsum("thd,the->hde", key_rows, value_rows, preferred_element_type=jnp.float32)
    qg_state = jnp.einsum("thd,the->hde", queries, grad_in, preferred_element_type=jnp.float32)
    prefix, suffix = exchange_states(kv_state, qg_state, "seq")
    prefix = prefix.astype(jnp.bfloat16)
    suffix = suffix.astype(jnp.bfloat16)
    causal = (jnp.arange(num_rows)[:, None] >= jnp.arange(num_rows)[None, :])[None]
    scores = jnp.einsum("thd,shd->hts", queries, key_rows, preferred_element_type=jnp.float32)
    scores_qk = jnp.where(causal, scores, 0.0).astype(jnp.bfloat16)
    scores_g = jnp.einsum("thd,shd->hts", grad_in, value_rows, preferred_element_type=jnp.float32)
    scores_gv = jnp.where(causal, scores_g, 0.0).astype(jnp.bfloat16)
    inner_sum = jnp.einsum(
        "hts,she->the", scores_qk, value_rows, preferred_element_type=jnp.float32
    )
    cross_sum = jnp.einsum("thd,hde->the", queries, prefix, preferred_element_type=jnp.float32)
    attention = (
        ((inner_sum + cross_sum) * pos_scale[:, None, None])
        .astype(jnp.bfloat16)
        .reshape(num_rows, width)
    )
    d_query = jnp.einsum("hts,shd->thd", scores_gv, key_rows, preferred_element_type=jnp.float32)
    d_query = d_query + jnp.einsum(
        "the,hde->thd", grad_in, prefix, preferred_element_type=jnp.float32
    )
    d_keys = jnp.einsum("hts,thd->shd", scores_gv, queries, preferred_element_type=jnp.float32)
    d_keys = d_keys + jnp.einsum(
        "she,hde->shd", value_rows, suffix, preferred_element_type=jnp.float32
    )
    d_values = jnp.einsum("hts,the->she", scores_qk, grad_in, preferred_element_type=jnp.float32)
    d_values = d_values + jnp.einsum(
        "shd,hde->she", key_rows, suffix, preferred_element_type=jnp.float32
    )
    d_query = d_query.astype(jnp.bfloat16).reshape(num_rows, width)
    d_keys = d_keys.astype(jnp.bfloat16).reshape(num_rows, width)
    d_values = d_values.astype(jnp.bfloat16).reshape(num_rows, width)
    groups = lax.axis_size("head")

    def by_block(weight):
        return weight.reshape(groups, weight.shape[0] // groups, width)

    head_terms = jnp.einsum("tk,bdk->btd", d_query, by_block(w_query), preferred_element_type=jnp.float32)
    head_terms = head_terms + jnp.einsum(
        "tk,bdk->btd", d_keys, by_block(w_key), preferred_element_type=jnp.float32
    )
    head_terms = head_terms + jnp.einsum(
        "tk,bdk->btd", d_values, by_block(w_value), preferred_element_type=jnp.float32
    )
    total_rows = lax.axis_size("seq") * lax.axis_size("dp") * num_rows
    grad_scale = jnp.float32(1.0) / jnp.sqrt(jnp.float32(total_rows))
    seqs, shares = lax.axis_size("seq"), lax.axis_size("dp")
    grads = jnp.concatenate([d_query, d_keys, d_values], axis=1)
    term_qkv = jnp.einsum("td,tk->dk", in_rows, grads, preferred_element_type=jnp.float32) * grad_scale
    grad_blocks = grad_rows.reshape(num_rows, seqs, shares, -1)
    term_out = jnp.einsum(
        "tspr,tk->psrk", grad_blocks, attention, preferred_element_type=jnp.float32
    ) * grad_scale
    term_out = term_out.reshape(shares, -1, width)
    term_qkv, head_terms, term_out = lax.optimization_barrier((term_qkv, head_terms, term_out))
    summed = lax.psum_scatter(term_qkv, "seq", scatter_dimension=0, tiled=True)
    input_grad, out_shared = ring_scatter(
        [(head_terms, "head", jnp.bfloat16, 4, False), (term_out, "dp", jnp.float32, 2, False)], 0
    )
    input_grad = input_grad[None]
    summed, input_grad, out_shared = lax.optimization_barrier((summed, input_grad, out_shared))
    summed, out_summed = ring_scatter(
        [
            (summed.reshape(shares, -1, summed.shape[1]), "dp", jnp.float32, 2, False),
            (out_shared.reshape(seqs, -1, width), "seq", jnp.float32, 1, True),
        ],
        1,
    )
    grad_query = summed[:, :width]
    grad_key = summed[:, width:2 * width]
    grad_value = summed[:, 2 * width:]
    grad_out = out_summed.T
    return (input_grad, grad_query, grad_key, grad_value, grad_out)


def solution(mesh):
    return jax.shard_map(
        local,
        mesh=mesh,
        in_specs=(
            P("dp", "seq", None),
            P(None, "head"),
            P(None, "head"),
            P(None, "head"),
            P("head", None),
            P("dp", "seq", None),
        ),
        out_specs=(
            P("dp", "seq", "head"),
            P(("seq", "dp"), "head"),
            P(("seq", "dp"), "head"),
            P(("seq", "dp"), "head"),
            P("head", ("seq", "dp")),
        ),
        check_vma=False,
    )
```

```python
import functools

import jax
import jax.numpy as jnp
from jax import lax
from jax.experimental import pallas as pl
from jax.experimental.pallas import tpu as pltpu
from jax.sharding import PartitionSpec as P

HEAD_DIM = 128
MESH = pl.DeviceIdType.MESH


def ring_scatter_kernel(jobs, *refs):
    count = len(jobs)
    terms, outs, scratch = refs[:count], refs[count:2 * count], refs[2 * count:]
    barrier = pltpu.get_barrier_semaphore()
    places, greeted = [], 0
    for axis, n, _, direct in jobs:
        me = lax.axis_index(axis)
        right, left = lax.rem(me + 1, n), lax.rem(me + n - 1, n)
        places.append((me, right, left))
        offsets = range(1, n) if direct else (n - 1, 1)
        for offset in offsets:
            pl.semaphore_signal(
                barrier, inc=1, device_id={axis: lax.rem(me + offset, n)}, device_id_type=MESH
            )
        greeted += len(offsets)
    pl.semaphore_wait(barrier, greeted)

    def direct_copy(job, offset):
        axis, n, _, _ = jobs[job]
        me = places[job][0]
        recv, send_sem, recv_sem = scratch[4 * job], scratch[4 * job + 2], scratch[4 * job + 3]
        peer = lax.rem(me + offset, n)
        return pltpu.make_async_remote_copy(
            src_ref=terms[job].at[peer],
            dst_ref=recv.at[me],
            send_sem=send_sem.at[offset],
            recv_sem=recv_sem.at[me],
            device_id={axis: peer},
            device_id_type=MESH,
        )

    for job, (axis, n, _, direct) in enumerate(jobs):
        if direct:
            for offset in range(1, n):
                direct_copy(job, offset).start()

    copies = [[[] for _ in range(2 * pieces)] for _, _, pieces, _ in jobs]
    for step in range(max(n for _, n, _, _ in jobs) - 1):
        for job, (axis, n, pieces, direct) in enumerate(jobs):
            if direct or step >= n - 1:
                continue
            me, right, left = places[job]
            recv, sendbuf, send_sem, recv_sem = scratch[4 * job:4 * job + 4]
            term_ref = terms[job]
            rows, half = outs[job].shape[0] // pieces, outs[job].shape[1] // 2
            for slot in range(2 * pieces):
                piece, way = divmod(slot, 2)
                dest, sign = ((right, -1), (left, 1))[way]
                block = lax.rem(me + n + sign * (step + 1), n)
                span = (pl.ds(piece * rows, rows), pl.ds(way * half, half))
                if step == 0:
                    src = term_ref.at[block, span[0], span[1]]
                else:
                    copies[job][slot][step - 1].wait_recv()
                    sendbuf[slot, step] = recv[slot, step - 1] + term_ref[block, span[0], span[1]]
                    src = sendbuf.at[slot, step]
                copy = pltpu.make_async_remote_copy(
                    src_ref=src,
                    dst_ref=recv.at[slot, step],
                    send_sem=send_sem.at[slot, step],
                    recv_sem=recv_sem.at[slot, step],
                    device_id={axis: dest},
                    device_id_type=MESH,
                )
                copy.start()
                copies[job][slot].append(copy)
    for job, (axis, n, pieces, direct) in enumerate(jobs):
        me = places[job][0]
        recv = scratch[4 * job]
        if direct:
            outs[job][...] = terms[job][me]
            for sender in range(n):
                @pl.when(sender != me)
                def _():
                    pltpu.make_async_remote_copy(
                        src_ref=terms[job].at[sender],
                        dst_ref=recv.at[sender],
                        send_sem=scratch[4 * job + 2].at[0],
                        recv_sem=scratch[4 * job + 3].at[sender],
                        device_id={axis: sender},
                        device_id_type=MESH,
                    ).wait_recv()
                    outs[job][...] += recv[sender]
            continue
        rows, half = outs[job].shape[0] // pieces, outs[job].shape[1] // 2
        for slot in range(2 * pieces):
            piece, way = divmod(slot, 2)
            span = (pl.ds(piece * rows, rows), pl.ds(way * half, half))
            copies[job][slot][n - 2].wait_recv()
            outs[job][span[0], span[1]] = (
                recv[slot, n - 2] + terms[job][me, span[0], span[1]]
            ).astype(outs[job].dtype)
    for job, (axis, n, pieces, direct) in enumerate(jobs):
        if direct:
            for offset in range(1, n):
                direct_copy(job, offset).wait_send()
        for slot in range(2 * pieces):
            for copy in copies[job][slot]:
                copy.wait_send()


def ring_scatter(parts, channel):
    jobs = tuple((axis, terms.shape[0], pieces, direct) for terms, axis, _, pieces, direct in parts)
    scratch = []
    for terms, _, _, pieces, direct in parts:
        n, rows, width = terms.shape
        if direct:
            scratch += [
                pltpu.VMEM((n, rows, width), jnp.float32),
                pltpu.VMEM((8, 128), jnp.float32),
                pltpu.SemaphoreType.DMA((n,)),
                pltpu.SemaphoreType.DMA((n,)),
            ]
            continue
        scratch += [
            pltpu.VMEM((2 * pieces, n - 1, rows // pieces, width // 2), jnp.float32),
            pltpu.VMEM((2 * pieces, n - 1, rows // pieces, width // 2), jnp.float32),
            pltpu.SemaphoreType.DMA((2 * pieces, n - 1)),
            pltpu.SemaphoreType.DMA((2 * pieces, n - 1)),
        ]
    size = sum(part[0].size for part in parts)
    return pl.pallas_call(
        functools.partial(ring_scatter_kernel, jobs),
        out_shape=tuple(
            jax.ShapeDtypeStruct(part[0].shape[1:], part[2]) for part in parts
        ),
        in_specs=[pl.BlockSpec(memory_space=pltpu.VMEM)] * len(parts),
        out_specs=tuple(pl.BlockSpec(memory_space=pltpu.VMEM) for _ in parts),
        scratch_shapes=scratch,
        compiler_params=pltpu.CompilerParams(
            collective_id=channel, has_side_effects=True, vmem_limit_bytes=48 * 1024 * 1024
        ),
        cost_estimate=pl.CostEstimate(flops=2 * size, bytes_accessed=8 * size, transcendentals=0),
    )(*(part[0] for part in parts))


def exchange_kernel(n, axis, kv_ref, qg_ref, prefix_ref, suffix_ref, kv_in, qg_in, send_sem, recv_sem):
    me = lax.axis_index(axis)
    barrier = pltpu.get_barrier_semaphore()
    for offset in range(1, n):
        pl.semaphore_signal(
            barrier, inc=1, device_id={axis: lax.rem(me + offset, n)}, device_id_type=MESH
        )
    pl.semaphore_wait(barrier, n - 1)

    def route(offset, later):
        peer = lax.rem(me + offset, n)
        kind = 0 if later else 1
        return pltpu.make_async_remote_copy(
            src_ref=kv_ref if later else qg_ref,
            dst_ref=(kv_in if later else qg_in).at[me],
            send_sem=send_sem.at[kind, offset],
            recv_sem=recv_sem.at[kind, me],
            device_id={axis: peer},
            device_id_type=MESH,
        )

    for offset in range(1, n):
        for later in (True, False):
            @pl.when((me + offset < n) == later)
            def _():
                route(offset, later).start()

    prefix_ref[...] = jnp.zeros_like(prefix_ref)
    suffix_ref[...] = jnp.zeros_like(suffix_ref)
    for peer in range(n):
        @pl.when(peer < me)
        def _():
            pltpu.make_async_remote_copy(
                src_ref=kv_ref, dst_ref=kv_in.at[peer], send_sem=send_sem.at[0, 0],
                recv_sem=recv_sem.at[0, peer], device_id={axis: peer}, device_id_type=MESH,
            ).wait_recv()
            prefix_ref[...] += kv_in[peer]

        @pl.when(peer > me)
        def _():
            pltpu.make_async_remote_copy(
                src_ref=qg_ref, dst_ref=qg_in.at[peer], send_sem=send_sem.at[1, 0],
                recv_sem=recv_sem.at[1, peer], device_id={axis: peer}, device_id_type=MESH,
            ).wait_recv()
            suffix_ref[...] += qg_in[peer]

    for offset in range(1, n):
        for later in (True, False):
            @pl.when((me + offset < n) == later)
            def _():
                route(offset, later).wait_send()


def exchange_states(kv_state, qg_state, axis):
    n = lax.axis_size(axis)
    shape = kv_state.shape
    return pl.pallas_call(
        functools.partial(exchange_kernel, n, axis),
        out_shape=(jax.ShapeDtypeStruct(shape, jnp.float32),) * 2,
        in_specs=[pl.BlockSpec(memory_space=pltpu.VMEM)] * 2,
        out_specs=(pl.BlockSpec(memory_space=pltpu.VMEM),) * 2,
        scratch_shapes=[
            pltpu.VMEM((n,) + shape, jnp.float32),
            pltpu.VMEM((n,) + shape, jnp.float32),
            pltpu.SemaphoreType.DMA((2, n)),
            pltpu.SemaphoreType.DMA((2, n)),
        ],
        compiler_params=pltpu.CompilerParams(collective_id=2, has_side_effects=True),
    )(kv_state, qg_state)


def local(layer_input, w_query, w_key, w_value, w_out, out_grad):
    num_rows = layer_input.shape[1]
    local_heads = w_query.shape[1] // HEAD_DIM
    width = local_heads * HEAD_DIM
    in_rows = layer_input[0]
    grad_rows = out_grad[0]

    def project(weight):
        result = jnp.dot(in_rows, weight, preferred_element_type=jnp.float32).astype(jnp.bfloat16)
        return result.reshape(num_rows, local_heads, HEAD_DIM)

    queries = project(w_query)
    key_rows = project(w_key)
    value_rows = project(w_value)
    row_start = lax.axis_index("seq") * num_rows
    positions = (row_start + jnp.arange(num_rows, dtype=jnp.int32)).astype(jnp.float32)
    pos_scale = 1.0 / jnp.sqrt(HEAD_DIM * (positions + 1.0))
    backward = jnp.einsum("td,kd->tk", grad_rows, w_out, preferred_element_type=jnp.float32)
    grad_in = (
        (backward * pos_scale[:, None])
        .astype(jnp.bfloat16)
        .reshape(num_rows, local_heads, HEAD_DIM)
    )
    kv_state = jnp.einsum("thd,the->hde", key_rows, value_rows, preferred_element_type=jnp.float32)
    qg_state = jnp.einsum("thd,the->hde", queries, grad_in, preferred_element_type=jnp.float32)
    prefix, suffix = exchange_states(kv_state, qg_state, "seq")
    prefix = prefix.astype(jnp.bfloat16)
    suffix = suffix.astype(jnp.bfloat16)
    causal = (jnp.arange(num_rows)[:, None] >= jnp.arange(num_rows)[None, :])[None]
    scores = jnp.einsum("thd,shd->hts", queries, key_rows, preferred_element_type=jnp.float32)
    scores_qk = jnp.where(causal, scores, 0.0).astype(jnp.bfloat16)
    scores_g = jnp.einsum("thd,shd->hts", grad_in, value_rows, preferred_element_type=jnp.float32)
    scores_gv = jnp.where(causal, scores_g, 0.0).astype(jnp.bfloat16)
    inner_sum = jnp.einsum(
        "hts,she->the", scores_qk, value_rows, preferred_element_type=jnp.float32
    )
    cross_sum = jnp.einsum("thd,hde->the", queries, prefix, preferred_element_type=jnp.float32)
    attention = (
        ((inner_sum + cross_sum) * pos_scale[:, None, None])
        .astype(jnp.bfloat16)
        .reshape(num_rows, width)
    )
    d_query = jnp.einsum("hts,shd->thd", scores_gv, key_rows, preferred_element_type=jnp.float32)
    d_query = d_query + jnp.einsum(
        "the,hde->thd", grad_in, prefix, preferred_element_type=jnp.float32
    )
    d_keys = jnp.einsum("hts,thd->shd", scores_gv, queries, preferred_element_type=jnp.float32)
    d_keys = d_keys + jnp.einsum(
        "she,hde->shd", value_rows, suffix, preferred_element_type=jnp.float32
    )
    d_values = jnp.einsum("hts,the->she", scores_qk, grad_in, preferred_element_type=jnp.float32)
    d_values = d_values + jnp.einsum(
        "shd,hde->she", key_rows, suffix, preferred_element_type=jnp.float32
    )
    d_query = d_query.astype(jnp.bfloat16).reshape(num_rows, width)
    d_keys = d_keys.astype(jnp.bfloat16).reshape(num_rows, width)
    d_values = d_values.astype(jnp.bfloat16).reshape(num_rows, width)
    groups = lax.axis_size("head")
    grads = jnp.concatenate([d_query, d_keys, d_values], axis=1)
    w_all = jnp.concatenate([w_query, w_key, w_value], axis=1)
    head_terms = jnp.einsum(
        "tk,bdk->btd", grads, w_all.reshape(groups, w_all.shape[0] // groups, 3 * width),
        preferred_element_type=jnp.float32,
    )
    total_rows = lax.axis_size("seq") * lax.axis_size("dp") * num_rows
    grad_scale = jnp.float32(1.0) / jnp.sqrt(jnp.float32(total_rows))
    seqs, shares = lax.axis_size("seq"), lax.axis_size("dp")
    term_qkv = jnp.einsum("td,tk->dk", in_rows, grads, preferred_element_type=jnp.float32) * grad_scale
    grad_blocks = grad_rows.reshape(num_rows, seqs, shares, -1)
    term_out = jnp.einsum(
        "tspr,tk->psrk", grad_blocks, attention, preferred_element_type=jnp.float32
    ) * grad_scale
    term_out = term_out.reshape(shares, -1, width)
    term_qkv, head_terms, term_out = lax.optimization_barrier((term_qkv, head_terms, term_out))
    summed = lax.psum_scatter(term_qkv, "seq", scatter_dimension=0, tiled=True)
    input_grad, out_shared = ring_scatter(
        [(head_terms, "head", jnp.float32, 4, False), (term_out, "dp", jnp.float32, 2, False)], 0
    )
    input_grad = input_grad.astype(jnp.bfloat16)[None]
    summed, input_grad, out_shared = lax.optimization_barrier((summed, input_grad, out_shared))
    summed, out_summed = ring_scatter(
        [
            (summed.reshape(shares, -1, summed.shape[1]), "dp", jnp.float32, 2, False),
            (out_shared.reshape(seqs, -1, width), "seq", jnp.float32, 1, True),
        ],
        1,
    )
    grad_query = summed[:, :width]
    grad_key = summed[:, width:2 * width]
    grad_value = summed[:, 2 * width:]
    grad_out = out_summed.T
    return (input_grad, grad_query, grad_key, grad_value, grad_out)


def solution(mesh):
    return jax.shard_map(
        local,
        mesh=mesh,
        in_specs=(
            P("dp", "seq", None),
            P(None, "head"),
            P(None, "head"),
            P(None, "head"),
            P("head", None),
            P("dp", "seq", None),
        ),
        out_specs=(
            P("dp", "seq", "head"),
            P(("seq", "dp"), "head"),
            P(("seq", "dp"), "head"),
            P(("seq", "dp"), "head"),
            P("head", ("seq", "dp")),
        ),
        check_vma=False,
    )
```

```python
import functools

import jax
import jax.numpy as jnp
from jax import lax
from jax.experimental import pallas as pl
from jax.experimental.pallas import tpu as pltpu
from jax.sharding import PartitionSpec as P

HEAD_DIM = 128
MESH = pl.DeviceIdType.MESH


def ring_scatter_kernel(jobs, *refs):
    count = len(jobs)
    terms, outs, scratch = refs[:count], refs[count:2 * count], refs[2 * count:]
    barrier = pltpu.get_barrier_semaphore()
    places, greeted = [], 0
    for axis, n, _, direct in jobs:
        me = lax.axis_index(axis)
        right, left = lax.rem(me + 1, n), lax.rem(me + n - 1, n)
        places.append((me, right, left))
        offsets = range(1, n) if direct else (n - 1, 1)
        for offset in offsets:
            pl.semaphore_signal(
                barrier, inc=1, device_id={axis: lax.rem(me + offset, n)}, device_id_type=MESH
            )
        greeted += len(offsets)
    pl.semaphore_wait(barrier, greeted)

    def direct_copy(job, offset):
        axis, n, _, _ = jobs[job]
        me = places[job][0]
        recv, send_sem, recv_sem = scratch[4 * job], scratch[4 * job + 2], scratch[4 * job + 3]
        peer = lax.rem(me + offset, n)
        return pltpu.make_async_remote_copy(
            src_ref=terms[job].at[peer],
            dst_ref=recv.at[me],
            send_sem=send_sem.at[offset],
            recv_sem=recv_sem.at[me],
            device_id={axis: peer},
            device_id_type=MESH,
        )

    for job, (axis, n, _, direct) in enumerate(jobs):
        if direct:
            for offset in range(1, n):
                direct_copy(job, offset).start()

    copies = [[[] for _ in range(2 * pieces)] for _, _, pieces, _ in jobs]
    for step in range(max(n for _, n, _, _ in jobs) - 1):
        for job, (axis, n, pieces, direct) in enumerate(jobs):
            if direct or step >= n - 1:
                continue
            me, right, left = places[job]
            recv, sendbuf, send_sem, recv_sem = scratch[4 * job:4 * job + 4]
            term_ref = terms[job]
            rows, half = outs[job].shape[0] // pieces, outs[job].shape[1] // 2
            for slot in range(2 * pieces):
                piece, way = divmod(slot, 2)
                dest, sign = ((right, -1), (left, 1))[way]
                block = lax.rem(me + n + sign * (step + 1), n)
                span = (pl.ds(piece * rows, rows), pl.ds(way * half, half))
                if step == 0:
                    src = term_ref.at[block, span[0], span[1]]
                else:
                    copies[job][slot][step - 1].wait_recv()
                    sendbuf[slot, step] = recv[slot, step - 1] + term_ref[block, span[0], span[1]]
                    src = sendbuf.at[slot, step]
                copy = pltpu.make_async_remote_copy(
                    src_ref=src,
                    dst_ref=recv.at[slot, step],
                    send_sem=send_sem.at[slot, step],
                    recv_sem=recv_sem.at[slot, step],
                    device_id={axis: dest},
                    device_id_type=MESH,
                )
                copy.start()
                copies[job][slot].append(copy)
    for job, (axis, n, pieces, direct) in enumerate(jobs):
        me = places[job][0]
        recv = scratch[4 * job]
        if direct:
            outs[job][...] = terms[job][me]
            for sender in range(n):
                @pl.when(sender != me)
                def _():
                    pltpu.make_async_remote_copy(
                        src_ref=terms[job].at[sender],
                        dst_ref=recv.at[sender],
                        send_sem=scratch[4 * job + 2].at[0],
                        recv_sem=scratch[4 * job + 3].at[sender],
                        device_id={axis: sender},
                        device_id_type=MESH,
                    ).wait_recv()
                    outs[job][...] += recv[sender]
            continue
        rows, half = outs[job].shape[0] // pieces, outs[job].shape[1] // 2
        for slot in range(2 * pieces):
            piece, way = divmod(slot, 2)
            span = (pl.ds(piece * rows, rows), pl.ds(way * half, half))
            copies[job][slot][n - 2].wait_recv()
            outs[job][span[0], span[1]] = (
                recv[slot, n - 2] + terms[job][me, span[0], span[1]]
            ).astype(outs[job].dtype)
    for job, (axis, n, pieces, direct) in enumerate(jobs):
        if direct:
            for offset in range(1, n):
                direct_copy(job, offset).wait_send()
        for slot in range(2 * pieces):
            for copy in copies[job][slot]:
                copy.wait_send()


def ring_scatter(parts, channel):
    jobs = tuple((axis, terms.shape[0], pieces, direct) for terms, axis, _, pieces, direct in parts)
    scratch = []
    for terms, _, _, pieces, direct in parts:
        n, rows, width = terms.shape
        if direct:
            scratch += [
                pltpu.VMEM((n, rows, width), jnp.float32),
                pltpu.VMEM((8, 128), jnp.float32),
                pltpu.SemaphoreType.DMA((n,)),
                pltpu.SemaphoreType.DMA((n,)),
            ]
            continue
        scratch += [
            pltpu.VMEM((2 * pieces, n - 1, rows // pieces, width // 2), jnp.float32),
            pltpu.VMEM((2 * pieces, n - 1, rows // pieces, width // 2), jnp.float32),
            pltpu.SemaphoreType.DMA((2 * pieces, n - 1)),
            pltpu.SemaphoreType.DMA((2 * pieces, n - 1)),
        ]
    size = sum(part[0].size for part in parts)
    return pl.pallas_call(
        functools.partial(ring_scatter_kernel, jobs),
        out_shape=tuple(
            jax.ShapeDtypeStruct(part[0].shape[1:], part[2]) for part in parts
        ),
        in_specs=[pl.BlockSpec(memory_space=pltpu.VMEM)] * len(parts),
        out_specs=tuple(pl.BlockSpec(memory_space=pltpu.VMEM) for _ in parts),
        scratch_shapes=scratch,
        compiler_params=pltpu.CompilerParams(
            collective_id=channel, has_side_effects=True, vmem_limit_bytes=48 * 1024 * 1024
        ),
        cost_estimate=pl.CostEstimate(flops=2 * size, bytes_accessed=8 * size, transcendentals=0),
    )(*(part[0] for part in parts))


def exchange_kernel(n, axis, kv_ref, qg_ref, prefix_ref, suffix_ref,
                    pair_in, chip_sum, kv_in, qg_in, pair_sem, send_sem, recv_sem):
    me = lax.axis_index(axis)
    chips = n // 2
    chip, core = me // 2, lax.rem(me, 2)
    partner = me + 1 - 2 * core
    barrier = pltpu.get_barrier_semaphore()
    pl.semaphore_signal(barrier, inc=1, device_id={axis: partner}, device_id_type=MESH)
    for offset in range(1, chips):
        peer = lax.rem(chip + offset, chips) * 2 + core
        pl.semaphore_signal(barrier, inc=1, device_id={axis: peer}, device_id_type=MESH)
    pl.semaphore_wait(barrier, chips)

    swaps = []
    for kind, ref in enumerate((kv_ref, qg_ref)):
        swap = pltpu.make_async_remote_copy(
            src_ref=ref, dst_ref=pair_in.at[kind], send_sem=pair_sem.at[0, kind],
            recv_sem=pair_sem.at[1, kind], device_id={axis: partner}, device_id_type=MESH,
        )
        swap.start()
        swaps.append(swap)
    for swap in swaps:
        swap.wait_recv()
    chip_sum[0] = kv_ref[...] + pair_in[0]
    chip_sum[1] = qg_ref[...] + pair_in[1]

    def route(offset, later):
        peer = lax.rem(chip + offset, chips) * 2 + core
        kind = 0 if later else 1
        return pltpu.make_async_remote_copy(
            src_ref=chip_sum.at[kind],
            dst_ref=(kv_in if later else qg_in).at[chip],
            send_sem=send_sem.at[kind, offset],
            recv_sem=recv_sem.at[kind, chip],
            device_id={axis: peer},
            device_id_type=MESH,
        )

    for offset in range(1, chips):
        for later in (True, False):
            @pl.when((chip + offset < chips) == later)
            def _():
                route(offset, later).start()

    prefix_ref[...] = jnp.where(core == 1, pair_in[0], 0.0)
    suffix_ref[...] = jnp.where(core == 0, pair_in[1], 0.0)
    for sender in range(chips):
        @pl.when(sender < chip)
        def _():
            pltpu.make_async_remote_copy(
                src_ref=chip_sum.at[0], dst_ref=kv_in.at[sender], send_sem=send_sem.at[0, 0],
                recv_sem=recv_sem.at[0, sender], device_id={axis: sender * 2 + core},
                device_id_type=MESH,
            ).wait_recv()
            prefix_ref[...] += kv_in[sender]

        @pl.when(sender > chip)
        def _():
            pltpu.make_async_remote_copy(
                src_ref=chip_sum.at[1], dst_ref=qg_in.at[sender], send_sem=send_sem.at[1, 0],
                recv_sem=recv_sem.at[1, sender], device_id={axis: sender * 2 + core},
                device_id_type=MESH,
            ).wait_recv()
            suffix_ref[...] += qg_in[sender]

    for swap in swaps:
        swap.wait_send()
    for offset in range(1, chips):
        for later in (True, False):
            @pl.when((chip + offset < chips) == later)
            def _():
                route(offset, later).wait_send()


def exchange_states(kv_state, qg_state, axis):
    n = lax.axis_size(axis)
    chips = n // 2
    shape = kv_state.shape
    return pl.pallas_call(
        functools.partial(exchange_kernel, n, axis),
        out_shape=(jax.ShapeDtypeStruct(shape, jnp.float32),) * 2,
        in_specs=[pl.BlockSpec(memory_space=pltpu.VMEM)] * 2,
        out_specs=(pl.BlockSpec(memory_space=pltpu.VMEM),) * 2,
        scratch_shapes=[
            pltpu.VMEM((2,) + shape, jnp.float32),
            pltpu.VMEM((2,) + shape, jnp.float32),
            pltpu.VMEM((chips,) + shape, jnp.float32),
            pltpu.VMEM((chips,) + shape, jnp.float32),
            pltpu.SemaphoreType.DMA((2, 2)),
            pltpu.SemaphoreType.DMA((2, chips)),
            pltpu.SemaphoreType.DMA((2, chips)),
        ],
        compiler_params=pltpu.CompilerParams(collective_id=2, has_side_effects=True),
    )(kv_state, qg_state)


def local(layer_input, w_query, w_key, w_value, w_out, out_grad):
    num_rows = layer_input.shape[1]
    local_heads = w_query.shape[1] // HEAD_DIM
    width = local_heads * HEAD_DIM
    in_rows = layer_input[0]
    grad_rows = out_grad[0]

    def project(weight):
        result = jnp.dot(in_rows, weight, preferred_element_type=jnp.float32).astype(jnp.bfloat16)
        return result.reshape(num_rows, local_heads, HEAD_DIM)

    queries = project(w_query)
    key_rows = project(w_key)
    value_rows = project(w_value)
    row_start = lax.axis_index("seq") * num_rows
    positions = (row_start + jnp.arange(num_rows, dtype=jnp.int32)).astype(jnp.float32)
    pos_scale = 1.0 / jnp.sqrt(HEAD_DIM * (positions + 1.0))
    backward = jnp.einsum("td,kd->tk", grad_rows, w_out, preferred_element_type=jnp.float32)
    grad_in = (
        (backward * pos_scale[:, None])
        .astype(jnp.bfloat16)
        .reshape(num_rows, local_heads, HEAD_DIM)
    )
    kv_state = jnp.einsum("thd,the->hde", key_rows, value_rows, preferred_element_type=jnp.float32)
    qg_state = jnp.einsum("thd,the->hde", queries, grad_in, preferred_element_type=jnp.float32)
    prefix, suffix = exchange_states(kv_state, qg_state, "seq")
    prefix = prefix.astype(jnp.bfloat16)
    suffix = suffix.astype(jnp.bfloat16)
    causal = (jnp.arange(num_rows)[:, None] >= jnp.arange(num_rows)[None, :])[None]
    scores = jnp.einsum("thd,shd->hts", queries, key_rows, preferred_element_type=jnp.float32)
    scores_qk = jnp.where(causal, scores, 0.0).astype(jnp.bfloat16)
    scores_g = jnp.einsum("thd,shd->hts", grad_in, value_rows, preferred_element_type=jnp.float32)
    scores_gv = jnp.where(causal, scores_g, 0.0).astype(jnp.bfloat16)
    inner_sum = jnp.einsum(
        "hts,she->the", scores_qk, value_rows, preferred_element_type=jnp.float32
    )
    cross_sum = jnp.einsum("thd,hde->the", queries, prefix, preferred_element_type=jnp.float32)
    attention = (
        ((inner_sum + cross_sum) * pos_scale[:, None, None])
        .astype(jnp.bfloat16)
        .reshape(num_rows, width)
    )
    d_query = jnp.einsum("hts,shd->thd", scores_gv, key_rows, preferred_element_type=jnp.float32)
    d_query = d_query + jnp.einsum(
        "the,hde->thd", grad_in, prefix, preferred_element_type=jnp.float32
    )
    d_keys = jnp.einsum("hts,thd->shd", scores_gv, queries, preferred_element_type=jnp.float32)
    d_keys = d_keys + jnp.einsum(
        "she,hde->shd", value_rows, suffix, preferred_element_type=jnp.float32
    )
    d_values = jnp.einsum("hts,the->she", scores_qk, grad_in, preferred_element_type=jnp.float32)
    d_values = d_values + jnp.einsum(
        "shd,hde->she", key_rows, suffix, preferred_element_type=jnp.float32
    )
    d_query = d_query.astype(jnp.bfloat16).reshape(num_rows, width)
    d_keys = d_keys.astype(jnp.bfloat16).reshape(num_rows, width)
    d_values = d_values.astype(jnp.bfloat16).reshape(num_rows, width)
    groups = lax.axis_size("head")

    def by_block(weight):
        return weight.reshape(groups, weight.shape[0] // groups, width)

    head_terms = jnp.einsum("tk,bdk->btd", d_query, by_block(w_query), preferred_element_type=jnp.float32)
    head_terms = head_terms + jnp.einsum(
        "tk,bdk->btd", d_keys, by_block(w_key), preferred_element_type=jnp.float32
    )
    head_terms = head_terms + jnp.einsum(
        "tk,bdk->btd", d_values, by_block(w_value), preferred_element_type=jnp.float32
    )
    total_rows = lax.axis_size("seq") * lax.axis_size("dp") * num_rows
    grad_scale = jnp.float32(1.0) / jnp.sqrt(jnp.float32(total_rows))
    seqs, shares = lax.axis_size("seq"), lax.axis_size("dp")
    grads = jnp.concatenate([d_query, d_keys, d_values], axis=1)
    term_qkv = jnp.einsum("td,tk->dk", in_rows, grads, preferred_element_type=jnp.float32) * grad_scale
    grad_blocks = grad_rows.reshape(num_rows, seqs, shares, -1)
    term_out = jnp.einsum(
        "tspr,tk->psrk", grad_blocks, attention, preferred_element_type=jnp.float32
    ) * grad_scale
    term_out = term_out.reshape(shares, -1, width)
    term_qkv, head_terms, term_out = lax.optimization_barrier((term_qkv, head_terms, term_out))
    summed = lax.psum_scatter(term_qkv, "seq", scatter_dimension=0, tiled=True)
    input_grad, out_shared = ring_scatter(
        [(head_terms, "head", jnp.bfloat16, 4, False), (term_out, "dp", jnp.float32, 2, False)], 0
    )
    input_grad = input_grad[None]
    summed, input_grad, out_shared = lax.optimization_barrier((summed, input_grad, out_shared))
    summed, out_summed = ring_scatter(
        [
            (summed.reshape(shares, -1, summed.shape[1]), "dp", jnp.float32, 2, False),
            (out_shared.reshape(seqs, -1, width), "seq", jnp.float32, 1, True),
        ],
        1,
    )
    grad_query = summed[:, :width]
    grad_key = summed[:, width:2 * width]
    grad_value = summed[:, 2 * width:]
    grad_out = out_summed.T
    return (input_grad, grad_query, grad_key, grad_value, grad_out)


def solution(mesh):
    return jax.shard_map(
        local,
        mesh=mesh,
        in_specs=(
            P("dp", "seq", None),
            P(None, "head"),
            P(None, "head"),
            P(None, "head"),
            P("head", None),
            P("dp", "seq", None),
        ),
        out_specs=(
            P("dp", "seq", "head"),
            P(("seq", "dp"), "head"),
            P(("seq", "dp"), "head"),
            P(("seq", "dp"), "head"),
            P("head", ("seq", "dp")),
        ),
        check_vma=False,
    )
```

```python
import functools
import math

import jax
import jax.numpy as jnp
from jax import lax
from jax.experimental import pallas as pl
from jax.experimental.pallas import tpu as pltpu
from jax.sharding import PartitionSpec as P

HEAD_DIM = 128
MESH = pl.DeviceIdType.MESH


def ring_scatter_kernel(jobs, produce, *refs):
    count = len(jobs)
    if produce:
        factors, refs = refs[:2 * produce], refs[2 * produce:]
        made, refs = refs[-1], refs[:-1]
        terms = (made,) + refs[:count - 1]
        outs, scratch = refs[count - 1:2 * count - 1], refs[2 * count - 1:]
        grads, weights = factors[:produce], factors[produce:]
        block_rows = made.shape[2]
        for block in range(made.shape[0]):
            rows = pl.ds(block * block_rows, block_rows)
            total = None
            for grad, weight in zip(grads, weights):
                part = lax.dot_general(
                    grad[...], weight[rows, :], (((1,), (1,)), ((), ())),
                    preferred_element_type=jnp.float32,
                )
                total = part if total is None else total + part
            made[block] = total
    else:
        terms, outs, scratch = refs[:count], refs[count:2 * count], refs[2 * count:]
    barrier = pltpu.get_barrier_semaphore()
    places, greeted = [], 0
    for axis, n, _, direct in jobs:
        me = lax.axis_index(axis)
        right, left = lax.rem(me + 1, n), lax.rem(me + n - 1, n)
        places.append((me, right, left))
        offsets = range(1, n) if direct else (n - 1, 1)
        for offset in offsets:
            pl.semaphore_signal(
                barrier, inc=1, device_id={axis: lax.rem(me + offset, n)}, device_id_type=MESH
            )
        greeted += len(offsets)
    pl.semaphore_wait(barrier, greeted)

    def direct_copy(job, offset):
        axis, n, _, _ = jobs[job]
        me = places[job][0]
        recv, send_sem, recv_sem = scratch[4 * job], scratch[4 * job + 2], scratch[4 * job + 3]
        peer = lax.rem(me + offset, n)
        return pltpu.make_async_remote_copy(
            src_ref=terms[job].at[peer],
            dst_ref=recv.at[me],
            send_sem=send_sem.at[offset],
            recv_sem=recv_sem.at[me],
            device_id={axis: peer},
            device_id_type=MESH,
        )

    for job, (axis, n, _, direct) in enumerate(jobs):
        if direct:
            for offset in range(1, n):
                direct_copy(job, offset).start()

    copies = [[[] for _ in range(2 * pieces)] for _, _, pieces, _ in jobs]
    for step in range(max(n for _, n, _, _ in jobs) - 1):
        for job, (axis, n, pieces, direct) in enumerate(jobs):
            if direct or step >= n - 1:
                continue
            me, right, left = places[job]
            recv, sendbuf, send_sem, recv_sem = scratch[4 * job:4 * job + 4]
            term_ref = terms[job]
            rows, half = outs[job].shape[0] // pieces, outs[job].shape[1] // 2
            for slot in range(2 * pieces):
                piece, way = divmod(slot, 2)
                dest, sign = ((right, -1), (left, 1))[way]
                block = lax.rem(me + n + sign * (step + 1), n)
                span = (pl.ds(piece * rows, rows), pl.ds(way * half, half))
                if step == 0:
                    src = term_ref.at[block, span[0], span[1]]
                else:
                    copies[job][slot][step - 1].wait_recv()
                    sendbuf[slot, step] = recv[slot, step - 1] + term_ref[block, span[0], span[1]]
                    src = sendbuf.at[slot, step]
                copy = pltpu.make_async_remote_copy(
                    src_ref=src,
                    dst_ref=recv.at[slot, step],
                    send_sem=send_sem.at[slot, step],
                    recv_sem=recv_sem.at[slot, step],
                    device_id={axis: dest},
                    device_id_type=MESH,
                )
                copy.start()
                copies[job][slot].append(copy)
    for job, (axis, n, pieces, direct) in enumerate(jobs):
        me = places[job][0]
        recv = scratch[4 * job]
        if direct:
            outs[job][...] = terms[job][me]
            for sender in range(n):
                @pl.when(sender != me)
                def _():
                    pltpu.make_async_remote_copy(
                        src_ref=terms[job].at[sender],
                        dst_ref=recv.at[sender],
                        send_sem=scratch[4 * job + 2].at[0],
                        recv_sem=scratch[4 * job + 3].at[sender],
                        device_id={axis: sender},
                        device_id_type=MESH,
                    ).wait_recv()
                    outs[job][...] += recv[sender]
            continue
        rows, half = outs[job].shape[0] // pieces, outs[job].shape[1] // 2
        for slot in range(2 * pieces):
            piece, way = divmod(slot, 2)
            span = (pl.ds(piece * rows, rows), pl.ds(way * half, half))
            copies[job][slot][n - 2].wait_recv()
            outs[job][span[0], span[1]] = (
                recv[slot, n - 2] + terms[job][me, span[0], span[1]]
            ).astype(outs[job].dtype)
    for job, (axis, n, pieces, direct) in enumerate(jobs):
        if direct:
            for offset in range(1, n):
                direct_copy(job, offset).wait_send()
        for slot in range(2 * pieces):
            for copy in copies[job][slot]:
                copy.wait_send()


def ring_scatter(parts, channel, factors=None):
    jobs = tuple((axis, terms.shape[0], pieces, direct) for terms, axis, _, pieces, direct in parts)
    produce = len(factors[0]) if factors else 0
    scratch = []
    for terms, _, _, pieces, direct in parts:
        n, rows, width = terms.shape
        if direct:
            scratch += [
                pltpu.VMEM((n, rows, width), jnp.float32),
                pltpu.VMEM((8, 128), jnp.float32),
                pltpu.SemaphoreType.DMA((n,)),
                pltpu.SemaphoreType.DMA((n,)),
            ]
            continue
        scratch += [
            pltpu.VMEM((2 * pieces, n - 1, rows // pieces, width // 2), jnp.float32),
            pltpu.VMEM((2 * pieces, n - 1, rows // pieces, width // 2), jnp.float32),
            pltpu.SemaphoreType.DMA((2 * pieces, n - 1)),
            pltpu.SemaphoreType.DMA((2 * pieces, n - 1)),
        ]
    size = sum(math.prod(part[0].shape) for part in parts)
    operands = [part[0] for part in parts]
    if produce:
        scratch.append(pltpu.VMEM(parts[0][0].shape, jnp.float32))
        operands = list(factors[0]) + list(factors[1]) + operands[1:]
    return pl.pallas_call(
        functools.partial(ring_scatter_kernel, jobs, produce),
        out_shape=tuple(
            jax.ShapeDtypeStruct(part[0].shape[1:], part[2]) for part in parts
        ),
        in_specs=[pl.BlockSpec(memory_space=pltpu.VMEM)] * len(operands),
        out_specs=tuple(pl.BlockSpec(memory_space=pltpu.VMEM) for _ in parts),
        scratch_shapes=scratch,
        compiler_params=pltpu.CompilerParams(
            collective_id=channel, has_side_effects=True, vmem_limit_bytes=48 * 1024 * 1024
        ),
        cost_estimate=pl.CostEstimate(flops=2 * size, bytes_accessed=8 * size, transcendentals=0),
    )(*operands)


def exchange_kernel(n, axis, kv_ref, qg_ref, prefix_ref, suffix_ref,
                    pair_in, chip_sum, kv_in, qg_in, pair_sem, send_sem, recv_sem):
    me = lax.axis_index(axis)
    chips = n // 2
    chip, core = me // 2, lax.rem(me, 2)
    partner = me + 1 - 2 * core
    barrier = pltpu.get_barrier_semaphore()
    pl.semaphore_signal(barrier, inc=1, device_id={axis: partner}, device_id_type=MESH)
    for offset in range(1, chips):
        peer = lax.rem(chip + offset, chips) * 2 + core
        pl.semaphore_signal(barrier, inc=1, device_id={axis: peer}, device_id_type=MESH)
    pl.semaphore_wait(barrier, chips)

    swaps = []
    for kind, ref in enumerate((kv_ref, qg_ref)):
        swap = pltpu.make_async_remote_copy(
            src_ref=ref, dst_ref=pair_in.at[kind], send_sem=pair_sem.at[0, kind],
            recv_sem=pair_sem.at[1, kind], device_id={axis: partner}, device_id_type=MESH,
        )
        swap.start()
        swaps.append(swap)
    for swap in swaps:
        swap.wait_recv()
    chip_sum[0] = kv_ref[...] + pair_in[0]
    chip_sum[1] = qg_ref[...] + pair_in[1]

    def route(offset, later):
        peer = lax.rem(chip + offset, chips) * 2 + core
        kind = 0 if later else 1
        return pltpu.make_async_remote_copy(
            src_ref=chip_sum.at[kind],
            dst_ref=(kv_in if later else qg_in).at[chip],
            send_sem=send_sem.at[kind, offset],
            recv_sem=recv_sem.at[kind, chip],
            device_id={axis: peer},
            device_id_type=MESH,
        )

    for offset in range(1, chips):
        for later in (True, False):
            @pl.when((chip + offset < chips) == later)
            def _():
                route(offset, later).start()

    prefix_ref[...] = jnp.where(core == 1, pair_in[0], 0.0)
    suffix_ref[...] = jnp.where(core == 0, pair_in[1], 0.0)
    for sender in range(chips):
        @pl.when(sender < chip)
        def _():
            pltpu.make_async_remote_copy(
                src_ref=chip_sum.at[0], dst_ref=kv_in.at[sender], send_sem=send_sem.at[0, 0],
                recv_sem=recv_sem.at[0, sender], device_id={axis: sender * 2 + core},
                device_id_type=MESH,
            ).wait_recv()
            prefix_ref[...] += kv_in[sender]

        @pl.when(sender > chip)
        def _():
            pltpu.make_async_remote_copy(
                src_ref=chip_sum.at[1], dst_ref=qg_in.at[sender], send_sem=send_sem.at[1, 0],
                recv_sem=recv_sem.at[1, sender], device_id={axis: sender * 2 + core},
                device_id_type=MESH,
            ).wait_recv()
            suffix_ref[...] += qg_in[sender]

    for swap in swaps:
        swap.wait_send()
    for offset in range(1, chips):
        for later in (True, False):
            @pl.when((chip + offset < chips) == later)
            def _():
                route(offset, later).wait_send()


def exchange_states(kv_state, qg_state, axis):
    n = lax.axis_size(axis)
    chips = n // 2
    shape = kv_state.shape
    return pl.pallas_call(
        functools.partial(exchange_kernel, n, axis),
        out_shape=(jax.ShapeDtypeStruct(shape, jnp.float32),) * 2,
        in_specs=[pl.BlockSpec(memory_space=pltpu.VMEM)] * 2,
        out_specs=(pl.BlockSpec(memory_space=pltpu.VMEM),) * 2,
        scratch_shapes=[
            pltpu.VMEM((2,) + shape, jnp.float32),
            pltpu.VMEM((2,) + shape, jnp.float32),
            pltpu.VMEM((chips,) + shape, jnp.float32),
            pltpu.VMEM((chips,) + shape, jnp.float32),
            pltpu.SemaphoreType.DMA((2, 2)),
            pltpu.SemaphoreType.DMA((2, chips)),
            pltpu.SemaphoreType.DMA((2, chips)),
        ],
        compiler_params=pltpu.CompilerParams(collective_id=2, has_side_effects=True),
    )(kv_state, qg_state)


def local(layer_input, w_query, w_key, w_value, w_out, out_grad):
    num_rows = layer_input.shape[1]
    local_heads = w_query.shape[1] // HEAD_DIM
    width = local_heads * HEAD_DIM
    in_rows = layer_input[0]
    grad_rows = out_grad[0]

    def project(weight):
        result = jnp.dot(in_rows, weight, preferred_element_type=jnp.float32).astype(jnp.bfloat16)
        return result.reshape(num_rows, local_heads, HEAD_DIM)

    queries = project(w_query)
    key_rows = project(w_key)
    value_rows = project(w_value)
    row_start = lax.axis_index("seq") * num_rows
    positions = (row_start + jnp.arange(num_rows, dtype=jnp.int32)).astype(jnp.float32)
    pos_scale = 1.0 / jnp.sqrt(HEAD_DIM * (positions + 1.0))
    backward = jnp.einsum("td,kd->tk", grad_rows, w_out, preferred_element_type=jnp.float32)
    grad_in = (
        (backward * pos_scale[:, None])
        .astype(jnp.bfloat16)
        .reshape(num_rows, local_heads, HEAD_DIM)
    )
    kv_state = jnp.einsum("thd,the->hde", key_rows, value_rows, preferred_element_type=jnp.float32)
    qg_state = jnp.einsum("thd,the->hde", queries, grad_in, preferred_element_type=jnp.float32)
    prefix, suffix = exchange_states(kv_state, qg_state, "seq")
    prefix = prefix.astype(jnp.bfloat16)
    suffix = suffix.astype(jnp.bfloat16)
    causal = (jnp.arange(num_rows)[:, None] >= jnp.arange(num_rows)[None, :])[None]
    scores = jnp.einsum("thd,shd->hts", queries, key_rows, preferred_element_type=jnp.float32)
    scores_qk = jnp.where(causal, scores, 0.0).astype(jnp.bfloat16)
    scores_g = jnp.einsum("thd,shd->hts", grad_in, value_rows, preferred_element_type=jnp.float32)
    scores_gv = jnp.where(causal, scores_g, 0.0).astype(jnp.bfloat16)
    inner_sum = jnp.einsum(
        "hts,she->the", scores_qk, value_rows, preferred_element_type=jnp.float32
    )
    cross_sum = jnp.einsum("thd,hde->the", queries, prefix, preferred_element_type=jnp.float32)
    attention = (
        ((inner_sum + cross_sum) * pos_scale[:, None, None])
        .astype(jnp.bfloat16)
        .reshape(num_rows, width)
    )
    d_query = jnp.einsum("hts,shd->thd", scores_gv, key_rows, preferred_element_type=jnp.float32)
    d_query = d_query + jnp.einsum(
        "the,hde->thd", grad_in, prefix, preferred_element_type=jnp.float32
    )
    d_keys = jnp.einsum("hts,thd->shd", scores_gv, queries, preferred_element_type=jnp.float32)
    d_keys = d_keys + jnp.einsum(
        "she,hde->shd", value_rows, suffix, preferred_element_type=jnp.float32
    )
    d_values = jnp.einsum("hts,the->she", scores_qk, grad_in, preferred_element_type=jnp.float32)
    d_values = d_values + jnp.einsum(
        "shd,hde->she", key_rows, suffix, preferred_element_type=jnp.float32
    )
    d_query = d_query.astype(jnp.bfloat16).reshape(num_rows, width)
    d_keys = d_keys.astype(jnp.bfloat16).reshape(num_rows, width)
    d_values = d_values.astype(jnp.bfloat16).reshape(num_rows, width)
    groups = lax.axis_size("head")
    head_terms = jax.ShapeDtypeStruct((groups, num_rows, w_query.shape[0] // groups), jnp.float32)
    total_rows = lax.axis_size("seq") * lax.axis_size("dp") * num_rows
    grad_scale = jnp.float32(1.0) / jnp.sqrt(jnp.float32(total_rows))
    seqs, shares = lax.axis_size("seq"), lax.axis_size("dp")
    grads = jnp.concatenate([d_query, d_keys, d_values], axis=1)
    term_qkv = jnp.einsum("td,tk->dk", in_rows, grads, preferred_element_type=jnp.float32) * grad_scale
    grad_blocks = grad_rows.reshape(num_rows, seqs, shares, -1)
    term_out = jnp.einsum(
        "tspr,tk->psrk", grad_blocks, attention, preferred_element_type=jnp.float32
    ) * grad_scale
    term_out = term_out.reshape(shares, -1, width)
    factors = ((d_query, d_keys, d_values), (w_query, w_key, w_value))
    term_qkv, factors, term_out = lax.optimization_barrier((term_qkv, factors, term_out))
    summed = lax.psum_scatter(term_qkv, "seq", scatter_dimension=0, tiled=True)
    input_grad, out_shared = ring_scatter(
        [(head_terms, "head", jnp.bfloat16, 4, False), (term_out, "dp", jnp.float32, 2, False)], 0,
        factors,
    )
    input_grad = input_grad[None]
    summed, input_grad, out_shared = lax.optimization_barrier((summed, input_grad, out_shared))
    summed, out_summed = ring_scatter(
        [
            (summed.reshape(shares, -1, summed.shape[1]), "dp", jnp.float32, 2, False),
            (out_shared.reshape(seqs, -1, width), "seq", jnp.float32, 1, True),
        ],
        1,
    )
    grad_query = summed[:, :width]
    grad_key = summed[:, width:2 * width]
    grad_value = summed[:, 2 * width:]
    grad_out = out_summed.T
    return (input_grad, grad_query, grad_key, grad_value, grad_out)


def solution(mesh):
    return jax.shard_map(
        local,
        mesh=mesh,
        in_specs=(
            P("dp", "seq", None),
            P(None, "head"),
            P(None, "head"),
            P(None, "head"),
            P("head", None),
            P("dp", "seq", None),
        ),
        out_specs=(
            P("dp", "seq", "head"),
            P(("seq", "dp"), "head"),
            P(("seq", "dp"), "head"),
            P(("seq", "dp"), "head"),
            P("head", ("seq", "dp")),
        ),
        check_vma=False,
    )
```

```python
import functools
import math

import jax
import jax.numpy as jnp
from jax import lax
from jax.experimental import pallas as pl
from jax.experimental.pallas import tpu as pltpu
from jax.sharding import PartitionSpec as P

HEAD_DIM = 128
MESH = pl.DeviceIdType.MESH


def ring_scatter_kernel(jobs, produce, *refs):
    count = len(jobs)
    if produce:
        factors, refs = refs[:2 * produce], refs[2 * produce:]
        made, refs = refs[-1], refs[:-1]
        terms = (made,) + refs[:count - 1]
        outs, scratch = refs[count - 1:2 * count - 1], refs[2 * count - 1:]
        grads, weights = factors[:produce], factors[produce:]
        block_rows = made.shape[2]
        for block in range(made.shape[0]):
            rows = pl.ds(block * block_rows, block_rows)
            total = None
            for grad, weight in zip(grads, weights):
                part = lax.dot_general(
                    grad[...], weight[rows, :], (((1,), (1,)), ((), ())),
                    preferred_element_type=jnp.float32,
                )
                total = part if total is None else total + part
            made[block] = total
    else:
        terms, outs, scratch = refs[:count], refs[count:2 * count], refs[2 * count:]
    barrier = pltpu.get_barrier_semaphore()
    places, greeted = [], 0
    for axis, n, _, direct in jobs:
        me = lax.axis_index(axis)
        right, left = lax.rem(me + 1, n), lax.rem(me + n - 1, n)
        places.append((me, right, left))
        offsets = range(1, n) if direct else (n - 1, 1)
        for offset in offsets:
            pl.semaphore_signal(
                barrier, inc=1, device_id={axis: lax.rem(me + offset, n)}, device_id_type=MESH
            )
        greeted += len(offsets)
    pl.semaphore_wait(barrier, greeted)

    def direct_copy(job, offset):
        axis, n, _, _ = jobs[job]
        me = places[job][0]
        recv, send_sem, recv_sem = scratch[4 * job], scratch[4 * job + 2], scratch[4 * job + 3]
        peer = lax.rem(me + offset, n)
        return pltpu.make_async_remote_copy(
            src_ref=terms[job].at[peer],
            dst_ref=recv.at[me],
            send_sem=send_sem.at[offset],
            recv_sem=recv_sem.at[me],
            device_id={axis: peer},
            device_id_type=MESH,
        )

    for job, (axis, n, _, direct) in enumerate(jobs):
        if direct:
            for offset in range(1, n):
                direct_copy(job, offset).start()

    copies = [[[] for _ in range(2 * pieces)] for _, _, pieces, _ in jobs]
    for step in range(max(n for _, n, _, _ in jobs) - 1):
        for job, (axis, n, pieces, direct) in enumerate(jobs):
            if direct or step >= n - 1:
                continue
            me, right, left = places[job]
            recv, sendbuf, send_sem, recv_sem = scratch[4 * job:4 * job + 4]
            term_ref = terms[job]
            rows, half = outs[job].shape[0] // pieces, outs[job].shape[1] // 2
            for slot in range(2 * pieces):
                piece, way = divmod(slot, 2)
                dest, sign = ((right, -1), (left, 1))[way]
                block = lax.rem(me + n + sign * (step + 1), n)
                span = (pl.ds(piece * rows, rows), pl.ds(way * half, half))
                if step == 0:
                    src = term_ref.at[block, span[0], span[1]]
                else:
                    copies[job][slot][step - 1].wait_recv()
                    sendbuf[slot, step] = recv[slot, step - 1] + term_ref[block, span[0], span[1]]
                    src = sendbuf.at[slot, step]
                copy = pltpu.make_async_remote_copy(
                    src_ref=src,
                    dst_ref=recv.at[slot, step],
                    send_sem=send_sem.at[slot, step],
                    recv_sem=recv_sem.at[slot, step],
                    device_id={axis: dest},
                    device_id_type=MESH,
                )
                copy.start()
                copies[job][slot].append(copy)
    for job, (axis, n, pieces, direct) in enumerate(jobs):
        me = places[job][0]
        recv = scratch[4 * job]
        if direct:
            outs[job][...] = terms[job][me]
            for sender in range(n):
                @pl.when(sender != me)
                def _():
                    pltpu.make_async_remote_copy(
                        src_ref=terms[job].at[sender],
                        dst_ref=recv.at[sender],
                        send_sem=scratch[4 * job + 2].at[0],
                        recv_sem=scratch[4 * job + 3].at[sender],
                        device_id={axis: sender},
                        device_id_type=MESH,
                    ).wait_recv()
                    outs[job][...] += recv[sender]
            continue
        rows, half = outs[job].shape[0] // pieces, outs[job].shape[1] // 2
        for slot in range(2 * pieces):
            piece, way = divmod(slot, 2)
            span = (pl.ds(piece * rows, rows), pl.ds(way * half, half))
            copies[job][slot][n - 2].wait_recv()
            outs[job][span[0], span[1]] = (
                recv[slot, n - 2] + terms[job][me, span[0], span[1]]
            ).astype(outs[job].dtype)
    for job, (axis, n, pieces, direct) in enumerate(jobs):
        if direct:
            for offset in range(1, n):
                direct_copy(job, offset).wait_send()
        for slot in range(2 * pieces):
            for copy in copies[job][slot]:
                copy.wait_send()


def ring_scatter(parts, channel, factors=None):
    jobs = tuple((axis, terms.shape[0], pieces, direct) for terms, axis, _, pieces, direct in parts)
    produce = len(factors[0]) if factors else 0
    scratch = []
    for terms, _, _, pieces, direct in parts:
        n, rows, width = terms.shape
        if direct:
            scratch += [
                pltpu.VMEM((n, rows, width), jnp.float32),
                pltpu.VMEM((8, 128), jnp.float32),
                pltpu.SemaphoreType.DMA((n,)),
                pltpu.SemaphoreType.DMA((n,)),
            ]
            continue
        scratch += [
            pltpu.VMEM((2 * pieces, n - 1, rows // pieces, width // 2), jnp.float32),
            pltpu.VMEM((2 * pieces, n - 1, rows // pieces, width // 2), jnp.float32),
            pltpu.SemaphoreType.DMA((2 * pieces, n - 1)),
            pltpu.SemaphoreType.DMA((2 * pieces, n - 1)),
        ]
    size = sum(math.prod(part[0].shape) for part in parts)
    operands = [part[0] for part in parts]
    if produce:
        scratch.append(pltpu.VMEM(parts[0][0].shape, jnp.float32))
        operands = list(factors[0]) + list(factors[1]) + operands[1:]
    return pl.pallas_call(
        functools.partial(ring_scatter_kernel, jobs, produce),
        out_shape=tuple(
            jax.ShapeDtypeStruct(part[0].shape[1:], part[2]) for part in parts
        ),
        in_specs=[pl.BlockSpec(memory_space=pltpu.VMEM)] * len(operands),
        out_specs=tuple(pl.BlockSpec(memory_space=pltpu.VMEM) for _ in parts),
        scratch_shapes=scratch,
        compiler_params=pltpu.CompilerParams(
            collective_id=channel, has_side_effects=True, vmem_limit_bytes=48 * 1024 * 1024
        ),
        cost_estimate=pl.CostEstimate(flops=2 * size, bytes_accessed=8 * size, transcendentals=0),
    )(*operands)


def exchange_kernel(n, axis, kv_ref, qg_ref, prefix_ref, suffix_ref,
                    pair_in, chip_sum, kv_in, qg_in, pair_sem, send_sem, recv_sem):
    me = lax.axis_index(axis)
    chips = n // 2
    chip, core = me // 2, lax.rem(me, 2)
    partner = me + 1 - 2 * core
    barrier = pltpu.get_barrier_semaphore()
    pl.semaphore_signal(barrier, inc=1, device_id={axis: partner}, device_id_type=MESH)
    for offset in range(1, chips):
        peer = lax.rem(chip + offset, chips) * 2 + core
        pl.semaphore_signal(barrier, inc=1, device_id={axis: peer}, device_id_type=MESH)
    pl.semaphore_wait(barrier, chips)

    swaps = []
    for kind, ref in enumerate((kv_ref, qg_ref)):
        swap = pltpu.make_async_remote_copy(
            src_ref=ref, dst_ref=pair_in.at[kind], send_sem=pair_sem.at[0, kind],
            recv_sem=pair_sem.at[1, kind], device_id={axis: partner}, device_id_type=MESH,
        )
        swap.start()
        swaps.append(swap)
    for swap in swaps:
        swap.wait_recv()
    chip_sum[0] = kv_ref[...] + pair_in[0]
    chip_sum[1] = qg_ref[...] + pair_in[1]

    def route(offset, later):
        peer = lax.rem(chip + offset, chips) * 2 + core
        kind = 0 if later else 1
        return pltpu.make_async_remote_copy(
            src_ref=chip_sum.at[kind],
            dst_ref=(kv_in if later else qg_in).at[chip],
            send_sem=send_sem.at[kind, offset],
            recv_sem=recv_sem.at[kind, chip],
            device_id={axis: peer},
            device_id_type=MESH,
        )

    for offset in range(1, chips):
        for later in (True, False):
            @pl.when((chip + offset < chips) == later)
            def _():
                route(offset, later).start()

    prefix_ref[...] = jnp.where(core == 1, pair_in[0], 0.0)
    suffix_ref[...] = jnp.where(core == 0, pair_in[1], 0.0)
    for sender in range(chips):
        @pl.when(sender < chip)
        def _():
            pltpu.make_async_remote_copy(
                src_ref=chip_sum.at[0], dst_ref=kv_in.at[sender], send_sem=send_sem.at[0, 0],
                recv_sem=recv_sem.at[0, sender], device_id={axis: sender * 2 + core},
                device_id_type=MESH,
            ).wait_recv()
            prefix_ref[...] += kv_in[sender]

        @pl.when(sender > chip)
        def _():
            pltpu.make_async_remote_copy(
                src_ref=chip_sum.at[1], dst_ref=qg_in.at[sender], send_sem=send_sem.at[1, 0],
                recv_sem=recv_sem.at[1, sender], device_id={axis: sender * 2 + core},
                device_id_type=MESH,
            ).wait_recv()
            suffix_ref[...] += qg_in[sender]

    for swap in swaps:
        swap.wait_send()
    for offset in range(1, chips):
        for later in (True, False):
            @pl.when((chip + offset < chips) == later)
            def _():
                route(offset, later).wait_send()


def exchange_states(kv_state, qg_state, axis):
    n = lax.axis_size(axis)
    chips = n // 2
    shape = kv_state.shape
    return pl.pallas_call(
        functools.partial(exchange_kernel, n, axis),
        out_shape=(jax.ShapeDtypeStruct(shape, jnp.float32),) * 2,
        in_specs=[pl.BlockSpec(memory_space=pltpu.VMEM)] * 2,
        out_specs=(pl.BlockSpec(memory_space=pltpu.VMEM),) * 2,
        scratch_shapes=[
            pltpu.VMEM((2,) + shape, jnp.float32),
            pltpu.VMEM((2,) + shape, jnp.float32),
            pltpu.VMEM((chips,) + shape, jnp.float32),
            pltpu.VMEM((chips,) + shape, jnp.float32),
            pltpu.SemaphoreType.DMA((2, 2)),
            pltpu.SemaphoreType.DMA((2, chips)),
            pltpu.SemaphoreType.DMA((2, chips)),
        ],
        compiler_params=pltpu.CompilerParams(collective_id=2, has_side_effects=True),
    )(kv_state, qg_state)


def local(layer_input, w_query, w_key, w_value, w_out, out_grad):
    num_rows = layer_input.shape[1]
    local_heads = w_query.shape[1] // HEAD_DIM
    width = local_heads * HEAD_DIM
    in_rows = layer_input[0]
    grad_rows = out_grad[0]

    def project(weight):
        result = jnp.dot(in_rows, weight, preferred_element_type=jnp.float32).astype(jnp.bfloat16)
        return result.reshape(num_rows, local_heads, HEAD_DIM)

    queries = project(w_query)
    key_rows = project(w_key)
    value_rows = project(w_value)
    row_start = lax.axis_index("seq") * num_rows
    positions = (row_start + jnp.arange(num_rows, dtype=jnp.int32)).astype(jnp.float32)
    pos_scale = 1.0 / jnp.sqrt(HEAD_DIM * (positions + 1.0))
    backward = jnp.einsum("td,kd->tk", grad_rows, w_out, preferred_element_type=jnp.float32)
    grad_in = (
        (backward * pos_scale[:, None])
        .astype(jnp.bfloat16)
        .reshape(num_rows, local_heads, HEAD_DIM)
    )
    kv_state = jnp.einsum("thd,the->hde", key_rows, value_rows, preferred_element_type=jnp.float32)
    qg_state = jnp.einsum("thd,the->hde", queries, grad_in, preferred_element_type=jnp.float32)
    prefix, suffix = exchange_states(kv_state, qg_state, "seq")
    prefix = prefix.astype(jnp.bfloat16)
    suffix = suffix.astype(jnp.bfloat16)
    causal = (jnp.arange(num_rows)[:, None] >= jnp.arange(num_rows)[None, :])[None]
    scores = jnp.einsum("thd,shd->hts", queries, key_rows, preferred_element_type=jnp.float32)
    scores_qk = jnp.where(causal, scores, 0.0).astype(jnp.bfloat16)
    scores_g = jnp.einsum("thd,shd->hts", grad_in, value_rows, preferred_element_type=jnp.float32)
    scores_gv = jnp.where(causal, scores_g, 0.0).astype(jnp.bfloat16)
    inner_sum = jnp.einsum(
        "hts,she->the", scores_qk, value_rows, preferred_element_type=jnp.float32
    )
    cross_sum = jnp.einsum("thd,hde->the", queries, prefix, preferred_element_type=jnp.float32)
    attention = (
        ((inner_sum + cross_sum) * pos_scale[:, None, None])
        .astype(jnp.bfloat16)
        .reshape(num_rows, width)
    )
    d_query = jnp.einsum("hts,shd->thd", scores_gv, key_rows, preferred_element_type=jnp.float32)
    d_query = d_query + jnp.einsum(
        "the,hde->thd", grad_in, prefix, preferred_element_type=jnp.float32
    )
    d_keys = jnp.einsum("hts,thd->shd", scores_gv, queries, preferred_element_type=jnp.float32)
    d_keys = d_keys + jnp.einsum(
        "she,hde->shd", value_rows, suffix, preferred_element_type=jnp.float32
    )
    d_values = jnp.einsum("hts,the->she", scores_qk, grad_in, preferred_element_type=jnp.float32)
    d_values = d_values + jnp.einsum(
        "shd,hde->she", key_rows, suffix, preferred_element_type=jnp.float32
    )
    d_query = d_query.astype(jnp.bfloat16).reshape(num_rows, width)
    d_keys = d_keys.astype(jnp.bfloat16).reshape(num_rows, width)
    d_values = d_values.astype(jnp.bfloat16).reshape(num_rows, width)
    groups = lax.axis_size("head")
    head_terms = jax.ShapeDtypeStruct((groups, num_rows, w_query.shape[0] // groups), jnp.float32)
    total_rows = lax.axis_size("seq") * lax.axis_size("dp") * num_rows
    grad_scale = jnp.float32(1.0) / jnp.sqrt(jnp.float32(total_rows))
    seqs, shares = lax.axis_size("seq"), lax.axis_size("dp")
    grads = jnp.concatenate([d_query, d_keys, d_values], axis=1)
    term_qkv = jnp.einsum("td,tk->dk", in_rows, grads, preferred_element_type=jnp.float32) * grad_scale
    grad_blocks = grad_rows.reshape(num_rows, seqs, shares, -1)
    term_out = jnp.einsum(
        "tspr,tk->psrk", grad_blocks, attention, preferred_element_type=jnp.float32
    ) * grad_scale
    term_out = term_out.reshape(shares, -1, width)
    factors = ((d_query, d_keys, d_values), (w_query, w_key, w_value))
    term_qkv, factors, term_out = lax.optimization_barrier((term_qkv, factors, term_out))
    summed = lax.psum_scatter(term_qkv, "seq", scatter_dimension=0, tiled=True)
    input_grad, out_shared = ring_scatter(
        [(head_terms, "head", jnp.bfloat16, 4, False), (term_out, "dp", jnp.float32, 1, True)], 0,
        factors,
    )
    input_grad = input_grad[None]
    summed, input_grad, out_shared = lax.optimization_barrier((summed, input_grad, out_shared))
    summed, out_summed = ring_scatter(
        [
            (summed.reshape(shares, -1, summed.shape[1]), "dp", jnp.float32, 2, False),
            (out_shared.reshape(seqs, -1, width), "seq", jnp.float32, 1, True),
        ],
        1,
    )
    grad_query = summed[:, :width]
    grad_key = summed[:, width:2 * width]
    grad_value = summed[:, 2 * width:]
    grad_out = out_summed.T
    return (input_grad, grad_query, grad_key, grad_value, grad_out)


def solution(mesh):
    return jax.shard_map(
        local,
        mesh=mesh,
        in_specs=(
            P("dp", "seq", None),
            P(None, "head"),
            P(None, "head"),
            P(None, "head"),
            P("head", None),
            P("dp", "seq", None),
        ),
        out_specs=(
            P("dp", "seq", "head"),
            P(("seq", "dp"), "head"),
            P(("seq", "dp"), "head"),
            P(("seq", "dp"), "head"),
            P("head", ("seq", "dp")),
        ),
        check_vma=False,
    )
```

```python
import functools
import math

import jax
import jax.numpy as jnp
from jax import lax
from jax.experimental import pallas as pl
from jax.experimental.pallas import tpu as pltpu
from jax.sharding import PartitionSpec as P

HEAD_DIM = 128
MESH = pl.DeviceIdType.MESH


def ring_scatter_kernel(jobs, produce, *refs):
    count = len(jobs)
    if produce:
        factors, refs = refs[:2 * produce], refs[2 * produce:]
        made, refs = refs[-1], refs[:-1]
        terms = (made,) + refs[:count - 1]
        outs, scratch = refs[count - 1:2 * count - 1], refs[2 * count - 1:]
        grads, weights = factors[:produce], factors[produce:]
        block_rows = made.shape[2]
        for block in range(made.shape[0]):
            rows = pl.ds(block * block_rows, block_rows)
            total = None
            for grad, weight in zip(grads, weights):
                part = lax.dot_general(
                    grad[...], weight[rows, :], (((1,), (1,)), ((), ())),
                    preferred_element_type=jnp.float32,
                )
                total = part if total is None else total + part
            made[block] = total
    else:
        terms, outs, scratch = refs[:count], refs[count:2 * count], refs[2 * count:]
    barrier = pltpu.get_barrier_semaphore()
    places, greeted = [], 0
    for axis, n, _, direct in jobs:
        me = lax.axis_index(axis)
        right, left = lax.rem(me + 1, n), lax.rem(me + n - 1, n)
        places.append((me, right, left))
        offsets = range(1, n) if direct else (n - 1, 1)
        for offset in offsets:
            pl.semaphore_signal(
                barrier, inc=1, device_id={axis: lax.rem(me + offset, n)}, device_id_type=MESH
            )
        greeted += len(offsets)
    pl.semaphore_wait(barrier, greeted)

    def direct_copy(job, offset):
        axis, n, _, _ = jobs[job]
        me = places[job][0]
        recv, send_sem, recv_sem = scratch[4 * job], scratch[4 * job + 2], scratch[4 * job + 3]
        peer = lax.rem(me + offset, n)
        return pltpu.make_async_remote_copy(
            src_ref=terms[job].at[peer],
            dst_ref=recv.at[me],
            send_sem=send_sem.at[offset],
            recv_sem=recv_sem.at[me],
            device_id={axis: peer},
            device_id_type=MESH,
        )

    for job, (axis, n, _, direct) in enumerate(jobs):
        if direct:
            for offset in range(1, n):
                direct_copy(job, offset).start()

    copies = [[[] for _ in range(2 * pieces)] for _, _, pieces, _ in jobs]
    for step in range(max(n for _, n, _, _ in jobs) - 1):
        for job, (axis, n, pieces, direct) in enumerate(jobs):
            if direct or step >= n - 1:
                continue
            me, right, left = places[job]
            recv, sendbuf, send_sem, recv_sem = scratch[4 * job:4 * job + 4]
            term_ref = terms[job]
            rows, half = outs[job].shape[0] // pieces, outs[job].shape[1] // 2
            for slot in range(2 * pieces):
                piece, way = divmod(slot, 2)
                dest, sign = ((right, -1), (left, 1))[way]
                block = lax.rem(me + n + sign * (step + 1), n)
                span = (pl.ds(piece * rows, rows), pl.ds(way * half, half))
                if step == 0:
                    src = term_ref.at[block, span[0], span[1]]
                else:
                    copies[job][slot][step - 1].wait_recv()
                    sendbuf[slot, step] = recv[slot, step - 1] + term_ref[block, span[0], span[1]]
                    src = sendbuf.at[slot, step]
                copy = pltpu.make_async_remote_copy(
                    src_ref=src,
                    dst_ref=recv.at[slot, step],
                    send_sem=send_sem.at[slot, step],
                    recv_sem=recv_sem.at[slot, step],
                    device_id={axis: dest},
                    device_id_type=MESH,
                )
                copy.start()
                copies[job][slot].append(copy)
    for job, (axis, n, pieces, direct) in enumerate(jobs):
        me = places[job][0]
        recv = scratch[4 * job]
        if direct:
            outs[job][...] = terms[job][me]
            for sender in range(n):
                @pl.when(sender != me)
                def _():
                    pltpu.make_async_remote_copy(
                        src_ref=terms[job].at[sender],
                        dst_ref=recv.at[sender],
                        send_sem=scratch[4 * job + 2].at[0],
                        recv_sem=scratch[4 * job + 3].at[sender],
                        device_id={axis: sender},
                        device_id_type=MESH,
                    ).wait_recv()
                    outs[job][...] += recv[sender]
            continue
        rows, half = outs[job].shape[0] // pieces, outs[job].shape[1] // 2
        for slot in range(2 * pieces):
            piece, way = divmod(slot, 2)
            span = (pl.ds(piece * rows, rows), pl.ds(way * half, half))
            copies[job][slot][n - 2].wait_recv()
            outs[job][span[0], span[1]] = (
                recv[slot, n - 2] + terms[job][me, span[0], span[1]]
            ).astype(outs[job].dtype)
    for job, (axis, n, pieces, direct) in enumerate(jobs):
        if direct:
            for offset in range(1, n):
                direct_copy(job, offset).wait_send()
        for slot in range(2 * pieces):
            for copy in copies[job][slot]:
                copy.wait_send()


def ring_scatter(parts, channel, factors=None):
    jobs = tuple((axis, terms.shape[0], pieces, direct) for terms, axis, _, pieces, direct in parts)
    produce = len(factors[0]) if factors else 0
    scratch = []
    for terms, _, _, pieces, direct in parts:
        n, rows, width = terms.shape
        if direct:
            scratch += [
                pltpu.VMEM((n, rows, width), jnp.float32),
                pltpu.VMEM((8, 128), jnp.float32),
                pltpu.SemaphoreType.DMA((n,)),
                pltpu.SemaphoreType.DMA((n,)),
            ]
            continue
        scratch += [
            pltpu.VMEM((2 * pieces, n - 1, rows // pieces, width // 2), jnp.float32),
            pltpu.VMEM((2 * pieces, n - 1, rows // pieces, width // 2), jnp.float32),
            pltpu.SemaphoreType.DMA((2 * pieces, n - 1)),
            pltpu.SemaphoreType.DMA((2 * pieces, n - 1)),
        ]
    size = sum(math.prod(part[0].shape) for part in parts)
    operands = [part[0] for part in parts]
    if produce:
        scratch.append(pltpu.VMEM(parts[0][0].shape, jnp.float32))
        operands = list(factors[0]) + list(factors[1]) + operands[1:]
    return pl.pallas_call(
        functools.partial(ring_scatter_kernel, jobs, produce),
        out_shape=tuple(
            jax.ShapeDtypeStruct(part[0].shape[1:], part[2]) for part in parts
        ),
        in_specs=[pl.BlockSpec(memory_space=pltpu.VMEM)] * len(operands),
        out_specs=tuple(pl.BlockSpec(memory_space=pltpu.VMEM) for _ in parts),
        scratch_shapes=scratch,
        compiler_params=pltpu.CompilerParams(
            collective_id=channel, has_side_effects=True, vmem_limit_bytes=48 * 1024 * 1024
        ),
        cost_estimate=pl.CostEstimate(flops=2 * size, bytes_accessed=8 * size, transcendentals=0),
    )(*operands)


def exchange_kernel(n, axis, kv_ref, qg_ref, prefix_ref, suffix_ref,
                    pair_in, chip_sum, kv_in, qg_in, pair_sem, send_sem, recv_sem):
    me = lax.axis_index(axis)
    chips = n // 2
    chip, core = me // 2, lax.rem(me, 2)
    partner = me + 1 - 2 * core
    barrier = pltpu.get_barrier_semaphore()
    pl.semaphore_signal(barrier, inc=1, device_id={axis: partner}, device_id_type=MESH)
    for offset in range(1, chips):
        peer = lax.rem(chip + offset, chips) * 2 + core
        pl.semaphore_signal(barrier, inc=1, device_id={axis: peer}, device_id_type=MESH)
    pl.semaphore_wait(barrier, chips)

    swaps = []
    for kind, ref in enumerate((kv_ref, qg_ref)):
        swap = pltpu.make_async_remote_copy(
            src_ref=ref, dst_ref=pair_in.at[kind], send_sem=pair_sem.at[0, kind],
            recv_sem=pair_sem.at[1, kind], device_id={axis: partner}, device_id_type=MESH,
        )
        swap.start()
        swaps.append(swap)
    for swap in swaps:
        swap.wait_recv()
    chip_sum[0] = kv_ref[...] + pair_in[0]
    chip_sum[1] = qg_ref[...] + pair_in[1]

    def route(offset, later):
        peer = lax.rem(chip + offset, chips) * 2 + core
        kind = 0 if later else 1
        return pltpu.make_async_remote_copy(
            src_ref=chip_sum.at[kind],
            dst_ref=(kv_in if later else qg_in).at[chip],
            send_sem=send_sem.at[kind, offset],
            recv_sem=recv_sem.at[kind, chip],
            device_id={axis: peer},
            device_id_type=MESH,
        )

    for offset in range(1, chips):
        for later in (True, False):
            @pl.when((chip + offset < chips) == later)
            def _():
                route(offset, later).start()

    prefix_ref[...] = jnp.where(core == 1, pair_in[0], 0.0)
    suffix_ref[...] = jnp.where(core == 0, pair_in[1], 0.0)
    for sender in range(chips):
        @pl.when(sender < chip)
        def _():
            pltpu.make_async_remote_copy(
                src_ref=chip_sum.at[0], dst_ref=kv_in.at[sender], send_sem=send_sem.at[0, 0],
                recv_sem=recv_sem.at[0, sender], device_id={axis: sender * 2 + core},
                device_id_type=MESH,
            ).wait_recv()
            prefix_ref[...] += kv_in[sender]

        @pl.when(sender > chip)
        def _():
            pltpu.make_async_remote_copy(
                src_ref=chip_sum.at[1], dst_ref=qg_in.at[sender], send_sem=send_sem.at[1, 0],
                recv_sem=recv_sem.at[1, sender], device_id={axis: sender * 2 + core},
                device_id_type=MESH,
            ).wait_recv()
            suffix_ref[...] += qg_in[sender]

    for swap in swaps:
        swap.wait_send()
    for offset in range(1, chips):
        for later in (True, False):
            @pl.when((chip + offset < chips) == later)
            def _():
                route(offset, later).wait_send()


def exchange_states(kv_state, qg_state, axis):
    n = lax.axis_size(axis)
    chips = n // 2
    shape = kv_state.shape
    return pl.pallas_call(
        functools.partial(exchange_kernel, n, axis),
        out_shape=(jax.ShapeDtypeStruct(shape, jnp.float32),) * 2,
        in_specs=[pl.BlockSpec(memory_space=pltpu.VMEM)] * 2,
        out_specs=(pl.BlockSpec(memory_space=pltpu.VMEM),) * 2,
        scratch_shapes=[
            pltpu.VMEM((2,) + shape, jnp.float32),
            pltpu.VMEM((2,) + shape, jnp.float32),
            pltpu.VMEM((chips,) + shape, jnp.float32),
            pltpu.VMEM((chips,) + shape, jnp.float32),
            pltpu.SemaphoreType.DMA((2, 2)),
            pltpu.SemaphoreType.DMA((2, chips)),
            pltpu.SemaphoreType.DMA((2, chips)),
        ],
        compiler_params=pltpu.CompilerParams(collective_id=2, has_side_effects=True),
    )(kv_state, qg_state)


def local(layer_input, w_query, w_key, w_value, w_out, out_grad):
    num_rows = layer_input.shape[1]
    local_heads = w_query.shape[1] // HEAD_DIM
    width = local_heads * HEAD_DIM
    in_rows = layer_input[0]
    grad_rows = out_grad[0]

    def project(weight):
        result = jnp.dot(in_rows, weight, preferred_element_type=jnp.float32).astype(jnp.bfloat16)
        return result.reshape(num_rows, local_heads, HEAD_DIM)

    queries = project(w_query)
    key_rows = project(w_key)
    value_rows = project(w_value)
    row_start = lax.axis_index("seq") * num_rows
    positions = (row_start + jnp.arange(num_rows, dtype=jnp.int32)).astype(jnp.float32)
    pos_scale = 1.0 / jnp.sqrt(HEAD_DIM * (positions + 1.0))
    backward = jnp.einsum("td,kd->tk", grad_rows, w_out, preferred_element_type=jnp.float32)
    grad_in = (
        (backward * pos_scale[:, None])
        .astype(jnp.bfloat16)
        .reshape(num_rows, local_heads, HEAD_DIM)
    )
    kv_state = jnp.einsum("thd,the->hde", key_rows, value_rows, preferred_element_type=jnp.float32)
    qg_state = jnp.einsum("thd,the->hde", queries, grad_in, preferred_element_type=jnp.float32)
    prefix, suffix = exchange_states(kv_state, qg_state, "seq")
    prefix = prefix.astype(jnp.bfloat16)
    suffix = suffix.astype(jnp.bfloat16)
    causal = (jnp.arange(num_rows)[:, None] >= jnp.arange(num_rows)[None, :])[None]
    scores = jnp.einsum("thd,shd->hts", queries, key_rows, preferred_element_type=jnp.float32)
    scores_qk = jnp.where(causal, scores, 0.0).astype(jnp.bfloat16)
    scores_g = jnp.einsum("thd,shd->hts", grad_in, value_rows, preferred_element_type=jnp.float32)
    scores_gv = jnp.where(causal, scores_g, 0.0).astype(jnp.bfloat16)
    inner_sum = jnp.einsum(
        "hts,she->the", scores_qk, value_rows, preferred_element_type=jnp.float32
    )
    cross_sum = jnp.einsum("thd,hde->the", queries, prefix, preferred_element_type=jnp.float32)
    attention = (
        ((inner_sum + cross_sum) * pos_scale[:, None, None])
        .astype(jnp.bfloat16)
        .reshape(num_rows, width)
    )
    d_query = jnp.einsum("hts,shd->thd", scores_gv, key_rows, preferred_element_type=jnp.float32)
    d_query = d_query + jnp.einsum(
        "the,hde->thd", grad_in, prefix, preferred_element_type=jnp.float32
    )
    d_keys = jnp.einsum("hts,thd->shd", scores_gv, queries, preferred_element_type=jnp.float32)
    d_keys = d_keys + jnp.einsum(
        "she,hde->shd", value_rows, suffix, preferred_element_type=jnp.float32
    )
    d_values = jnp.einsum("hts,the->she", scores_qk, grad_in, preferred_element_type=jnp.float32)
    d_values = d_values + jnp.einsum(
        "shd,hde->she", key_rows, suffix, preferred_element_type=jnp.float32
    )
    d_query = d_query.astype(jnp.bfloat16).reshape(num_rows, width)
    d_keys = d_keys.astype(jnp.bfloat16).reshape(num_rows, width)
    d_values = d_values.astype(jnp.bfloat16).reshape(num_rows, width)
    groups = lax.axis_size("head")
    head_terms = jax.ShapeDtypeStruct((groups, num_rows, w_query.shape[0] // groups), jnp.float32)
    total_rows = lax.axis_size("seq") * lax.axis_size("dp") * num_rows
    grad_scale = jnp.float32(1.0) / jnp.sqrt(jnp.float32(total_rows))
    seqs, shares = lax.axis_size("seq"), lax.axis_size("dp")
    grads = jnp.concatenate([d_query, d_keys, d_values], axis=1)
    term_qkv = jnp.einsum("td,tk->dk", in_rows, grads, preferred_element_type=jnp.float32) * grad_scale
    grad_blocks = grad_rows.reshape(num_rows, seqs, shares, -1)
    term_out = jnp.einsum(
        "tspr,tk->psrk", grad_blocks, attention, preferred_element_type=jnp.float32
    ) * grad_scale
    term_out = term_out.reshape(shares, -1, width)
    factors = ((d_query, d_keys, d_values), (w_query, w_key, w_value))
    term_qkv, factors, term_out = lax.optimization_barrier((term_qkv, factors, term_out))
    summed = lax.psum_scatter(term_qkv, "seq", scatter_dimension=0, tiled=True)
    input_grad, out_shared = ring_scatter(
        [(head_terms, "head", jnp.float32, 4, False), (term_out, "dp", jnp.float32, 2, False)], 0,
        factors,
    )
    input_grad = input_grad.astype(jnp.bfloat16)[None]
    summed, input_grad, out_shared = lax.optimization_barrier((summed, input_grad, out_shared))
    summed, out_summed = ring_scatter(
        [
            (summed.reshape(shares, -1, summed.shape[1]), "dp", jnp.float32, 2, False),
            (out_shared.reshape(seqs, -1, width), "seq", jnp.float32, 1, True),
        ],
        1,
    )
    grad_query = summed[:, :width]
    grad_key = summed[:, width:2 * width]
    grad_value = summed[:, 2 * width:]
    grad_out = out_summed.T
    return (input_grad, grad_query, grad_key, grad_value, grad_out)


def solution(mesh):
    return jax.shard_map(
        local,
        mesh=mesh,
        in_specs=(
            P("dp", "seq", None),
            P(None, "head"),
            P(None, "head"),
            P(None, "head"),
            P("head", None),
            P("dp", "seq", None),
        ),
        out_specs=(
            P("dp", "seq", "head"),
            P(("seq", "dp"), "head"),
            P(("seq", "dp"), "head"),
            P(("seq", "dp"), "head"),
            P("head", ("seq", "dp")),
        ),
        check_vma=False,
    )
```

```python
import functools
import math

import jax
import jax.numpy as jnp
from jax import lax
from jax.experimental import pallas as pl
from jax.experimental.pallas import tpu as pltpu
from jax.sharding import PartitionSpec as P

HEAD_DIM = 128
MESH = pl.DeviceIdType.MESH


def ring_scatter_kernel(jobs, produce, *refs):
    count = len(jobs)
    terms, outs, scratch = refs[:count], refs[count:2 * count], refs[2 * count:]
    if produce:
        factors, refs = refs[:2 * produce], refs[2 * produce:]
        made, held, held_sem = refs[-2 - produce], refs[-1 - produce:-1], refs[-1]
        refs = refs[:-2 - produce]
        terms = (made,) + refs[:count - 1]
        outs, scratch = refs[count - 1:2 * count - 1], refs[2 * count - 1:]
        grads, weights = factors[:produce], held
        loads = [
            pltpu.make_async_copy(source, target, held_sem.at[index])
            for index, (source, target) in enumerate(zip(factors[produce:], held))
        ]
        for load in loads:
            load.start()
    barrier = pltpu.get_barrier_semaphore()
    places, greeted = [], 0
    for axis, n, _, direct in jobs:
        me = lax.axis_index(axis)
        right, left = lax.rem(me + 1, n), lax.rem(me + n - 1, n)
        places.append((me, right, left))
        offsets = range(1, n) if direct else (n - 1, 1)
        for offset in offsets:
            pl.semaphore_signal(
                barrier, inc=1, device_id={axis: lax.rem(me + offset, n)}, device_id_type=MESH
            )
        greeted += len(offsets)
    pl.semaphore_wait(barrier, greeted)
    if produce:
        for load in loads:
            load.wait()
        block_rows = made.shape[2]
        for block in range(made.shape[0]):
            rows = pl.ds(block * block_rows, block_rows)
            total = None
            for grad, weight in zip(grads, weights):
                part = lax.dot_general(
                    grad[...], weight[rows, :], (((1,), (1,)), ((), ())),
                    preferred_element_type=jnp.float32,
                )
                total = part if total is None else total + part
            made[block] = total

    def direct_copy(job, offset):
        axis, n, _, _ = jobs[job]
        me = places[job][0]
        recv, send_sem, recv_sem = scratch[4 * job], scratch[4 * job + 2], scratch[4 * job + 3]
        peer = lax.rem(me + offset, n)
        return pltpu.make_async_remote_copy(
            src_ref=terms[job].at[peer],
            dst_ref=recv.at[me],
            send_sem=send_sem.at[offset],
            recv_sem=recv_sem.at[me],
            device_id={axis: peer},
            device_id_type=MESH,
        )

    for job, (axis, n, _, direct) in enumerate(jobs):
        if direct:
            for offset in range(1, n):
                direct_copy(job, offset).start()

    copies = [[[] for _ in range(2 * pieces)] for _, _, pieces, _ in jobs]
    for step in range(max(n for _, n, _, _ in jobs) - 1):
        for job, (axis, n, pieces, direct) in enumerate(jobs):
            if direct or step >= n - 1:
                continue
            me, right, left = places[job]
            recv, sendbuf, send_sem, recv_sem = scratch[4 * job:4 * job + 4]
            term_ref = terms[job]
            rows, half = outs[job].shape[0] // pieces, outs[job].shape[1] // 2
            for slot in range(2 * pieces):
                piece, way = divmod(slot, 2)
                dest, sign = ((right, -1), (left, 1))[way]
                block = lax.rem(me + n + sign * (step + 1), n)
                span = (pl.ds(piece * rows, rows), pl.ds(way * half, half))
                if step == 0:
                    src = term_ref.at[block, span[0], span[1]]
                else:
                    copies[job][slot][step - 1].wait_recv()
                    sendbuf[slot, step] = recv[slot, step - 1] + term_ref[block, span[0], span[1]]
                    src = sendbuf.at[slot, step]
                copy = pltpu.make_async_remote_copy(
                    src_ref=src,
                    dst_ref=recv.at[slot, step],
                    send_sem=send_sem.at[slot, step],
                    recv_sem=recv_sem.at[slot, step],
                    device_id={axis: dest},
                    device_id_type=MESH,
                )
                copy.start()
                copies[job][slot].append(copy)
    for job, (axis, n, pieces, direct) in enumerate(jobs):
        me = places[job][0]
        recv = scratch[4 * job]
        if direct:
            outs[job][...] = terms[job][me]
            for sender in range(n):
                @pl.when(sender != me)
                def _():
                    pltpu.make_async_remote_copy(
                        src_ref=terms[job].at[sender],
                        dst_ref=recv.at[sender],
                        send_sem=scratch[4 * job + 2].at[0],
                        recv_sem=scratch[4 * job + 3].at[sender],
                        device_id={axis: sender},
                        device_id_type=MESH,
                    ).wait_recv()
                    outs[job][...] += recv[sender]
            continue
        rows, half = outs[job].shape[0] // pieces, outs[job].shape[1] // 2
        for slot in range(2 * pieces):
            piece, way = divmod(slot, 2)
            span = (pl.ds(piece * rows, rows), pl.ds(way * half, half))
            copies[job][slot][n - 2].wait_recv()
            outs[job][span[0], span[1]] = (
                recv[slot, n - 2] + terms[job][me, span[0], span[1]]
            ).astype(outs[job].dtype)
    for job, (axis, n, pieces, direct) in enumerate(jobs):
        if direct:
            for offset in range(1, n):
                direct_copy(job, offset).wait_send()
        for slot in range(2 * pieces):
            for copy in copies[job][slot]:
                copy.wait_send()


def ring_scatter(parts, channel, factors=None):
    jobs = tuple((axis, terms.shape[0], pieces, direct) for terms, axis, _, pieces, direct in parts)
    produce = len(factors[0]) if factors else 0
    scratch = []
    for terms, _, _, pieces, direct in parts:
        n, rows, width = terms.shape
        if direct:
            scratch += [
                pltpu.VMEM((n, rows, width), jnp.float32),
                pltpu.VMEM((8, 128), jnp.float32),
                pltpu.SemaphoreType.DMA((n,)),
                pltpu.SemaphoreType.DMA((n,)),
            ]
            continue
        scratch += [
            pltpu.VMEM((2 * pieces, n - 1, rows // pieces, width // 2), jnp.float32),
            pltpu.VMEM((2 * pieces, n - 1, rows // pieces, width // 2), jnp.float32),
            pltpu.SemaphoreType.DMA((2 * pieces, n - 1)),
            pltpu.SemaphoreType.DMA((2 * pieces, n - 1)),
        ]
    size = sum(math.prod(part[0].shape) for part in parts)
    operands = [part[0] for part in parts]
    in_specs = [pl.BlockSpec(memory_space=pltpu.VMEM)] * len(operands)
    if produce:
        scratch.append(pltpu.VMEM(parts[0][0].shape, jnp.float32))
        scratch += [pltpu.VMEM(weight.shape, weight.dtype) for weight in factors[1]]
        scratch.append(pltpu.SemaphoreType.DMA((produce,)))
        operands = list(factors[0]) + list(factors[1]) + operands[1:]
        in_specs = (
            [pl.BlockSpec(memory_space=pltpu.VMEM)] * produce
            + [pl.BlockSpec(memory_space=pl.ANY)] * produce
            + [pl.BlockSpec(memory_space=pltpu.VMEM)] * (len(parts) - 1)
        )
    return pl.pallas_call(
        functools.partial(ring_scatter_kernel, jobs, produce),
        out_shape=tuple(
            jax.ShapeDtypeStruct(part[0].shape[1:], part[2]) for part in parts
        ),
        in_specs=in_specs,
        out_specs=tuple(pl.BlockSpec(memory_space=pltpu.VMEM) for _ in parts),
        scratch_shapes=scratch,
        compiler_params=pltpu.CompilerParams(
            collective_id=channel, has_side_effects=True
        ),
        cost_estimate=pl.CostEstimate(flops=2 * size, bytes_accessed=8 * size, transcendentals=0),
    )(*operands)


def exchange_kernel(n, axis, kv_ref, qg_ref, prefix_ref, suffix_ref,
                    pair_in, chip_sum, kv_in, qg_in, pair_sem, send_sem, recv_sem):
    me = lax.axis_index(axis)
    chips = n // 2
    chip, core = me // 2, lax.rem(me, 2)
    partner = me + 1 - 2 * core
    barrier = pltpu.get_barrier_semaphore()
    pl.semaphore_signal(barrier, inc=1, device_id={axis: partner}, device_id_type=MESH)
    for offset in range(1, chips):
        peer = lax.rem(chip + offset, chips) * 2 + core
        pl.semaphore_signal(barrier, inc=1, device_id={axis: peer}, device_id_type=MESH)
    pl.semaphore_wait(barrier, chips)

    swaps = []
    for kind, ref in enumerate((kv_ref, qg_ref)):
        swap = pltpu.make_async_remote_copy(
            src_ref=ref, dst_ref=pair_in.at[kind], send_sem=pair_sem.at[0, kind],
            recv_sem=pair_sem.at[1, kind], device_id={axis: partner}, device_id_type=MESH,
        )
        swap.start()
        swaps.append(swap)
    for swap in swaps:
        swap.wait_recv()
    chip_sum[0] = kv_ref[...] + pair_in[0]
    chip_sum[1] = qg_ref[...] + pair_in[1]

    def route(offset, later):
        peer = lax.rem(chip + offset, chips) * 2 + core
        kind = 0 if later else 1
        return pltpu.make_async_remote_copy(
            src_ref=chip_sum.at[kind],
            dst_ref=(kv_in if later else qg_in).at[chip],
            send_sem=send_sem.at[kind, offset],
            recv_sem=recv_sem.at[kind, chip],
            device_id={axis: peer},
            device_id_type=MESH,
        )

    for offset in range(1, chips):
        for later in (True, False):
            @pl.when((chip + offset < chips) == later)
            def _():
                route(offset, later).start()

    prefix_ref[...] = jnp.where(core == 1, pair_in[0], 0.0)
    suffix_ref[...] = jnp.where(core == 0, pair_in[1], 0.0)
    for sender in range(chips):
        @pl.when(sender < chip)
        def _():
            pltpu.make_async_remote_copy(
                src_ref=chip_sum.at[0], dst_ref=kv_in.at[sender], send_sem=send_sem.at[0, 0],
                recv_sem=recv_sem.at[0, sender], device_id={axis: sender * 2 + core},
                device_id_type=MESH,
            ).wait_recv()
            prefix_ref[...] += kv_in[sender]

        @pl.when(sender > chip)
        def _():
            pltpu.make_async_remote_copy(
                src_ref=chip_sum.at[1], dst_ref=qg_in.at[sender], send_sem=send_sem.at[1, 0],
                recv_sem=recv_sem.at[1, sender], device_id={axis: sender * 2 + core},
                device_id_type=MESH,
            ).wait_recv()
            suffix_ref[...] += qg_in[sender]

    for swap in swaps:
        swap.wait_send()
    for offset in range(1, chips):
        for later in (True, False):
            @pl.when((chip + offset < chips) == later)
            def _():
                route(offset, later).wait_send()


def exchange_states(kv_state, qg_state, axis):
    n = lax.axis_size(axis)
    chips = n // 2
    shape = kv_state.shape
    return pl.pallas_call(
        functools.partial(exchange_kernel, n, axis),
        out_shape=(jax.ShapeDtypeStruct(shape, jnp.float32),) * 2,
        in_specs=[pl.BlockSpec(memory_space=pltpu.VMEM)] * 2,
        out_specs=(pl.BlockSpec(memory_space=pltpu.VMEM),) * 2,
        scratch_shapes=[
            pltpu.VMEM((2,) + shape, jnp.float32),
            pltpu.VMEM((2,) + shape, jnp.float32),
            pltpu.VMEM((chips,) + shape, jnp.float32),
            pltpu.VMEM((chips,) + shape, jnp.float32),
            pltpu.SemaphoreType.DMA((2, 2)),
            pltpu.SemaphoreType.DMA((2, chips)),
            pltpu.SemaphoreType.DMA((2, chips)),
        ],
        compiler_params=pltpu.CompilerParams(collective_id=2, has_side_effects=True),
    )(kv_state, qg_state)


def local(layer_input, w_query, w_key, w_value, w_out, out_grad):
    num_rows = layer_input.shape[1]
    local_heads = w_query.shape[1] // HEAD_DIM
    width = local_heads * HEAD_DIM
    in_rows = layer_input[0]
    grad_rows = out_grad[0]

    def project(weight):
        result = jnp.dot(in_rows, weight, preferred_element_type=jnp.float32).astype(jnp.bfloat16)
        return result.reshape(num_rows, local_heads, HEAD_DIM)

    queries = project(w_query)
    key_rows = project(w_key)
    value_rows = project(w_value)
    row_start = lax.axis_index("seq") * num_rows
    positions = (row_start + jnp.arange(num_rows, dtype=jnp.int32)).astype(jnp.float32)
    pos_scale = 1.0 / jnp.sqrt(HEAD_DIM * (positions + 1.0))
    backward = jnp.einsum("td,kd->tk", grad_rows, w_out, preferred_element_type=jnp.float32)
    grad_in = (
        (backward * pos_scale[:, None])
        .astype(jnp.bfloat16)
        .reshape(num_rows, local_heads, HEAD_DIM)
    )
    kv_state = jnp.einsum("thd,the->hde", key_rows, value_rows, preferred_element_type=jnp.float32)
    qg_state = jnp.einsum("thd,the->hde", queries, grad_in, preferred_element_type=jnp.float32)
    prefix, suffix = exchange_states(kv_state, qg_state, "seq")
    prefix = prefix.astype(jnp.bfloat16)
    suffix = suffix.astype(jnp.bfloat16)
    causal = (jnp.arange(num_rows)[:, None] >= jnp.arange(num_rows)[None, :])[None]
    scores = jnp.einsum("thd,shd->hts", queries, key_rows, preferred_element_type=jnp.float32)
    scores_qk = jnp.where(causal, scores, 0.0).astype(jnp.bfloat16)
    scores_g = jnp.einsum("thd,shd->hts", grad_in, value_rows, preferred_element_type=jnp.float32)
    scores_gv = jnp.where(causal, scores_g, 0.0).astype(jnp.bfloat16)
    inner_sum = jnp.einsum(
        "hts,she->the", scores_qk, value_rows, preferred_element_type=jnp.float32
    )
    cross_sum = jnp.einsum("thd,hde->the", queries, prefix, preferred_element_type=jnp.float32)
    attention = (
        ((inner_sum + cross_sum) * pos_scale[:, None, None])
        .astype(jnp.bfloat16)
        .reshape(num_rows, width)
    )
    d_query = jnp.einsum("hts,shd->thd", scores_gv, key_rows, preferred_element_type=jnp.float32)
    d_query = d_query + jnp.einsum(
        "the,hde->thd", grad_in, prefix, preferred_element_type=jnp.float32
    )
    d_keys = jnp.einsum("hts,thd->shd", scores_gv, queries, preferred_element_type=jnp.float32)
    d_keys = d_keys + jnp.einsum(
        "she,hde->shd", value_rows, suffix, preferred_element_type=jnp.float32
    )
    d_values = jnp.einsum("hts,the->she", scores_qk, grad_in, preferred_element_type=jnp.float32)
    d_values = d_values + jnp.einsum(
        "shd,hde->she", key_rows, suffix, preferred_element_type=jnp.float32
    )
    d_query = d_query.astype(jnp.bfloat16).reshape(num_rows, width)
    d_keys = d_keys.astype(jnp.bfloat16).reshape(num_rows, width)
    d_values = d_values.astype(jnp.bfloat16).reshape(num_rows, width)
    groups = lax.axis_size("head")
    head_terms = jax.ShapeDtypeStruct((groups, num_rows, w_query.shape[0] // groups), jnp.float32)
    total_rows = lax.axis_size("seq") * lax.axis_size("dp") * num_rows
    grad_scale = jnp.float32(1.0) / jnp.sqrt(jnp.float32(total_rows))
    seqs, shares = lax.axis_size("seq"), lax.axis_size("dp")
    grads = jnp.concatenate([d_query, d_keys, d_values], axis=1)
    term_qkv = jnp.einsum("td,tk->dk", in_rows, grads, preferred_element_type=jnp.float32) * grad_scale
    grad_blocks = grad_rows.reshape(num_rows, seqs, shares, -1)
    term_out = jnp.einsum(
        "tspr,tk->psrk", grad_blocks, attention, preferred_element_type=jnp.float32
    ) * grad_scale
    term_out = term_out.reshape(shares, -1, width)
    factors = ((d_query, d_keys, d_values), (w_query, w_key, w_value))
    term_qkv, factors, term_out = lax.optimization_barrier((term_qkv, factors, term_out))
    summed = lax.psum_scatter(term_qkv, "seq", scatter_dimension=0, tiled=True)
    input_grad, out_shared = ring_scatter(
        [(head_terms, "head", jnp.float32, 4, False), (term_out, "dp", jnp.float32, 2, False)], 0,
        factors,
    )
    input_grad = input_grad.astype(jnp.bfloat16)[None]
    summed, input_grad, out_shared = lax.optimization_barrier((summed, input_grad, out_shared))
    summed, out_summed = ring_scatter(
        [
            (summed.reshape(shares, -1, summed.shape[1]), "dp", jnp.float32, 2, False),
            (out_shared.reshape(seqs, -1, width), "seq", jnp.float32, 1, True),
        ],
        1,
    )
    grad_query = summed[:, :width]
    grad_key = summed[:, width:2 * width]
    grad_value = summed[:, 2 * width:]
    grad_out = out_summed.T
    return (input_grad, grad_query, grad_key, grad_value, grad_out)


def solution(mesh):
    return jax.shard_map(
        local,
        mesh=mesh,
        in_specs=(
            P("dp", "seq", None),
            P(None, "head"),
            P(None, "head"),
            P(None, "head"),
            P("head", None),
            P("dp", "seq", None),
        ),
        out_specs=(
            P("dp", "seq", "head"),
            P(("seq", "dp"), "head"),
            P(("seq", "dp"), "head"),
            P(("seq", "dp"), "head"),
            P("head", ("seq", "dp")),
        ),
        check_vma=False,
    )
```

```python
import functools
import math

import jax
import jax.numpy as jnp
from jax import lax
from jax.experimental import pallas as pl
from jax.experimental.pallas import tpu as pltpu
from jax.sharding import PartitionSpec as P

HEAD_DIM = 128
MESH = pl.DeviceIdType.MESH


def ring_scatter_kernel(jobs, produce, *refs):
    count = len(jobs)
    if produce:
        factors, refs = refs[:2 * produce], refs[2 * produce:]
        made, refs = refs[-1], refs[:-1]
        terms = (made,) + refs[:count - 1]
        outs, scratch = refs[count - 1:2 * count - 1], refs[2 * count - 1:]
        grads, weights = factors[:produce], factors[produce:]
        block_rows = made.shape[2]
        for block in range(made.shape[0]):
            rows = pl.ds(block * block_rows, block_rows)
            total = None
            for grad, weight in zip(grads, weights):
                part = lax.dot_general(
                    grad[...], weight[rows, :], (((1,), (1,)), ((), ())),
                    preferred_element_type=jnp.float32,
                )
                total = part if total is None else total + part
            made[block] = total
    else:
        terms, outs, scratch = refs[:count], refs[count:2 * count], refs[2 * count:]
    barrier = pltpu.get_barrier_semaphore()
    places, greeted = [], 0
    for axis, n, _, direct in jobs:
        me = lax.axis_index(axis)
        right, left = lax.rem(me + 1, n), lax.rem(me + n - 1, n)
        places.append((me, right, left))
        offsets = range(1, n) if direct else (n - 1, 1)
        for offset in offsets:
            pl.semaphore_signal(
                barrier, inc=1, device_id={axis: lax.rem(me + offset, n)}, device_id_type=MESH
            )
        greeted += len(offsets)
    pl.semaphore_wait(barrier, greeted)

    def direct_copy(job, offset):
        axis, n, _, _ = jobs[job]
        me = places[job][0]
        recv, send_sem, recv_sem = scratch[4 * job], scratch[4 * job + 2], scratch[4 * job + 3]
        peer = lax.rem(me + offset, n)
        return pltpu.make_async_remote_copy(
            src_ref=terms[job].at[peer],
            dst_ref=recv.at[me],
            send_sem=send_sem.at[offset],
            recv_sem=recv_sem.at[me],
            device_id={axis: peer},
            device_id_type=MESH,
        )

    for job, (axis, n, _, direct) in enumerate(jobs):
        if direct:
            for offset in range(1, n):
                direct_copy(job, offset).start()

    copies = [[[] for _ in range(2 * pieces)] for _, _, pieces, _ in jobs]
    for step in range(max(n for _, n, _, _ in jobs) - 1):
        for job, (axis, n, pieces, direct) in enumerate(jobs):
            if direct or step >= n - 1:
                continue
            me, right, left = places[job]
            recv, sendbuf, send_sem, recv_sem = scratch[4 * job:4 * job + 4]
            term_ref = terms[job]
            rows, half = outs[job].shape[0] // pieces, outs[job].shape[1] // 2
            for slot in range(2 * pieces):
                piece, way = divmod(slot, 2)
                dest, sign = ((right, -1), (left, 1))[way]
                block = lax.rem(me + n + sign * (step + 1), n)
                span = (pl.ds(piece * rows, rows), pl.ds(way * half, half))
                if step == 0:
                    src = term_ref.at[block, span[0], span[1]]
                else:
                    copies[job][slot][step - 1].wait_recv()
                    sendbuf[slot, step] = recv[slot, step - 1] + term_ref[block, span[0], span[1]]
                    src = sendbuf.at[slot, step]
                copy = pltpu.make_async_remote_copy(
                    src_ref=src,
                    dst_ref=recv.at[slot, step],
                    send_sem=send_sem.at[slot, step],
                    recv_sem=recv_sem.at[slot, step],
                    device_id={axis: dest},
                    device_id_type=MESH,
                )
                copy.start()
                copies[job][slot].append(copy)
    for job, (axis, n, pieces, direct) in enumerate(jobs):
        me = places[job][0]
        recv = scratch[4 * job]
        if direct:
            outs[job][...] = terms[job][me]
            for sender in range(n):
                @pl.when(sender != me)
                def _():
                    pltpu.make_async_remote_copy(
                        src_ref=terms[job].at[sender],
                        dst_ref=recv.at[sender],
                        send_sem=scratch[4 * job + 2].at[0],
                        recv_sem=scratch[4 * job + 3].at[sender],
                        device_id={axis: sender},
                        device_id_type=MESH,
                    ).wait_recv()
                    outs[job][...] += recv[sender]
            continue
        rows, half = outs[job].shape[0] // pieces, outs[job].shape[1] // 2
        for slot in range(2 * pieces):
            piece, way = divmod(slot, 2)
            span = (pl.ds(piece * rows, rows), pl.ds(way * half, half))
            copies[job][slot][n - 2].wait_recv()
            outs[job][span[0], span[1]] = (
                recv[slot, n - 2] + terms[job][me, span[0], span[1]]
            ).astype(outs[job].dtype)
    for job, (axis, n, pieces, direct) in enumerate(jobs):
        if direct:
            for offset in range(1, n):
                direct_copy(job, offset).wait_send()
        for slot in range(2 * pieces):
            for copy in copies[job][slot]:
                copy.wait_send()


def ring_scatter(parts, channel, factors=None):
    jobs = tuple((axis, terms.shape[0], pieces, direct) for terms, axis, _, pieces, direct in parts)
    produce = len(factors[0]) if factors else 0
    scratch = []
    for terms, _, _, pieces, direct in parts:
        n, rows, width = terms.shape
        if direct:
            scratch += [
                pltpu.VMEM((n, rows, width), jnp.float32),
                pltpu.VMEM((8, 128), jnp.float32),
                pltpu.SemaphoreType.DMA((n,)),
                pltpu.SemaphoreType.DMA((n,)),
            ]
            continue
        scratch += [
            pltpu.VMEM((2 * pieces, n - 1, rows // pieces, width // 2), jnp.float32),
            pltpu.VMEM((2 * pieces, n - 1, rows // pieces, width // 2), jnp.float32),
            pltpu.SemaphoreType.DMA((2 * pieces, n - 1)),
            pltpu.SemaphoreType.DMA((2 * pieces, n - 1)),
        ]
    size = sum(math.prod(part[0].shape) for part in parts)
    operands = [part[0] for part in parts]
    if produce:
        scratch.append(pltpu.VMEM(parts[0][0].shape, jnp.float32))
        operands = list(factors[0]) + list(factors[1]) + operands[1:]
    return pl.pallas_call(
        functools.partial(ring_scatter_kernel, jobs, produce),
        out_shape=tuple(
            jax.ShapeDtypeStruct(part[0].shape[1:], part[2]) for part in parts
        ),
        in_specs=[pl.BlockSpec(memory_space=pltpu.VMEM)] * len(operands),
        out_specs=tuple(pl.BlockSpec(memory_space=pltpu.VMEM) for _ in parts),
        scratch_shapes=scratch,
        compiler_params=pltpu.CompilerParams(
            collective_id=channel, has_side_effects=True, vmem_limit_bytes=48 * 1024 * 1024
        ),
        cost_estimate=pl.CostEstimate(flops=2 * size, bytes_accessed=8 * size, transcendentals=0),
    )(*operands)


def exchange_kernel(n, axis, kv_ref, qg_ref, prefix_ref, suffix_ref,
                    pair_in, chip_sum, kv_in, qg_in, pair_sem, send_sem, recv_sem):
    me = lax.axis_index(axis)
    chips = n // 2
    chip, core = me // 2, lax.rem(me, 2)
    partner = me + 1 - 2 * core
    barrier = pltpu.get_barrier_semaphore()
    pl.semaphore_signal(barrier, inc=1, device_id={axis: partner}, device_id_type=MESH)
    for offset in range(1, chips):
        peer = lax.rem(chip + offset, chips) * 2 + core
        pl.semaphore_signal(barrier, inc=1, device_id={axis: peer}, device_id_type=MESH)
    pl.semaphore_wait(barrier, chips)

    swaps = []
    for kind, ref in enumerate((kv_ref, qg_ref)):
        swap = pltpu.make_async_remote_copy(
            src_ref=ref, dst_ref=pair_in.at[kind], send_sem=pair_sem.at[0, kind],
            recv_sem=pair_sem.at[1, kind], device_id={axis: partner}, device_id_type=MESH,
        )
        swap.start()
        swaps.append(swap)
    for swap in swaps:
        swap.wait_recv()
    chip_sum[0] = kv_ref[...] + pair_in[0]
    chip_sum[1] = qg_ref[...] + pair_in[1]

    def route(offset, later):
        peer = lax.rem(chip + offset, chips) * 2 + core
        kind = 0 if later else 1
        return pltpu.make_async_remote_copy(
            src_ref=chip_sum.at[kind],
            dst_ref=(kv_in if later else qg_in).at[chip],
            send_sem=send_sem.at[kind, offset],
            recv_sem=recv_sem.at[kind, chip],
            device_id={axis: peer},
            device_id_type=MESH,
        )

    for offset in range(1, chips):
        for later in (True, False):
            @pl.when((chip + offset < chips) == later)
            def _():
                route(offset, later).start()

    prefix_ref[...] = jnp.where(core == 1, pair_in[0], 0.0)
    suffix_ref[...] = jnp.where(core == 0, pair_in[1], 0.0)
    for sender in range(chips):
        @pl.when(sender < chip)
        def _():
            pltpu.make_async_remote_copy(
                src_ref=chip_sum.at[0], dst_ref=kv_in.at[sender], send_sem=send_sem.at[0, 0],
                recv_sem=recv_sem.at[0, sender], device_id={axis: sender * 2 + core},
                device_id_type=MESH,
            ).wait_recv()
            prefix_ref[...] += kv_in[sender]

        @pl.when(sender > chip)
        def _():
            pltpu.make_async_remote_copy(
                src_ref=chip_sum.at[1], dst_ref=qg_in.at[sender], send_sem=send_sem.at[1, 0],
                recv_sem=recv_sem.at[1, sender], device_id={axis: sender * 2 + core},
                device_id_type=MESH,
            ).wait_recv()
            suffix_ref[...] += qg_in[sender]

    for swap in swaps:
        swap.wait_send()
    for offset in range(1, chips):
        for later in (True, False):
            @pl.when((chip + offset < chips) == later)
            def _():
                route(offset, later).wait_send()


def exchange_states(kv_state, qg_state, axis):
    n = lax.axis_size(axis)
    chips = n // 2
    shape = kv_state.shape
    return pl.pallas_call(
        functools.partial(exchange_kernel, n, axis),
        out_shape=(jax.ShapeDtypeStruct(shape, jnp.float32),) * 2,
        in_specs=[pl.BlockSpec(memory_space=pltpu.VMEM)] * 2,
        out_specs=(pl.BlockSpec(memory_space=pltpu.VMEM),) * 2,
        scratch_shapes=[
            pltpu.VMEM((2,) + shape, jnp.float32),
            pltpu.VMEM((2,) + shape, jnp.float32),
            pltpu.VMEM((chips,) + shape, jnp.float32),
            pltpu.VMEM((chips,) + shape, jnp.float32),
            pltpu.SemaphoreType.DMA((2, 2)),
            pltpu.SemaphoreType.DMA((2, chips)),
            pltpu.SemaphoreType.DMA((2, chips)),
        ],
        compiler_params=pltpu.CompilerParams(collective_id=2, has_side_effects=True),
    )(kv_state, qg_state)


def local(layer_input, w_query, w_key, w_value, w_out, out_grad):
    num_rows = layer_input.shape[1]
    local_heads = w_query.shape[1] // HEAD_DIM
    width = local_heads * HEAD_DIM
    in_rows = layer_input[0]
    grad_rows = out_grad[0]

    def project(weight):
        result = jnp.dot(in_rows, weight, preferred_element_type=jnp.float32).astype(jnp.bfloat16)
        return result.reshape(num_rows, local_heads, HEAD_DIM)

    queries = project(w_query)
    key_rows = project(w_key)
    value_rows = project(w_value)
    row_start = lax.axis_index("seq") * num_rows
    positions = (row_start + jnp.arange(num_rows, dtype=jnp.int32)).astype(jnp.float32)
    pos_scale = 1.0 / jnp.sqrt(HEAD_DIM * (positions + 1.0))
    backward = jnp.einsum("td,kd->tk", grad_rows, w_out, preferred_element_type=jnp.float32)
    grad_in = (
        (backward * pos_scale[:, None])
        .astype(jnp.bfloat16)
        .reshape(num_rows, local_heads, HEAD_DIM)
    )
    kv_state = jnp.einsum("thd,the->hde", key_rows, value_rows, preferred_element_type=jnp.float32)
    qg_state = jnp.einsum("thd,the->hde", queries, grad_in, preferred_element_type=jnp.float32)
    prefix, suffix = exchange_states(kv_state, qg_state, "seq")
    prefix = prefix.astype(jnp.bfloat16)
    suffix = suffix.astype(jnp.bfloat16)
    causal = (jnp.arange(num_rows)[:, None] >= jnp.arange(num_rows)[None, :])[None]
    scores = jnp.einsum("thd,shd->hts", queries, key_rows, preferred_element_type=jnp.float32)
    scores_qk = jnp.where(causal, scores, 0.0).astype(jnp.bfloat16)
    scores_g = jnp.einsum("thd,shd->hts", grad_in, value_rows, preferred_element_type=jnp.float32)
    scores_gv = jnp.where(causal, scores_g, 0.0).astype(jnp.bfloat16)
    inner_sum = jnp.einsum(
        "hts,she->the", scores_qk, value_rows, preferred_element_type=jnp.float32
    )
    cross_sum = jnp.einsum("thd,hde->the", queries, prefix, preferred_element_type=jnp.float32)
    attention = (
        ((inner_sum + cross_sum) * pos_scale[:, None, None])
        .astype(jnp.bfloat16)
        .reshape(num_rows, width)
    )
    d_query = jnp.einsum("hts,shd->thd", scores_gv, key_rows, preferred_element_type=jnp.float32)
    d_query = d_query + jnp.einsum(
        "the,hde->thd", grad_in, prefix, preferred_element_type=jnp.float32
    )
    d_keys = jnp.einsum("hts,thd->shd", scores_gv, queries, preferred_element_type=jnp.float32)
    d_keys = d_keys + jnp.einsum(
        "she,hde->shd", value_rows, suffix, preferred_element_type=jnp.float32
    )
    d_values = jnp.einsum("hts,the->she", scores_qk, grad_in, preferred_element_type=jnp.float32)
    d_values = d_values + jnp.einsum(
        "shd,hde->she", key_rows, suffix, preferred_element_type=jnp.float32
    )
    d_query = d_query.astype(jnp.bfloat16).reshape(num_rows, width)
    d_keys = d_keys.astype(jnp.bfloat16).reshape(num_rows, width)
    d_values = d_values.astype(jnp.bfloat16).reshape(num_rows, width)
    groups = lax.axis_size("head")
    head_terms = jax.ShapeDtypeStruct((groups, num_rows, w_query.shape[0] // groups), jnp.float32)
    total_rows = lax.axis_size("seq") * lax.axis_size("dp") * num_rows
    grad_scale = jnp.float32(1.0) / jnp.sqrt(jnp.float32(total_rows))
    seqs, shares = lax.axis_size("seq"), lax.axis_size("dp")
    grads = jnp.concatenate([d_query, d_keys, d_values], axis=1)
    term_qkv = jnp.einsum("td,tk->dk", in_rows, grads, preferred_element_type=jnp.float32) * grad_scale
    grad_blocks = grad_rows.reshape(num_rows, seqs, shares, -1)
    term_out = jnp.einsum(
        "tspr,tk->psrk", grad_blocks, attention, preferred_element_type=jnp.float32
    ) * grad_scale
    term_out = term_out.reshape(shares, -1, width)
    factors = ((d_query, d_keys, d_values), (w_query, w_key, w_value))
    term_qkv, factors, term_out = lax.optimization_barrier((term_qkv, factors, term_out))
    summed = lax.psum_scatter(term_qkv, "seq", scatter_dimension=0, tiled=True)
    input_grad, out_shared = ring_scatter(
        [(head_terms, "head", jnp.float32, 4, False), (term_out, "dp", jnp.float32, 2, False)], 0,
        factors,
    )
    input_grad = input_grad.astype(jnp.bfloat16)[None]
    summed, input_grad, out_shared = lax.optimization_barrier((summed, input_grad, out_shared))
    summed, out_summed = ring_scatter(
        [
            (summed.reshape(shares, -1, summed.shape[1]), "dp", jnp.float32, 1, True),
            (out_shared.reshape(seqs, -1, width), "seq", jnp.float32, 1, True),
        ],
        1,
    )
    grad_query = summed[:, :width]
    grad_key = summed[:, width:2 * width]
    grad_value = summed[:, 2 * width:]
    grad_out = out_summed.T
    return (input_grad, grad_query, grad_key, grad_value, grad_out)


def solution(mesh):
    return jax.shard_map(
        local,
        mesh=mesh,
        in_specs=(
            P("dp", "seq", None),
            P(None, "head"),
            P(None, "head"),
            P(None, "head"),
            P("head", None),
            P("dp", "seq", None),
        ),
        out_specs=(
            P("dp", "seq", "head"),
            P(("seq", "dp"), "head"),
            P(("seq", "dp"), "head"),
            P(("seq", "dp"), "head"),
            P("head", ("seq", "dp")),
        ),
        check_vma=False,
    )
```

```python
import functools
import math

import jax
import jax.numpy as jnp
from jax import lax
from jax.experimental import pallas as pl
from jax.experimental.pallas import tpu as pltpu
from jax.sharding import PartitionSpec as P

HEAD_DIM = 128
MESH = pl.DeviceIdType.MESH


def ring_scatter_kernel(jobs, produce, *refs):
    count = len(jobs)
    if produce:
        factors, refs = refs[:2 * produce], refs[2 * produce:]
        made, refs = refs[-1], refs[:-1]
        terms = (made,) + refs[:count - 1]
        outs, scratch = refs[count - 1:2 * count - 1], refs[2 * count - 1:]
        grads, weights = factors[:produce], factors[produce:]
        block_rows = made.shape[2]
        for block in range(made.shape[0]):
            rows = pl.ds(block * block_rows, block_rows)
            total = None
            for grad, weight in zip(grads, weights):
                part = lax.dot_general(
                    grad[...], weight[rows, :], (((1,), (1,)), ((), ())),
                    preferred_element_type=jnp.float32,
                )
                total = part if total is None else total + part
            made[block] = total
    else:
        terms, outs, scratch = refs[:count], refs[count:2 * count], refs[2 * count:]
    barrier = pltpu.get_barrier_semaphore()
    places, greeted = [], 0
    for axis, n, _, direct in jobs:
        me = lax.axis_index(axis)
        right, left = lax.rem(me + 1, n), lax.rem(me + n - 1, n)
        places.append((me, right, left))
        offsets = range(1, n) if direct else (n - 1, 1)
        for offset in offsets:
            pl.semaphore_signal(
                barrier, inc=1, device_id={axis: lax.rem(me + offset, n)}, device_id_type=MESH
            )
        greeted += len(offsets)
    pl.semaphore_wait(barrier, greeted)

    def direct_copy(job, offset):
        axis, n, _, _ = jobs[job]
        me = places[job][0]
        recv, send_sem, recv_sem = scratch[4 * job], scratch[4 * job + 2], scratch[4 * job + 3]
        peer = lax.rem(me + offset, n)
        return pltpu.make_async_remote_copy(
            src_ref=terms[job].at[peer],
            dst_ref=recv.at[me],
            send_sem=send_sem.at[offset],
            recv_sem=recv_sem.at[me],
            device_id={axis: peer},
            device_id_type=MESH,
        )

    for job, (axis, n, _, direct) in enumerate(jobs):
        if direct:
            for offset in range(1, n):
                direct_copy(job, offset).start()

    copies = [[[] for _ in range(2 * pieces)] for _, _, pieces, _ in jobs]
    for step in range(max(n for _, n, _, _ in jobs) - 1):
        for job, (axis, n, pieces, direct) in enumerate(jobs):
            if direct or step >= n - 1:
                continue
            me, right, left = places[job]
            recv, sendbuf, send_sem, recv_sem = scratch[4 * job:4 * job + 4]
            term_ref = terms[job]
            rows, half = outs[job].shape[0] // pieces, outs[job].shape[1] // 2
            for slot in range(2 * pieces):
                piece, way = divmod(slot, 2)
                dest, sign = ((right, -1), (left, 1))[way]
                block = lax.rem(me + n + sign * (step + 1), n)
                span = (pl.ds(piece * rows, rows), pl.ds(way * half, half))
                if step == 0:
                    src = term_ref.at[block, span[0], span[1]]
                else:
                    copies[job][slot][step - 1].wait_recv()
                    sendbuf[slot, step] = recv[slot, step - 1] + term_ref[block, span[0], span[1]]
                    src = sendbuf.at[slot, step]
                copy = pltpu.make_async_remote_copy(
                    src_ref=src,
                    dst_ref=recv.at[slot, step],
                    send_sem=send_sem.at[slot, step],
                    recv_sem=recv_sem.at[slot, step],
                    device_id={axis: dest},
                    device_id_type=MESH,
                )
                copy.start()
                copies[job][slot].append(copy)
    for job, (axis, n, pieces, direct) in enumerate(jobs):
        me = places[job][0]
        recv = scratch[4 * job]
        if direct:
            outs[job][...] = terms[job][me]
            for sender in range(n):
                @pl.when(sender != me)
                def _():
                    pltpu.make_async_remote_copy(
                        src_ref=terms[job].at[sender],
                        dst_ref=recv.at[sender],
                        send_sem=scratch[4 * job + 2].at[0],
                        recv_sem=scratch[4 * job + 3].at[sender],
                        device_id={axis: sender},
                        device_id_type=MESH,
                    ).wait_recv()
                    outs[job][...] += recv[sender]
            continue
        rows, half = outs[job].shape[0] // pieces, outs[job].shape[1] // 2
        for slot in range(2 * pieces):
            piece, way = divmod(slot, 2)
            span = (pl.ds(piece * rows, rows), pl.ds(way * half, half))
            copies[job][slot][n - 2].wait_recv()
            outs[job][span[0], span[1]] = (
                recv[slot, n - 2] + terms[job][me, span[0], span[1]]
            ).astype(outs[job].dtype)
    for job, (axis, n, pieces, direct) in enumerate(jobs):
        if direct:
            for offset in range(1, n):
                direct_copy(job, offset).wait_send()
        for slot in range(2 * pieces):
            for copy in copies[job][slot]:
                copy.wait_send()


def ring_scatter(parts, channel, factors=None):
    jobs = tuple((axis, terms.shape[0], pieces, direct) for terms, axis, _, pieces, direct in parts)
    produce = len(factors[0]) if factors else 0
    scratch = []
    for terms, _, _, pieces, direct in parts:
        n, rows, width = terms.shape
        if direct:
            scratch += [
                pltpu.VMEM((n, rows, width), jnp.float32),
                pltpu.VMEM((8, 128), jnp.float32),
                pltpu.SemaphoreType.DMA((n,)),
                pltpu.SemaphoreType.DMA((n,)),
            ]
            continue
        scratch += [
            pltpu.VMEM((2 * pieces, n - 1, rows // pieces, width // 2), jnp.float32),
            pltpu.VMEM((2 * pieces, n - 1, rows // pieces, width // 2), jnp.float32),
            pltpu.SemaphoreType.DMA((2 * pieces, n - 1)),
            pltpu.SemaphoreType.DMA((2 * pieces, n - 1)),
        ]
    size = sum(math.prod(part[0].shape) for part in parts)
    operands = [part[0] for part in parts]
    if produce:
        scratch.append(pltpu.VMEM(parts[0][0].shape, jnp.float32))
        operands = list(factors[0]) + list(factors[1]) + operands[1:]
    return pl.pallas_call(
        functools.partial(ring_scatter_kernel, jobs, produce),
        out_shape=tuple(
            jax.ShapeDtypeStruct(part[0].shape[1:], part[2]) for part in parts
        ),
        in_specs=[pl.BlockSpec(memory_space=pltpu.VMEM)] * len(operands),
        out_specs=tuple(pl.BlockSpec(memory_space=pltpu.VMEM) for _ in parts),
        scratch_shapes=scratch,
        compiler_params=pltpu.CompilerParams(
            collective_id=channel, has_side_effects=True, vmem_limit_bytes=48 * 1024 * 1024
        ),
        cost_estimate=pl.CostEstimate(flops=2 * size, bytes_accessed=8 * size, transcendentals=0),
    )(*operands)


def exchange_kernel(n, axis, kv_ref, qg_ref, prefix_ref, suffix_ref,
                    pair_in, chip_sum, kv_in, qg_in, pair_sem, send_sem, recv_sem):
    me = lax.axis_index(axis)
    chips = n // 2
    chip, core = me // 2, lax.rem(me, 2)
    partner = me + 1 - 2 * core
    barrier = pltpu.get_barrier_semaphore()
    pl.semaphore_signal(barrier, inc=1, device_id={axis: partner}, device_id_type=MESH)
    for offset in range(1, chips):
        peer = lax.rem(chip + offset, chips) * 2 + core
        pl.semaphore_signal(barrier, inc=1, device_id={axis: peer}, device_id_type=MESH)
    pl.semaphore_wait(barrier, chips)

    swaps = []
    for kind, ref in enumerate((kv_ref, qg_ref)):
        swap = pltpu.make_async_remote_copy(
            src_ref=ref, dst_ref=pair_in.at[kind], send_sem=pair_sem.at[0, kind],
            recv_sem=pair_sem.at[1, kind], device_id={axis: partner}, device_id_type=MESH,
        )
        swap.start()
        swaps.append(swap)
    for swap in swaps:
        swap.wait_recv()
    chip_sum[0] = kv_ref[...] + pair_in[0]
    chip_sum[1] = qg_ref[...] + pair_in[1]

    def route(offset, later):
        peer = lax.rem(chip + offset, chips) * 2 + core
        kind = 0 if later else 1
        return pltpu.make_async_remote_copy(
            src_ref=chip_sum.at[kind],
            dst_ref=(kv_in if later else qg_in).at[chip],
            send_sem=send_sem.at[kind, offset],
            recv_sem=recv_sem.at[kind, chip],
            device_id={axis: peer},
            device_id_type=MESH,
        )

    for offset in range(1, chips):
        for later in (True, False):
            @pl.when((chip + offset < chips) == later)
            def _():
                route(offset, later).start()

    prefix_ref[...] = jnp.where(core == 1, pair_in[0], 0.0)
    suffix_ref[...] = jnp.where(core == 0, pair_in[1], 0.0)
    for sender in range(chips):
        @pl.when(sender < chip)
        def _():
            pltpu.make_async_remote_copy(
                src_ref=chip_sum.at[0], dst_ref=kv_in.at[sender], send_sem=send_sem.at[0, 0],
                recv_sem=recv_sem.at[0, sender], device_id={axis: sender * 2 + core},
                device_id_type=MESH,
            ).wait_recv()
            prefix_ref[...] += kv_in[sender]

        @pl.when(sender > chip)
        def _():
            pltpu.make_async_remote_copy(
                src_ref=chip_sum.at[1], dst_ref=qg_in.at[sender], send_sem=send_sem.at[1, 0],
                recv_sem=recv_sem.at[1, sender], device_id={axis: sender * 2 + core},
                device_id_type=MESH,
            ).wait_recv()
            suffix_ref[...] += qg_in[sender]

    for swap in swaps:
        swap.wait_send()
    for offset in range(1, chips):
        for later in (True, False):
            @pl.when((chip + offset < chips) == later)
            def _():
                route(offset, later).wait_send()


def exchange_states(kv_state, qg_state, axis):
    n = lax.axis_size(axis)
    chips = n // 2
    shape = kv_state.shape
    return pl.pallas_call(
        functools.partial(exchange_kernel, n, axis),
        out_shape=(jax.ShapeDtypeStruct(shape, jnp.float32),) * 2,
        in_specs=[pl.BlockSpec(memory_space=pltpu.VMEM)] * 2,
        out_specs=(pl.BlockSpec(memory_space=pltpu.VMEM),) * 2,
        scratch_shapes=[
            pltpu.VMEM((2,) + shape, jnp.float32),
            pltpu.VMEM((2,) + shape, jnp.float32),
            pltpu.VMEM((chips,) + shape, jnp.float32),
            pltpu.VMEM((chips,) + shape, jnp.float32),
            pltpu.SemaphoreType.DMA((2, 2)),
            pltpu.SemaphoreType.DMA((2, chips)),
            pltpu.SemaphoreType.DMA((2, chips)),
        ],
        compiler_params=pltpu.CompilerParams(collective_id=2, has_side_effects=True),
    )(kv_state, qg_state)


def local(layer_input, w_query, w_key, w_value, w_out, out_grad):
    num_rows = layer_input.shape[1]
    local_heads = w_query.shape[1] // HEAD_DIM
    width = local_heads * HEAD_DIM
    in_rows = layer_input[0]
    grad_rows = out_grad[0]

    def project(weight):
        result = jnp.dot(in_rows, weight, preferred_element_type=jnp.float32).astype(jnp.bfloat16)
        return result.reshape(num_rows, local_heads, HEAD_DIM)

    queries = project(w_query)
    key_rows = project(w_key)
    value_rows = project(w_value)
    row_start = lax.axis_index("seq") * num_rows
    positions = (row_start + jnp.arange(num_rows, dtype=jnp.int32)).astype(jnp.float32)
    pos_scale = 1.0 / jnp.sqrt(HEAD_DIM * (positions + 1.0))
    backward = jnp.einsum("td,kd->tk", grad_rows, w_out, preferred_element_type=jnp.float32)
    grad_in = (
        (backward * pos_scale[:, None])
        .astype(jnp.bfloat16)
        .reshape(num_rows, local_heads, HEAD_DIM)
    )
    kv_state = jnp.einsum("thd,the->hde", key_rows, value_rows, preferred_element_type=jnp.float32)
    qg_state = jnp.einsum("thd,the->hde", queries, grad_in, preferred_element_type=jnp.float32)
    prefix, suffix = exchange_states(kv_state, qg_state, "seq")
    prefix = prefix.astype(jnp.bfloat16)
    suffix = suffix.astype(jnp.bfloat16)
    causal = (jnp.arange(num_rows)[:, None] >= jnp.arange(num_rows)[None, :])[None]
    scores = jnp.einsum("thd,shd->hts", queries, key_rows, preferred_element_type=jnp.float32)
    scores_qk = jnp.where(causal, scores, 0.0).astype(jnp.bfloat16)
    scores_g = jnp.einsum("thd,shd->hts", grad_in, value_rows, preferred_element_type=jnp.float32)
    scores_gv = jnp.where(causal, scores_g, 0.0).astype(jnp.bfloat16)
    inner_sum = jnp.einsum(
        "hts,she->the", scores_qk, value_rows, preferred_element_type=jnp.float32
    )
    cross_sum = jnp.einsum("thd,hde->the", queries, prefix, preferred_element_type=jnp.float32)
    attention = (
        ((inner_sum + cross_sum) * pos_scale[:, None, None])
        .astype(jnp.bfloat16)
        .reshape(num_rows, width)
    )
    d_query = jnp.einsum("hts,shd->thd", scores_gv, key_rows, preferred_element_type=jnp.float32)
    d_query = d_query + jnp.einsum(
        "the,hde->thd", grad_in, prefix, preferred_element_type=jnp.float32
    )
    d_keys = jnp.einsum("hts,thd->shd", scores_gv, queries, preferred_element_type=jnp.float32)
    d_keys = d_keys + jnp.einsum(
        "she,hde->shd", value_rows, suffix, preferred_element_type=jnp.float32
    )
    d_values = jnp.einsum("hts,the->she", scores_qk, grad_in, preferred_element_type=jnp.float32)
    d_values = d_values + jnp.einsum(
        "shd,hde->she", key_rows, suffix, preferred_element_type=jnp.float32
    )
    d_query = d_query.astype(jnp.bfloat16).reshape(num_rows, width)
    d_keys = d_keys.astype(jnp.bfloat16).reshape(num_rows, width)
    d_values = d_values.astype(jnp.bfloat16).reshape(num_rows, width)
    groups = lax.axis_size("head")
    head_terms = jax.ShapeDtypeStruct((groups, num_rows, w_query.shape[0] // groups), jnp.float32)
    total_rows = lax.axis_size("seq") * lax.axis_size("dp") * num_rows
    grad_scale = jnp.float32(1.0) / jnp.sqrt(jnp.float32(total_rows))
    seqs, shares = lax.axis_size("seq"), lax.axis_size("dp")
    grads = jnp.concatenate([d_query, d_keys, d_values], axis=1)
    term_qkv = jnp.einsum("td,tk->dk", in_rows, grads, preferred_element_type=jnp.float32) * grad_scale
    grad_blocks = grad_rows.reshape(num_rows, seqs, shares, -1)
    term_out = jnp.einsum(
        "tspr,tk->psrk", grad_blocks, attention, preferred_element_type=jnp.float32
    ) * grad_scale
    term_out = term_out.reshape(shares, -1, width)
    factors = ((d_query, d_keys, d_values), (w_query, w_key, w_value))
    term_qkv, factors, term_out = lax.optimization_barrier((term_qkv, factors, term_out))
    summed = lax.psum_scatter(term_qkv, "seq", scatter_dimension=0, tiled=True)
    input_grad, out_shared = ring_scatter(
        [(head_terms, "head", jnp.float32, 8, False), (term_out, "dp", jnp.float32, 2, False)], 0,
        factors,
    )
    input_grad = input_grad.astype(jnp.bfloat16)[None]
    summed, input_grad, out_shared = lax.optimization_barrier((summed, input_grad, out_shared))
    summed, out_summed = ring_scatter(
        [
            (summed.reshape(shares, -1, summed.shape[1]), "dp", jnp.float32, 2, False),
            (out_shared.reshape(seqs, -1, width), "seq", jnp.float32, 1, True),
        ],
        1,
    )
    grad_query = summed[:, :width]
    grad_key = summed[:, width:2 * width]
    grad_value = summed[:, 2 * width:]
    grad_out = out_summed.T
    return (input_grad, grad_query, grad_key, grad_value, grad_out)


def solution(mesh):
    return jax.shard_map(
        local,
        mesh=mesh,
        in_specs=(
            P("dp", "seq", None),
            P(None, "head"),
            P(None, "head"),
            P(None, "head"),
            P("head", None),
            P("dp", "seq", None),
        ),
        out_specs=(
            P("dp", "seq", "head"),
            P(("seq", "dp"), "head"),
            P(("seq", "dp"), "head"),
            P(("seq", "dp"), "head"),
            P("head", ("seq", "dp")),
        ),
        check_vma=False,
    )
```

```python
import functools
import math

import jax
import jax.numpy as jnp
from jax import lax
from jax.experimental import pallas as pl
from jax.experimental.pallas import tpu as pltpu
from jax.sharding import PartitionSpec as P

HEAD_DIM = 128
MESH = pl.DeviceIdType.MESH


def ring_scatter_kernel(jobs, produce, *refs):
    count = len(jobs)
    if produce:
        factors, refs = refs[:2 * produce], refs[2 * produce:]
        made, refs = refs[-1], refs[:-1]
        terms = (made,) + refs[:count - 1]
        outs, scratch = refs[count - 1:2 * count - 1], refs[2 * count - 1:]
        grads, weights = factors[:produce], factors[produce:]
    else:
        terms, outs, scratch = refs[:count], refs[count:2 * count], refs[2 * count:]
    barrier = pltpu.get_barrier_semaphore()
    places, greeted = [], 0
    for axis, n, _, direct in jobs:
        me = lax.axis_index(axis)
        right, left = lax.rem(me + 1, n), lax.rem(me + n - 1, n)
        places.append((me, right, left))
        offsets = range(1, n) if direct else (n - 1, 1)
        for offset in offsets:
            pl.semaphore_signal(
                barrier, inc=1, device_id={axis: lax.rem(me + offset, n)}, device_id_type=MESH
            )
        greeted += len(offsets)
    pl.semaphore_wait(barrier, greeted)

    def make_block(block):
        block_rows = made.shape[2]
        rows = pl.ds(pl.multiple_of(block * block_rows, block_rows), block_rows)
        total = None
        for grad, weight in zip(grads, weights):
            part = lax.dot_general(
                grad[...], weight[rows, :], (((1,), (1,)), ((), ())),
                preferred_element_type=jnp.float32,
            )
            total = part if total is None else total + part
        made[block] = total

    def direct_copy(job, offset):
        axis, n, _, _ = jobs[job]
        me = places[job][0]
        recv, send_sem, recv_sem = scratch[4 * job], scratch[4 * job + 2], scratch[4 * job + 3]
        peer = lax.rem(me + offset, n)
        return pltpu.make_async_remote_copy(
            src_ref=terms[job].at[peer],
            dst_ref=recv.at[me],
            send_sem=send_sem.at[offset],
            recv_sem=recv_sem.at[me],
            device_id={axis: peer},
            device_id_type=MESH,
        )

    for job, (axis, n, _, direct) in enumerate(jobs):
        if direct:
            for offset in range(1, n):
                direct_copy(job, offset).start()

    copies = [[[] for _ in range(2 * pieces)] for _, _, pieces, _ in jobs]
    for step in range(max(n for _, n, _, _ in jobs) - 1):
        for job, (axis, n, pieces, direct) in enumerate(jobs):
            if direct or step >= n - 1:
                continue
            me, right, left = places[job]
            if produce and job == 0 and 2 * (step + 1) <= n:
                make_block(lax.rem(me + n - (step + 1), n))
                if 2 * (step + 1) != n:
                    make_block(lax.rem(me + step + 1, n))
            recv, sendbuf, send_sem, recv_sem = scratch[4 * job:4 * job + 4]
            term_ref = terms[job]
            rows, half = outs[job].shape[0] // pieces, outs[job].shape[1] // 2
            for slot in range(2 * pieces):
                piece, way = divmod(slot, 2)
                dest, sign = ((right, -1), (left, 1))[way]
                block = lax.rem(me + n + sign * (step + 1), n)
                span = (pl.ds(piece * rows, rows), pl.ds(way * half, half))
                if step == 0:
                    src = term_ref.at[block, span[0], span[1]]
                else:
                    copies[job][slot][step - 1].wait_recv()
                    sendbuf[slot, step] = recv[slot, step - 1] + term_ref[block, span[0], span[1]]
                    src = sendbuf.at[slot, step]
                copy = pltpu.make_async_remote_copy(
                    src_ref=src,
                    dst_ref=recv.at[slot, step],
                    send_sem=send_sem.at[slot, step],
                    recv_sem=recv_sem.at[slot, step],
                    device_id={axis: dest},
                    device_id_type=MESH,
                )
                copy.start()
                copies[job][slot].append(copy)
    for job, (axis, n, pieces, direct) in enumerate(jobs):
        me = places[job][0]
        recv = scratch[4 * job]
        if direct:
            outs[job][...] = terms[job][me]
            for sender in range(n):
                @pl.when(sender != me)
                def _():
                    pltpu.make_async_remote_copy(
                        src_ref=terms[job].at[sender],
                        dst_ref=recv.at[sender],
                        send_sem=scratch[4 * job + 2].at[0],
                        recv_sem=scratch[4 * job + 3].at[sender],
                        device_id={axis: sender},
                        device_id_type=MESH,
                    ).wait_recv()
                    outs[job][...] += recv[sender]
            continue
        if produce and job == 0:
            make_block(me)
        rows, half = outs[job].shape[0] // pieces, outs[job].shape[1] // 2
        for slot in range(2 * pieces):
            piece, way = divmod(slot, 2)
            span = (pl.ds(piece * rows, rows), pl.ds(way * half, half))
            copies[job][slot][n - 2].wait_recv()
            outs[job][span[0], span[1]] = (
                recv[slot, n - 2] + terms[job][me, span[0], span[1]]
            ).astype(outs[job].dtype)
    for job, (axis, n, pieces, direct) in enumerate(jobs):
        if direct:
            for offset in range(1, n):
                direct_copy(job, offset).wait_send()
        for slot in range(2 * pieces):
            for copy in copies[job][slot]:
                copy.wait_send()


def ring_scatter(parts, channel, factors=None):
    jobs = tuple((axis, terms.shape[0], pieces, direct) for terms, axis, _, pieces, direct in parts)
    produce = len(factors[0]) if factors else 0
    scratch = []
    for terms, _, _, pieces, direct in parts:
        n, rows, width = terms.shape
        if direct:
            scratch += [
                pltpu.VMEM((n, rows, width), jnp.float32),
                pltpu.VMEM((8, 128), jnp.float32),
                pltpu.SemaphoreType.DMA((n,)),
                pltpu.SemaphoreType.DMA((n,)),
            ]
            continue
        scratch += [
            pltpu.VMEM((2 * pieces, n - 1, rows // pieces, width // 2), jnp.float32),
            pltpu.VMEM((2 * pieces, n - 1, rows // pieces, width // 2), jnp.float32),
            pltpu.SemaphoreType.DMA((2 * pieces, n - 1)),
            pltpu.SemaphoreType.DMA((2 * pieces, n - 1)),
        ]
    size = sum(math.prod(part[0].shape) for part in parts)
    operands = [part[0] for part in parts]
    if produce:
        scratch.append(pltpu.VMEM(parts[0][0].shape, jnp.float32))
        operands = list(factors[0]) + list(factors[1]) + operands[1:]
    return pl.pallas_call(
        functools.partial(ring_scatter_kernel, jobs, produce),
        out_shape=tuple(
            jax.ShapeDtypeStruct(part[0].shape[1:], part[2]) for part in parts
        ),
        in_specs=[pl.BlockSpec(memory_space=pltpu.VMEM)] * len(operands),
        out_specs=tuple(pl.BlockSpec(memory_space=pltpu.VMEM) for _ in parts),
        scratch_shapes=scratch,
        compiler_params=pltpu.CompilerParams(
            collective_id=channel, has_side_effects=True, vmem_limit_bytes=48 * 1024 * 1024
        ),
        cost_estimate=pl.CostEstimate(flops=2 * size, bytes_accessed=8 * size, transcendentals=0),
    )(*operands)


def exchange_kernel(n, axis, kv_ref, qg_ref, prefix_ref, suffix_ref,
                    pair_in, chip_sum, kv_in, qg_in, pair_sem, send_sem, recv_sem):
    me = lax.axis_index(axis)
    chips = n // 2
    chip, core = me // 2, lax.rem(me, 2)
    partner = me + 1 - 2 * core
    barrier = pltpu.get_barrier_semaphore()
    pl.semaphore_signal(barrier, inc=1, device_id={axis: partner}, device_id_type=MESH)
    for offset in range(1, chips):
        peer = lax.rem(chip + offset, chips) * 2 + core
        pl.semaphore_signal(barrier, inc=1, device_id={axis: peer}, device_id_type=MESH)
    pl.semaphore_wait(barrier, chips)

    swaps = []
    for kind, ref in enumerate((kv_ref, qg_ref)):
        swap = pltpu.make_async_remote_copy(
            src_ref=ref, dst_ref=pair_in.at[kind], send_sem=pair_sem.at[0, kind],
            recv_sem=pair_sem.at[1, kind], device_id={axis: partner}, device_id_type=MESH,
        )
        swap.start()
        swaps.append(swap)
    for swap in swaps:
        swap.wait_recv()
    chip_sum[0] = kv_ref[...] + pair_in[0]
    chip_sum[1] = qg_ref[...] + pair_in[1]

    def route(offset, later):
        peer = lax.rem(chip + offset, chips) * 2 + core
        kind = 0 if later else 1
        return pltpu.make_async_remote_copy(
            src_ref=chip_sum.at[kind],
            dst_ref=(kv_in if later else qg_in).at[chip],
            send_sem=send_sem.at[kind, offset],
            recv_sem=recv_sem.at[kind, chip],
            device_id={axis: peer},
            device_id_type=MESH,
        )

    for offset in range(1, chips):
        for later in (True, False):
            @pl.when((chip + offset < chips) == later)
            def _():
                route(offset, later).start()

    prefix_ref[...] = jnp.where(core == 1, pair_in[0], 0.0)
    suffix_ref[...] = jnp.where(core == 0, pair_in[1], 0.0)
    for sender in range(chips):
        @pl.when(sender < chip)
        def _():
            pltpu.make_async_remote_copy(
                src_ref=chip_sum.at[0], dst_ref=kv_in.at[sender], send_sem=send_sem.at[0, 0],
                recv_sem=recv_sem.at[0, sender], device_id={axis: sender * 2 + core},
                device_id_type=MESH,
            ).wait_recv()
            prefix_ref[...] += kv_in[sender]

        @pl.when(sender > chip)
        def _():
            pltpu.make_async_remote_copy(
                src_ref=chip_sum.at[1], dst_ref=qg_in.at[sender], send_sem=send_sem.at[1, 0],
                recv_sem=recv_sem.at[1, sender], device_id={axis: sender * 2 + core},
                device_id_type=MESH,
            ).wait_recv()
            suffix_ref[...] += qg_in[sender]

    for swap in swaps:
        swap.wait_send()
    for offset in range(1, chips):
        for later in (True, False):
            @pl.when((chip + offset < chips) == later)
            def _():
                route(offset, later).wait_send()


def exchange_states(kv_state, qg_state, axis):
    n = lax.axis_size(axis)
    chips = n // 2
    shape = kv_state.shape
    return pl.pallas_call(
        functools.partial(exchange_kernel, n, axis),
        out_shape=(jax.ShapeDtypeStruct(shape, jnp.float32),) * 2,
        in_specs=[pl.BlockSpec(memory_space=pltpu.VMEM)] * 2,
        out_specs=(pl.BlockSpec(memory_space=pltpu.VMEM),) * 2,
        scratch_shapes=[
            pltpu.VMEM((2,) + shape, jnp.float32),
            pltpu.VMEM((2,) + shape, jnp.float32),
            pltpu.VMEM((chips,) + shape, jnp.float32),
            pltpu.VMEM((chips,) + shape, jnp.float32),
            pltpu.SemaphoreType.DMA((2, 2)),
            pltpu.SemaphoreType.DMA((2, chips)),
            pltpu.SemaphoreType.DMA((2, chips)),
        ],
        compiler_params=pltpu.CompilerParams(collective_id=2, has_side_effects=True),
    )(kv_state, qg_state)


def local(layer_input, w_query, w_key, w_value, w_out, out_grad):
    num_rows = layer_input.shape[1]
    local_heads = w_query.shape[1] // HEAD_DIM
    width = local_heads * HEAD_DIM
    in_rows = layer_input[0]
    grad_rows = out_grad[0]

    def project(weight):
        result = jnp.dot(in_rows, weight, preferred_element_type=jnp.float32).astype(jnp.bfloat16)
        return result.reshape(num_rows, local_heads, HEAD_DIM)

    queries = project(w_query)
    key_rows = project(w_key)
    value_rows = project(w_value)
    row_start = lax.axis_index("seq") * num_rows
    positions = (row_start + jnp.arange(num_rows, dtype=jnp.int32)).astype(jnp.float32)
    pos_scale = 1.0 / jnp.sqrt(HEAD_DIM * (positions + 1.0))
    backward = jnp.einsum("td,kd->tk", grad_rows, w_out, preferred_element_type=jnp.float32)
    grad_in = (
        (backward * pos_scale[:, None])
        .astype(jnp.bfloat16)
        .reshape(num_rows, local_heads, HEAD_DIM)
    )
    kv_state = jnp.einsum("thd,the->hde", key_rows, value_rows, preferred_element_type=jnp.float32)
    qg_state = jnp.einsum("thd,the->hde", queries, grad_in, preferred_element_type=jnp.float32)
    prefix, suffix = exchange_states(kv_state, qg_state, "seq")
    prefix = prefix.astype(jnp.bfloat16)
    suffix = suffix.astype(jnp.bfloat16)
    causal = (jnp.arange(num_rows)[:, None] >= jnp.arange(num_rows)[None, :])[None]
    scores = jnp.einsum("thd,shd->hts", queries, key_rows, preferred_element_type=jnp.float32)
    scores_qk = jnp.where(causal, scores, 0.0).astype(jnp.bfloat16)
    scores_g = jnp.einsum("thd,shd->hts", grad_in, value_rows, preferred_element_type=jnp.float32)
    scores_gv = jnp.where(causal, scores_g, 0.0).astype(jnp.bfloat16)
    inner_sum = jnp.einsum(
        "hts,she->the", scores_qk, value_rows, preferred_element_type=jnp.float32
    )
    cross_sum = jnp.einsum("thd,hde->the", queries, prefix, preferred_element_type=jnp.float32)
    attention = (
        ((inner_sum + cross_sum) * pos_scale[:, None, None])
        .astype(jnp.bfloat16)
        .reshape(num_rows, width)
    )
    d_query = jnp.einsum("hts,shd->thd", scores_gv, key_rows, preferred_element_type=jnp.float32)
    d_query = d_query + jnp.einsum(
        "the,hde->thd", grad_in, prefix, preferred_element_type=jnp.float32
    )
    d_keys = jnp.einsum("hts,thd->shd", scores_gv, queries, preferred_element_type=jnp.float32)
    d_keys = d_keys + jnp.einsum(
        "she,hde->shd", value_rows, suffix, preferred_element_type=jnp.float32
    )
    d_values = jnp.einsum("hts,the->she", scores_qk, grad_in, preferred_element_type=jnp.float32)
    d_values = d_values + jnp.einsum(
        "shd,hde->she", key_rows, suffix, preferred_element_type=jnp.float32
    )
    d_query = d_query.astype(jnp.bfloat16).reshape(num_rows, width)
    d_keys = d_keys.astype(jnp.bfloat16).reshape(num_rows, width)
    d_values = d_values.astype(jnp.bfloat16).reshape(num_rows, width)
    groups = lax.axis_size("head")
    head_terms = jax.ShapeDtypeStruct((groups, num_rows, w_query.shape[0] // groups), jnp.float32)
    total_rows = lax.axis_size("seq") * lax.axis_size("dp") * num_rows
    grad_scale = jnp.float32(1.0) / jnp.sqrt(jnp.float32(total_rows))
    seqs, shares = lax.axis_size("seq"), lax.axis_size("dp")
    grads = jnp.concatenate([d_query, d_keys, d_values], axis=1)
    term_qkv = jnp.einsum("td,tk->dk", in_rows, grads, preferred_element_type=jnp.float32) * grad_scale
    grad_blocks = grad_rows.reshape(num_rows, seqs, shares, -1)
    term_out = jnp.einsum(
        "tspr,tk->psrk", grad_blocks, attention, preferred_element_type=jnp.float32
    ) * grad_scale
    term_out = term_out.reshape(shares, -1, width)
    factors = ((d_query, d_keys, d_values), (w_query, w_key, w_value))
    term_qkv, factors, term_out = lax.optimization_barrier((term_qkv, factors, term_out))
    summed = lax.psum_scatter(term_qkv, "seq", scatter_dimension=0, tiled=True)
    input_grad, out_shared = ring_scatter(
        [(head_terms, "head", jnp.float32, 4, False), (term_out, "dp", jnp.float32, 2, False)], 0,
        factors,
    )
    input_grad = input_grad.astype(jnp.bfloat16)[None]
    summed, input_grad, out_shared = lax.optimization_barrier((summed, input_grad, out_shared))
    summed, out_summed = ring_scatter(
        [
            (summed.reshape(shares, -1, summed.shape[1]), "dp", jnp.float32, 2, False),
            (out_shared.reshape(seqs, -1, width), "seq", jnp.float32, 1, True),
        ],
        1,
    )
    grad_query = summed[:, :width]
    grad_key = summed[:, width:2 * width]
    grad_value = summed[:, 2 * width:]
    grad_out = out_summed.T
    return (input_grad, grad_query, grad_key, grad_value, grad_out)


def solution(mesh):
    return jax.shard_map(
        local,
        mesh=mesh,
        in_specs=(
            P("dp", "seq", None),
            P(None, "head"),
            P(None, "head"),
            P(None, "head"),
            P("head", None),
            P("dp", "seq", None),
        ),
        out_specs=(
            P("dp", "seq", "head"),
            P(("seq", "dp"), "head"),
            P(("seq", "dp"), "head"),
            P(("seq", "dp"), "head"),
            P("head", ("seq", "dp")),
        ),
        check_vma=False,
    )
```

```python
import functools
import math

import jax
import jax.numpy as jnp
from jax import lax
from jax.experimental import pallas as pl
from jax.experimental.pallas import tpu as pltpu
from jax.sharding import PartitionSpec as P

HEAD_DIM = 128
MESH = pl.DeviceIdType.MESH


def ring_scatter_kernel(jobs, produce, *refs):
    count = len(jobs)
    if produce:
        factors, refs = refs[:2 * produce], refs[2 * produce:]
        made, refs = refs[-1], refs[:-1]
        terms = (made,) + refs[:count - 1]
        outs, scratch = refs[count - 1:2 * count - 1], refs[2 * count - 1:]
        grads, weights = factors[:produce], factors[produce:]
    else:
        terms, outs, scratch = refs[:count], refs[count:2 * count], refs[2 * count:]
    barrier = pltpu.get_barrier_semaphore()
    places, greeted = [], 0
    for axis, n, _, direct in jobs:
        me = lax.axis_index(axis)
        right, left = lax.rem(me + 1, n), lax.rem(me + n - 1, n)
        places.append((me, right, left))
        offsets = range(1, n) if direct else (n - 1, 1)
        for offset in offsets:
            pl.semaphore_signal(
                barrier, inc=1, device_id={axis: lax.rem(me + offset, n)}, device_id_type=MESH
            )
        greeted += len(offsets)

    def make_block(block):
        block_rows = made.shape[2]
        rows = pl.ds(pl.multiple_of(block * block_rows, block_rows), block_rows)
        total = None
        for grad, weight in zip(grads, weights):
            part = lax.dot_general(
                grad[...], weight[rows, :], (((1,), (1,)), ((), ())),
                preferred_element_type=jnp.float32,
            )
            total = part if total is None else total + part
        made[block] = total

    if produce:
        me, n = places[0][0], jobs[0][1]
        make_block(lax.rem(me + n - 1, n))
        make_block(lax.rem(me + 1, n))
    pl.semaphore_wait(barrier, greeted)

    def direct_copy(job, offset):
        axis, n, _, _ = jobs[job]
        me = places[job][0]
        recv, send_sem, recv_sem = scratch[4 * job], scratch[4 * job + 2], scratch[4 * job + 3]
        peer = lax.rem(me + offset, n)
        return pltpu.make_async_remote_copy(
            src_ref=terms[job].at[peer],
            dst_ref=recv.at[me],
            send_sem=send_sem.at[offset],
            recv_sem=recv_sem.at[me],
            device_id={axis: peer},
            device_id_type=MESH,
        )

    for job, (axis, n, _, direct) in enumerate(jobs):
        if direct:
            for offset in range(1, n):
                direct_copy(job, offset).start()

    copies = [[[] for _ in range(2 * pieces)] for _, _, pieces, _ in jobs]
    for step in range(max(n for _, n, _, _ in jobs) - 1):
        for job, (axis, n, pieces, direct) in enumerate(jobs):
            if direct or step >= n - 1:
                continue
            me, right, left = places[job]
            if produce and job == 0 and 0 < step and 2 * (step + 1) <= n:
                make_block(lax.rem(me + n - (step + 1), n))
                if 2 * (step + 1) != n:
                    make_block(lax.rem(me + step + 1, n))
            recv, sendbuf, send_sem, recv_sem = scratch[4 * job:4 * job + 4]
            term_ref = terms[job]
            rows, half = outs[job].shape[0] // pieces, outs[job].shape[1] // 2
            for slot in range(2 * pieces):
                piece, way = divmod(slot, 2)
                dest, sign = ((right, -1), (left, 1))[way]
                block = lax.rem(me + n + sign * (step + 1), n)
                span = (pl.ds(piece * rows, rows), pl.ds(way * half, half))
                if step == 0:
                    src = term_ref.at[block, span[0], span[1]]
                else:
                    copies[job][slot][step - 1].wait_recv()
                    sendbuf[slot, step] = recv[slot, step - 1] + term_ref[block, span[0], span[1]]
                    src = sendbuf.at[slot, step]
                copy = pltpu.make_async_remote_copy(
                    src_ref=src,
                    dst_ref=recv.at[slot, step],
                    send_sem=send_sem.at[slot, step],
                    recv_sem=recv_sem.at[slot, step],
                    device_id={axis: dest},
                    device_id_type=MESH,
                )
                copy.start()
                copies[job][slot].append(copy)
    for job, (axis, n, pieces, direct) in enumerate(jobs):
        me = places[job][0]
        recv = scratch[4 * job]
        if direct:
            outs[job][...] = terms[job][me]
            for sender in range(n):
                @pl.when(sender != me)
                def _():
                    pltpu.make_async_remote_copy(
                        src_ref=terms[job].at[sender],
                        dst_ref=recv.at[sender],
                        send_sem=scratch[4 * job + 2].at[0],
                        recv_sem=scratch[4 * job + 3].at[sender],
                        device_id={axis: sender},
                        device_id_type=MESH,
                    ).wait_recv()
                    outs[job][...] += recv[sender]
            continue
        if produce and job == 0:
            make_block(me)
        rows, half = outs[job].shape[0] // pieces, outs[job].shape[1] // 2
        for slot in range(2 * pieces):
            piece, way = divmod(slot, 2)
            span = (pl.ds(piece * rows, rows), pl.ds(way * half, half))
            copies[job][slot][n - 2].wait_recv()
            outs[job][span[0], span[1]] = (
                recv[slot, n - 2] + terms[job][me, span[0], span[1]]
            ).astype(outs[job].dtype)
    for job, (axis, n, pieces, direct) in enumerate(jobs):
        if direct:
            for offset in range(1, n):
                direct_copy(job, offset).wait_send()
        for slot in range(2 * pieces):
            for copy in copies[job][slot]:
                copy.wait_send()


def ring_scatter(parts, channel, factors=None):
    jobs = tuple((axis, terms.shape[0], pieces, direct) for terms, axis, _, pieces, direct in parts)
    produce = len(factors[0]) if factors else 0
    scratch = []
    for terms, _, _, pieces, direct in parts:
        n, rows, width = terms.shape
        if direct:
            scratch += [
                pltpu.VMEM((n, rows, width), jnp.float32),
                pltpu.VMEM((8, 128), jnp.float32),
                pltpu.SemaphoreType.DMA((n,)),
                pltpu.SemaphoreType.DMA((n,)),
            ]
            continue
        scratch += [
            pltpu.VMEM((2 * pieces, n - 1, rows // pieces, width // 2), jnp.float32),
            pltpu.VMEM((2 * pieces, n - 1, rows // pieces, width // 2), jnp.float32),
            pltpu.SemaphoreType.DMA((2 * pieces, n - 1)),
            pltpu.SemaphoreType.DMA((2 * pieces, n - 1)),
        ]
    size = sum(math.prod(part[0].shape) for part in parts)
    operands = [part[0] for part in parts]
    if produce:
        scratch.append(pltpu.VMEM(parts[0][0].shape, jnp.float32))
        operands = list(factors[0]) + list(factors[1]) + operands[1:]
    return pl.pallas_call(
        functools.partial(ring_scatter_kernel, jobs, produce),
        out_shape=tuple(
            jax.ShapeDtypeStruct(part[0].shape[1:], part[2]) for part in parts
        ),
        in_specs=[pl.BlockSpec(memory_space=pltpu.VMEM)] * len(operands),
        out_specs=tuple(pl.BlockSpec(memory_space=pltpu.VMEM) for _ in parts),
        scratch_shapes=scratch,
        compiler_params=pltpu.CompilerParams(
            collective_id=channel, has_side_effects=True, vmem_limit_bytes=48 * 1024 * 1024
        ),
        cost_estimate=pl.CostEstimate(flops=2 * size, bytes_accessed=8 * size, transcendentals=0),
    )(*operands)


def exchange_kernel(n, axis, kv_ref, qg_ref, prefix_ref, suffix_ref,
                    pair_in, chip_sum, kv_in, qg_in, pair_sem, send_sem, recv_sem):
    me = lax.axis_index(axis)
    chips = n // 2
    chip, core = me // 2, lax.rem(me, 2)
    partner = me + 1 - 2 * core
    barrier = pltpu.get_barrier_semaphore()
    pl.semaphore_signal(barrier, inc=1, device_id={axis: partner}, device_id_type=MESH)
    for offset in range(1, chips):
        peer = lax.rem(chip + offset, chips) * 2 + core
        pl.semaphore_signal(barrier, inc=1, device_id={axis: peer}, device_id_type=MESH)
    pl.semaphore_wait(barrier, chips)

    swaps = []
    for kind, ref in enumerate((kv_ref, qg_ref)):
        swap = pltpu.make_async_remote_copy(
            src_ref=ref, dst_ref=pair_in.at[kind], send_sem=pair_sem.at[0, kind],
            recv_sem=pair_sem.at[1, kind], device_id={axis: partner}, device_id_type=MESH,
        )
        swap.start()
        swaps.append(swap)
    for swap in swaps:
        swap.wait_recv()
    chip_sum[0] = kv_ref[...] + pair_in[0]
    chip_sum[1] = qg_ref[...] + pair_in[1]

    def route(offset, later):
        peer = lax.rem(chip + offset, chips) * 2 + core
        kind = 0 if later else 1
        return pltpu.make_async_remote_copy(
            src_ref=chip_sum.at[kind],
            dst_ref=(kv_in if later else qg_in).at[chip],
            send_sem=send_sem.at[kind, offset],
            recv_sem=recv_sem.at[kind, chip],
            device_id={axis: peer},
            device_id_type=MESH,
        )

    for offset in range(1, chips):
        for later in (True, False):
            @pl.when((chip + offset < chips) == later)
            def _():
                route(offset, later).start()

    prefix_ref[...] = jnp.where(core == 1, pair_in[0], 0.0)
    suffix_ref[...] = jnp.where(core == 0, pair_in[1], 0.0)
    for sender in range(chips):
        @pl.when(sender < chip)
        def _():
            pltpu.make_async_remote_copy(
                src_ref=chip_sum.at[0], dst_ref=kv_in.at[sender], send_sem=send_sem.at[0, 0],
                recv_sem=recv_sem.at[0, sender], device_id={axis: sender * 2 + core},
                device_id_type=MESH,
            ).wait_recv()
            prefix_ref[...] += kv_in[sender]

        @pl.when(sender > chip)
        def _():
            pltpu.make_async_remote_copy(
                src_ref=chip_sum.at[1], dst_ref=qg_in.at[sender], send_sem=send_sem.at[1, 0],
                recv_sem=recv_sem.at[1, sender], device_id={axis: sender * 2 + core},
                device_id_type=MESH,
            ).wait_recv()
            suffix_ref[...] += qg_in[sender]

    for swap in swaps:
        swap.wait_send()
    for offset in range(1, chips):
        for later in (True, False):
            @pl.when((chip + offset < chips) == later)
            def _():
                route(offset, later).wait_send()


def exchange_states(kv_state, qg_state, axis):
    n = lax.axis_size(axis)
    chips = n // 2
    shape = kv_state.shape
    return pl.pallas_call(
        functools.partial(exchange_kernel, n, axis),
        out_shape=(jax.ShapeDtypeStruct(shape, jnp.float32),) * 2,
        in_specs=[pl.BlockSpec(memory_space=pltpu.VMEM)] * 2,
        out_specs=(pl.BlockSpec(memory_space=pltpu.VMEM),) * 2,
        scratch_shapes=[
            pltpu.VMEM((2,) + shape, jnp.float32),
            pltpu.VMEM((2,) + shape, jnp.float32),
            pltpu.VMEM((chips,) + shape, jnp.float32),
            pltpu.VMEM((chips,) + shape, jnp.float32),
            pltpu.SemaphoreType.DMA((2, 2)),
            pltpu.SemaphoreType.DMA((2, chips)),
            pltpu.SemaphoreType.DMA((2, chips)),
        ],
        compiler_params=pltpu.CompilerParams(collective_id=2, has_side_effects=True),
    )(kv_state, qg_state)


def local(layer_input, w_query, w_key, w_value, w_out, out_grad):
    num_rows = layer_input.shape[1]
    local_heads = w_query.shape[1] // HEAD_DIM
    width = local_heads * HEAD_DIM
    in_rows = layer_input[0]
    grad_rows = out_grad[0]

    def project(weight):
        result = jnp.dot(in_rows, weight, preferred_element_type=jnp.float32).astype(jnp.bfloat16)
        return result.reshape(num_rows, local_heads, HEAD_DIM)

    queries = project(w_query)
    key_rows = project(w_key)
    value_rows = project(w_value)
    row_start = lax.axis_index("seq") * num_rows
    positions = (row_start + jnp.arange(num_rows, dtype=jnp.int32)).astype(jnp.float32)
    pos_scale = 1.0 / jnp.sqrt(HEAD_DIM * (positions + 1.0))
    backward = jnp.einsum("td,kd->tk", grad_rows, w_out, preferred_element_type=jnp.float32)
    grad_in = (
        (backward * pos_scale[:, None])
        .astype(jnp.bfloat16)
        .reshape(num_rows, local_heads, HEAD_DIM)
    )
    kv_state = jnp.einsum("thd,the->hde", key_rows, value_rows, preferred_element_type=jnp.float32)
    qg_state = jnp.einsum("thd,the->hde", queries, grad_in, preferred_element_type=jnp.float32)
    prefix, suffix = exchange_states(kv_state, qg_state, "seq")
    prefix = prefix.astype(jnp.bfloat16)
    suffix = suffix.astype(jnp.bfloat16)
    causal = (jnp.arange(num_rows)[:, None] >= jnp.arange(num_rows)[None, :])[None]
    scores = jnp.einsum("thd,shd->hts", queries, key_rows, preferred_element_type=jnp.float32)
    scores_qk = jnp.where(causal, scores, 0.0).astype(jnp.bfloat16)
    scores_g = jnp.einsum("thd,shd->hts", grad_in, value_rows, preferred_element_type=jnp.float32)
    scores_gv = jnp.where(causal, scores_g, 0.0).astype(jnp.bfloat16)
    inner_sum = jnp.einsum(
        "hts,she->the", scores_qk, value_rows, preferred_element_type=jnp.float32
    )
    cross_sum = jnp.einsum("thd,hde->the", queries, prefix, preferred_element_type=jnp.float32)
    attention = (
        ((inner_sum + cross_sum) * pos_scale[:, None, None])
        .astype(jnp.bfloat16)
        .reshape(num_rows, width)
    )
    d_query = jnp.einsum("hts,shd->thd", scores_gv, key_rows, preferred_element_type=jnp.float32)
    d_query = d_query + jnp.einsum(
        "the,hde->thd", grad_in, prefix, preferred_element_type=jnp.float32
    )
    d_keys = jnp.einsum("hts,thd->shd", scores_gv, queries, preferred_element_type=jnp.float32)
    d_keys = d_keys + jnp.einsum(
        "she,hde->shd", value_rows, suffix, preferred_element_type=jnp.float32
    )
    d_values = jnp.einsum("hts,the->she", scores_qk, grad_in, preferred_element_type=jnp.float32)
    d_values = d_values + jnp.einsum(
        "shd,hde->she", key_rows, suffix, preferred_element_type=jnp.float32
    )
    d_query = d_query.astype(jnp.bfloat16).reshape(num_rows, width)
    d_keys = d_keys.astype(jnp.bfloat16).reshape(num_rows, width)
    d_values = d_values.astype(jnp.bfloat16).reshape(num_rows, width)
    groups = lax.axis_size("head")
    head_terms = jax.ShapeDtypeStruct((groups, num_rows, w_query.shape[0] // groups), jnp.float32)
    total_rows = lax.axis_size("seq") * lax.axis_size("dp") * num_rows
    grad_scale = jnp.float32(1.0) / jnp.sqrt(jnp.float32(total_rows))
    seqs, shares = lax.axis_size("seq"), lax.axis_size("dp")
    grads = jnp.concatenate([d_query, d_keys, d_values], axis=1)
    term_qkv = jnp.einsum("td,tk->dk", in_rows, grads, preferred_element_type=jnp.float32) * grad_scale
    grad_blocks = grad_rows.reshape(num_rows, seqs, shares, -1)
    term_out = jnp.einsum(
        "tspr,tk->psrk", grad_blocks, attention, preferred_element_type=jnp.float32
    ) * grad_scale
    term_out = term_out.reshape(shares, -1, width)
    factors = ((d_query, d_keys, d_values), (w_query, w_key, w_value))
    term_qkv, factors, term_out = lax.optimization_barrier((term_qkv, factors, term_out))
    summed = lax.psum_scatter(term_qkv, "seq", scatter_dimension=0, tiled=True)
    input_grad, out_shared = ring_scatter(
        [(head_terms, "head", jnp.float32, 4, False), (term_out, "dp", jnp.float32, 2, False)], 0,
        factors,
    )
    input_grad = input_grad.astype(jnp.bfloat16)[None]
    summed, input_grad, out_shared = lax.optimization_barrier((summed, input_grad, out_shared))
    summed, out_summed = ring_scatter(
        [
            (summed.reshape(shares, -1, summed.shape[1]), "dp", jnp.float32, 2, False),
            (out_shared.reshape(seqs, -1, width), "seq", jnp.float32, 1, True),
        ],
        1,
    )
    grad_query = summed[:, :width]
    grad_key = summed[:, width:2 * width]
    grad_value = summed[:, 2 * width:]
    grad_out = out_summed.T
    return (input_grad, grad_query, grad_key, grad_value, grad_out)


def solution(mesh):
    return jax.shard_map(
        local,
        mesh=mesh,
        in_specs=(
            P("dp", "seq", None),
            P(None, "head"),
            P(None, "head"),
            P(None, "head"),
            P("head", None),
            P("dp", "seq", None),
        ),
        out_specs=(
            P("dp", "seq", "head"),
            P(("seq", "dp"), "head"),
            P(("seq", "dp"), "head"),
            P(("seq", "dp"), "head"),
            P("head", ("seq", "dp")),
        ),
        check_vma=False,
    )
```

```python
import functools
import math

import jax
import jax.numpy as jnp
from jax import lax
from jax.experimental import pallas as pl
from jax.experimental.pallas import tpu as pltpu
from jax.sharding import PartitionSpec as P

HEAD_DIM = 128
MESH = pl.DeviceIdType.MESH


def ring_scatter_kernel(jobs, produce, *refs):
    count = len(jobs)
    if produce:
        factors, refs = refs[:2 * produce], refs[2 * produce:]
        made, refs = refs[-1], refs[:-1]
        terms = (made,) + refs[:count - 1]
        outs, scratch = refs[count - 1:2 * count - 1], refs[2 * count - 1:]
        grads, weights = factors[:produce], factors[produce:]
    else:
        terms, outs, scratch = refs[:count], refs[count:2 * count], refs[2 * count:]
    barrier = pltpu.get_barrier_semaphore()
    places, greeted = [], 0
    for axis, n, _, direct in jobs:
        me = lax.axis_index(axis)
        right, left = lax.rem(me + 1, n), lax.rem(me + n - 1, n)
        places.append((me, right, left))
        offsets = range(1, n) if direct else (n - 1, 1)
        for offset in offsets:
            pl.semaphore_signal(
                barrier, inc=1, device_id={axis: lax.rem(me + offset, n)}, device_id_type=MESH
            )
        greeted += len(offsets)

    def make_block(block):
        block_rows = made.shape[2]
        rows = pl.ds(pl.multiple_of(block * block_rows, block_rows), block_rows)
        total = None
        for grad, weight in zip(grads, weights):
            part = lax.dot_general(
                grad[...], weight[rows, :], (((1,), (1,)), ((), ())),
                preferred_element_type=jnp.float32,
            )
            total = part if total is None else total + part
        made[block] = total

    if produce:
        me, n = places[0][0], jobs[0][1]
        make_block(lax.rem(me + n - 1, n))
        make_block(lax.rem(me + 1, n))
    pl.semaphore_wait(barrier, greeted)

    def direct_copy(job, offset):
        axis, n, _, _ = jobs[job]
        me = places[job][0]
        recv, send_sem, recv_sem = scratch[4 * job], scratch[4 * job + 2], scratch[4 * job + 3]
        peer = lax.rem(me + offset, n)
        return pltpu.make_async_remote_copy(
            src_ref=terms[job].at[peer],
            dst_ref=recv.at[me],
            send_sem=send_sem.at[offset],
            recv_sem=recv_sem.at[me],
            device_id={axis: peer},
            device_id_type=MESH,
        )

    for job, (axis, n, _, direct) in enumerate(jobs):
        if direct:
            for offset in range(1, n):
                direct_copy(job, offset).start()

    copies = [[[] for _ in range(2 * pieces)] for _, _, pieces, _ in jobs]
    for step in range(max(n for _, n, _, _ in jobs) - 1):
        for job, (axis, n, pieces, direct) in enumerate(jobs):
            if direct or step >= n - 1:
                continue
            me, right, left = places[job]
            if produce and job == 0 and 0 < step and 2 * (step + 1) <= n:
                make_block(lax.rem(me + n - (step + 1), n))
                if 2 * (step + 1) != n:
                    make_block(lax.rem(me + step + 1, n))
            recv, sendbuf, send_sem, recv_sem = scratch[4 * job:4 * job + 4]
            term_ref = terms[job]
            rows, half = outs[job].shape[0] // pieces, outs[job].shape[1] // 2
            for slot in range(2 * pieces):
                piece, way = divmod(slot, 2)
                dest, sign = ((right, -1), (left, 1))[way]
                block = lax.rem(me + n + sign * (step + 1), n)
                span = (pl.ds(piece * rows, rows), pl.ds(way * half, half))
                if step == 0:
                    src = term_ref.at[block, span[0], span[1]]
                else:
                    copies[job][slot][step - 1].wait_recv()
                    sendbuf[slot, step] = recv[slot, step - 1] + term_ref[block, span[0], span[1]]
                    src = sendbuf.at[slot, step]
                copy = pltpu.make_async_remote_copy(
                    src_ref=src,
                    dst_ref=recv.at[slot, step],
                    send_sem=send_sem.at[slot, step],
                    recv_sem=recv_sem.at[slot, step],
                    device_id={axis: dest},
                    device_id_type=MESH,
                )
                copy.start()
                copies[job][slot].append(copy)
    for job, (axis, n, pieces, direct) in enumerate(jobs):
        me = places[job][0]
        recv = scratch[4 * job]
        if direct:
            outs[job][...] = terms[job][me]
            for sender in range(n):
                @pl.when(sender != me)
                def _():
                    pltpu.make_async_remote_copy(
                        src_ref=terms[job].at[sender],
                        dst_ref=recv.at[sender],
                        send_sem=scratch[4 * job + 2].at[0],
                        recv_sem=scratch[4 * job + 3].at[sender],
                        device_id={axis: sender},
                        device_id_type=MESH,
                    ).wait_recv()
                    outs[job][...] += recv[sender]
            continue
        if produce and job == 0:
            make_block(me)
        rows, half = outs[job].shape[0] // pieces, outs[job].shape[1] // 2
        for slot in range(2 * pieces):
            piece, way = divmod(slot, 2)
            span = (pl.ds(piece * rows, rows), pl.ds(way * half, half))
            copies[job][slot][n - 2].wait_recv()
            outs[job][span[0], span[1]] = (
                recv[slot, n - 2] + terms[job][me, span[0], span[1]]
            ).astype(outs[job].dtype)
    for job, (axis, n, pieces, direct) in enumerate(jobs):
        if direct:
            for offset in range(1, n):
                direct_copy(job, offset).wait_send()
        for slot in range(2 * pieces):
            for copy in copies[job][slot]:
                copy.wait_send()


def ring_scatter(parts, channel, factors=None):
    jobs = tuple((axis, terms.shape[0], pieces, direct) for terms, axis, _, pieces, direct in parts)
    produce = len(factors[0]) if factors else 0
    scratch = []
    for terms, _, _, pieces, direct in parts:
        n, rows, width = terms.shape
        if direct:
            scratch += [
                pltpu.VMEM((n, rows, width), jnp.float32),
                pltpu.VMEM((8, 128), jnp.float32),
                pltpu.SemaphoreType.DMA((n,)),
                pltpu.SemaphoreType.DMA((n,)),
            ]
            continue
        scratch += [
            pltpu.VMEM((2 * pieces, n - 1, rows // pieces, width // 2), jnp.float32),
            pltpu.VMEM((2 * pieces, n - 1, rows // pieces, width // 2), jnp.float32),
            pltpu.SemaphoreType.DMA((2 * pieces, n - 1)),
            pltpu.SemaphoreType.DMA((2 * pieces, n - 1)),
        ]
    size = sum(math.prod(part[0].shape) for part in parts)
    operands = [part[0] for part in parts]
    if produce:
        scratch.append(pltpu.VMEM(parts[0][0].shape, jnp.float32))
        operands = list(factors[0]) + list(factors[1]) + operands[1:]
    return pl.pallas_call(
        functools.partial(ring_scatter_kernel, jobs, produce),
        out_shape=tuple(
            jax.ShapeDtypeStruct(part[0].shape[1:], part[2]) for part in parts
        ),
        in_specs=[pl.BlockSpec(memory_space=pltpu.VMEM)] * len(operands),
        out_specs=tuple(pl.BlockSpec(memory_space=pltpu.VMEM) for _ in parts),
        scratch_shapes=scratch,
        compiler_params=pltpu.CompilerParams(
            collective_id=channel, has_side_effects=True, vmem_limit_bytes=48 * 1024 * 1024
        ),
        cost_estimate=pl.CostEstimate(flops=2 * size, bytes_accessed=8 * size, transcendentals=0),
    )(*operands)


def exchange_kernel(n, axis, kv_ref, qg_ref, prefix_ref, suffix_ref,
                    pair_in, chip_sum, kv_in, qg_in, pair_sem, send_sem, recv_sem):
    me = lax.axis_index(axis)
    chips = n // 2
    chip, core = me // 2, lax.rem(me, 2)
    partner = me + 1 - 2 * core
    barrier = pltpu.get_barrier_semaphore()
    pl.semaphore_signal(barrier, inc=1, device_id={axis: partner}, device_id_type=MESH)
    for offset in range(1, chips):
        peer = lax.rem(chip + offset, chips) * 2 + core
        pl.semaphore_signal(barrier, inc=1, device_id={axis: peer}, device_id_type=MESH)
    pl.semaphore_wait(barrier, chips)

    swaps = []
    for kind, ref in enumerate((kv_ref, qg_ref)):
        swap = pltpu.make_async_remote_copy(
            src_ref=ref, dst_ref=pair_in.at[kind], send_sem=pair_sem.at[0, kind],
            recv_sem=pair_sem.at[1, kind], device_id={axis: partner}, device_id_type=MESH,
        )
        swap.start()
        swaps.append(swap)
    for swap in swaps:
        swap.wait_recv()
    chip_sum[0] = kv_ref[...] + pair_in[0]
    chip_sum[1] = qg_ref[...] + pair_in[1]

    def route(offset, later):
        peer = lax.rem(chip + offset, chips) * 2 + core
        kind = 0 if later else 1
        return pltpu.make_async_remote_copy(
            src_ref=chip_sum.at[kind],
            dst_ref=(kv_in if later else qg_in).at[chip],
            send_sem=send_sem.at[kind, offset],
            recv_sem=recv_sem.at[kind, chip],
            device_id={axis: peer},
            device_id_type=MESH,
        )

    for offset in range(1, chips):
        for later in (True, False):
            @pl.when((chip + offset < chips) == later)
            def _():
                route(offset, later).start()

    prefix_ref[...] = jnp.where(core == 1, pair_in[0], 0.0)
    suffix_ref[...] = jnp.where(core == 0, pair_in[1], 0.0)
    for sender in range(chips):
        @pl.when(sender < chip)
        def _():
            pltpu.make_async_remote_copy(
                src_ref=chip_sum.at[0], dst_ref=kv_in.at[sender], send_sem=send_sem.at[0, 0],
                recv_sem=recv_sem.at[0, sender], device_id={axis: sender * 2 + core},
                device_id_type=MESH,
            ).wait_recv()
            prefix_ref[...] += kv_in[sender]

        @pl.when(sender > chip)
        def _():
            pltpu.make_async_remote_copy(
                src_ref=chip_sum.at[1], dst_ref=qg_in.at[sender], send_sem=send_sem.at[1, 0],
                recv_sem=recv_sem.at[1, sender], device_id={axis: sender * 2 + core},
                device_id_type=MESH,
            ).wait_recv()
            suffix_ref[...] += qg_in[sender]

    for swap in swaps:
        swap.wait_send()
    for offset in range(1, chips):
        for later in (True, False):
            @pl.when((chip + offset < chips) == later)
            def _():
                route(offset, later).wait_send()


def exchange_states(kv_state, qg_state, axis):
    n = lax.axis_size(axis)
    chips = n // 2
    shape = kv_state.shape
    return pl.pallas_call(
        functools.partial(exchange_kernel, n, axis),
        out_shape=(jax.ShapeDtypeStruct(shape, jnp.float32),) * 2,
        in_specs=[pl.BlockSpec(memory_space=pltpu.VMEM)] * 2,
        out_specs=(pl.BlockSpec(memory_space=pltpu.VMEM),) * 2,
        scratch_shapes=[
            pltpu.VMEM((2,) + shape, jnp.float32),
            pltpu.VMEM((2,) + shape, jnp.float32),
            pltpu.VMEM((chips,) + shape, jnp.float32),
            pltpu.VMEM((chips,) + shape, jnp.float32),
            pltpu.SemaphoreType.DMA((2, 2)),
            pltpu.SemaphoreType.DMA((2, chips)),
            pltpu.SemaphoreType.DMA((2, chips)),
        ],
        compiler_params=pltpu.CompilerParams(collective_id=2, has_side_effects=True),
    )(kv_state, qg_state)


def local(layer_input, w_query, w_key, w_value, w_out, out_grad):
    num_rows = layer_input.shape[1]
    local_heads = w_query.shape[1] // HEAD_DIM
    width = local_heads * HEAD_DIM
    in_rows = layer_input[0]
    grad_rows = out_grad[0]

    def project(weight):
        result = jnp.dot(in_rows, weight, preferred_element_type=jnp.float32).astype(jnp.bfloat16)
        return result.reshape(num_rows, local_heads, HEAD_DIM)

    queries = project(w_query)
    key_rows = project(w_key)
    value_rows = project(w_value)
    row_start = lax.axis_index("seq") * num_rows
    positions = (row_start + jnp.arange(num_rows, dtype=jnp.int32)).astype(jnp.float32)
    pos_scale = 1.0 / jnp.sqrt(HEAD_DIM * (positions + 1.0))
    backward = jnp.einsum("td,kd->tk", grad_rows, w_out, preferred_element_type=jnp.float32)
    grad_in = (
        (backward * pos_scale[:, None])
        .astype(jnp.bfloat16)
        .reshape(num_rows, local_heads, HEAD_DIM)
    )
    kv_state = jnp.einsum("thd,the->hde", key_rows, value_rows, preferred_element_type=jnp.float32)
    qg_state = jnp.einsum("thd,the->hde", queries, grad_in, preferred_element_type=jnp.float32)
    prefix, suffix = exchange_states(kv_state, qg_state, "seq")
    prefix = prefix.astype(jnp.bfloat16)
    suffix = suffix.astype(jnp.bfloat16)
    causal = (jnp.arange(num_rows)[:, None] >= jnp.arange(num_rows)[None, :])[None]
    scores = jnp.einsum("thd,shd->hts", queries, key_rows, preferred_element_type=jnp.float32)
    scores_qk = jnp.where(causal, scores, 0.0).astype(jnp.bfloat16)
    scores_g = jnp.einsum("thd,shd->hts", grad_in, value_rows, preferred_element_type=jnp.float32)
    scores_gv = jnp.where(causal, scores_g, 0.0).astype(jnp.bfloat16)
    inner_sum = jnp.einsum(
        "hts,she->the", scores_qk, value_rows, preferred_element_type=jnp.float32
    )
    cross_sum = jnp.einsum("thd,hde->the", queries, prefix, preferred_element_type=jnp.float32)
    attention = (
        ((inner_sum + cross_sum) * pos_scale[:, None, None])
        .astype(jnp.bfloat16)
        .reshape(num_rows, width)
    )
    d_query = jnp.einsum("hts,shd->thd", scores_gv, key_rows, preferred_element_type=jnp.float32)
    d_query = d_query + jnp.einsum(
        "the,hde->thd", grad_in, prefix, preferred_element_type=jnp.float32
    )
    d_keys = jnp.einsum("hts,thd->shd", scores_gv, queries, preferred_element_type=jnp.float32)
    d_keys = d_keys + jnp.einsum(
        "she,hde->shd", value_rows, suffix, preferred_element_type=jnp.float32
    )
    d_values = jnp.einsum("hts,the->she", scores_qk, grad_in, preferred_element_type=jnp.float32)
    d_values = d_values + jnp.einsum(
        "shd,hde->she", key_rows, suffix, preferred_element_type=jnp.float32
    )
    d_query = d_query.astype(jnp.bfloat16).reshape(num_rows, width)
    d_keys = d_keys.astype(jnp.bfloat16).reshape(num_rows, width)
    d_values = d_values.astype(jnp.bfloat16).reshape(num_rows, width)
    groups = lax.axis_size("head")
    head_terms = jax.ShapeDtypeStruct((groups, num_rows, w_query.shape[0] // groups), jnp.float32)
    total_rows = lax.axis_size("seq") * lax.axis_size("dp") * num_rows
    grad_scale = jnp.float32(1.0) / jnp.sqrt(jnp.float32(total_rows))
    seqs, shares = lax.axis_size("seq"), lax.axis_size("dp")
    grads = jnp.concatenate([d_query, d_keys, d_values], axis=1)
    term_qkv = jnp.einsum("td,tk->dk", in_rows, grads, preferred_element_type=jnp.float32) * grad_scale
    grad_blocks = grad_rows.reshape(num_rows, seqs, shares, -1)
    term_out = jnp.einsum(
        "tspr,tk->psrk", grad_blocks, attention, preferred_element_type=jnp.float32
    ) * grad_scale
    term_out = term_out.reshape(shares, -1, width)
    factors = ((d_query, d_keys, d_values), (w_query, w_key, w_value))
    term_qkv, factors, term_out = lax.optimization_barrier((term_qkv, factors, term_out))
    summed = lax.psum_scatter(term_qkv, "seq", scatter_dimension=0, tiled=True)
    input_grad, out_shared = ring_scatter(
        [(head_terms, "head", jnp.float32, 4, False), (term_out, "dp", jnp.float32, 2, False)], 0,
        factors,
    )
    input_grad = input_grad.astype(jnp.bfloat16)[None]
    summed, input_grad, out_shared = lax.optimization_barrier((summed, input_grad, out_shared))
    summed, out_summed = ring_scatter(
        [
            (summed.reshape(shares, -1, summed.shape[1]), "dp", jnp.float32, 1, False),
            (out_shared.reshape(seqs, -1, width), "seq", jnp.float32, 1, True),
        ],
        1,
    )
    grad_query = summed[:, :width]
    grad_key = summed[:, width:2 * width]
    grad_value = summed[:, 2 * width:]
    grad_out = out_summed.T
    return (input_grad, grad_query, grad_key, grad_value, grad_out)


def solution(mesh):
    return jax.shard_map(
        local,
        mesh=mesh,
        in_specs=(
            P("dp", "seq", None),
            P(None, "head"),
            P(None, "head"),
            P(None, "head"),
            P("head", None),
            P("dp", "seq", None),
        ),
        out_specs=(
            P("dp", "seq", "head"),
            P(("seq", "dp"), "head"),
            P(("seq", "dp"), "head"),
            P(("seq", "dp"), "head"),
            P("head", ("seq", "dp")),
        ),
        check_vma=False,
    )
```

```python
import functools
import math

import jax
import jax.numpy as jnp
from jax import lax
from jax.experimental import pallas as pl
from jax.experimental.pallas import tpu as pltpu
from jax.sharding import PartitionSpec as P

HEAD_DIM = 128
MESH = pl.DeviceIdType.MESH


def ring_scatter_kernel(jobs, produce, *refs):
    count = len(jobs)
    if produce:
        factors, refs = refs[:2 * produce], refs[2 * produce:]
        made, refs = refs[-1], refs[:-1]
        terms = (made,) + refs[:count - 1]
        outs, scratch = refs[count - 1:2 * count - 1], refs[2 * count - 1:]
        grads, weights = factors[:produce], factors[produce:]
    else:
        terms, outs, scratch = refs[:count], refs[count:2 * count], refs[2 * count:]
    barrier = pltpu.get_barrier_semaphore()
    places, greeted = [], 0
    for axis, n, _, direct in jobs:
        me = lax.axis_index(axis)
        right, left = lax.rem(me + 1, n), lax.rem(me + n - 1, n)
        places.append((me, right, left))
        offsets = range(1, n) if direct else (n - 1, 1)
        for offset in offsets:
            pl.semaphore_signal(
                barrier, inc=1, device_id={axis: lax.rem(me + offset, n)}, device_id_type=MESH
            )
        greeted += len(offsets)

    def make_block(block):
        block_rows = made.shape[2]
        rows = pl.ds(pl.multiple_of(block * block_rows, block_rows), block_rows)
        total = None
        for grad, weight in zip(grads, weights):
            part = lax.dot_general(
                grad[...], weight[rows, :], (((1,), (1,)), ((), ())),
                preferred_element_type=jnp.float32,
            )
            total = part if total is None else total + part
        made[block] = total

    if produce:
        me, n = places[0][0], jobs[0][1]
        make_block(lax.rem(me + n - 1, n))
        make_block(lax.rem(me + 1, n))
    pl.semaphore_wait(barrier, greeted)

    def direct_copy(job, offset):
        axis, n, _, _ = jobs[job]
        me = places[job][0]
        recv, send_sem, recv_sem = scratch[4 * job], scratch[4 * job + 2], scratch[4 * job + 3]
        peer = lax.rem(me + offset, n)
        return pltpu.make_async_remote_copy(
            src_ref=terms[job].at[peer],
            dst_ref=recv.at[me],
            send_sem=send_sem.at[offset],
            recv_sem=recv_sem.at[me],
            device_id={axis: peer},
            device_id_type=MESH,
        )

    for job, (axis, n, _, direct) in enumerate(jobs):
        if direct:
            for offset in range(1, n):
                direct_copy(job, offset).start()

    copies = [[[] for _ in range(2 * pieces)] for _, _, pieces, _ in jobs]
    for step in range(max(n for _, n, _, _ in jobs) - 1):
        for job, (axis, n, pieces, direct) in enumerate(jobs):
            if direct or step >= n - 1:
                continue
            me, right, left = places[job]
            if produce and job == 0 and 0 < step and 2 * (step + 1) <= n:
                make_block(lax.rem(me + n - (step + 1), n))
                if 2 * (step + 1) != n:
                    make_block(lax.rem(me + step + 1, n))
            recv, sendbuf, send_sem, recv_sem = scratch[4 * job:4 * job + 4]
            term_ref = terms[job]
            rows, half = outs[job].shape[0] // pieces, outs[job].shape[1] // 2
            for slot in range(2 * pieces):
                piece, way = divmod(slot, 2)
                dest, sign = ((right, -1), (left, 1))[way]
                block = lax.rem(me + n + sign * (step + 1), n)
                span = (pl.ds(piece * rows, rows), pl.ds(way * half, half))
                if step == 0:
                    src = term_ref.at[block, span[0], span[1]]
                else:
                    copies[job][slot][step - 1].wait_recv()
                    sendbuf[slot, step] = recv[slot, step - 1] + term_ref[block, span[0], span[1]]
                    src = sendbuf.at[slot, step]
                copy = pltpu.make_async_remote_copy(
                    src_ref=src,
                    dst_ref=recv.at[slot, step],
                    send_sem=send_sem.at[slot, step],
                    recv_sem=recv_sem.at[slot, step],
                    device_id={axis: dest},
                    device_id_type=MESH,
                )
                copy.start()
                copies[job][slot].append(copy)
    for job, (axis, n, pieces, direct) in enumerate(jobs):
        me = places[job][0]
        recv = scratch[4 * job]
        if direct:
            outs[job][...] = terms[job][me]
            for sender in range(n):
                @pl.when(sender != me)
                def _():
                    pltpu.make_async_remote_copy(
                        src_ref=terms[job].at[sender],
                        dst_ref=recv.at[sender],
                        send_sem=scratch[4 * job + 2].at[0],
                        recv_sem=scratch[4 * job + 3].at[sender],
                        device_id={axis: sender},
                        device_id_type=MESH,
                    ).wait_recv()
                    outs[job][...] += recv[sender]
            continue
        if produce and job == 0:
            make_block(me)
        rows, half = outs[job].shape[0] // pieces, outs[job].shape[1] // 2
        for slot in range(2 * pieces):
            piece, way = divmod(slot, 2)
            span = (pl.ds(piece * rows, rows), pl.ds(way * half, half))
            copies[job][slot][n - 2].wait_recv()
            outs[job][span[0], span[1]] = (
                recv[slot, n - 2] + terms[job][me, span[0], span[1]]
            ).astype(outs[job].dtype)
    for job, (axis, n, pieces, direct) in enumerate(jobs):
        if direct:
            for offset in range(1, n):
                direct_copy(job, offset).wait_send()
        for slot in range(2 * pieces):
            for copy in copies[job][slot]:
                copy.wait_send()


def ring_scatter(parts, channel, factors=None):
    jobs = tuple((axis, terms.shape[0], pieces, direct) for terms, axis, _, pieces, direct in parts)
    produce = len(factors[0]) if factors else 0
    scratch = []
    for terms, _, _, pieces, direct in parts:
        n, rows, width = terms.shape
        if direct:
            scratch += [
                pltpu.VMEM((n, rows, width), jnp.float32),
                pltpu.VMEM((8, 128), jnp.float32),
                pltpu.SemaphoreType.DMA((n,)),
                pltpu.SemaphoreType.DMA((n,)),
            ]
            continue
        scratch += [
            pltpu.VMEM((2 * pieces, n - 1, rows // pieces, width // 2), jnp.float32),
            pltpu.VMEM((2 * pieces, n - 1, rows // pieces, width // 2), jnp.float32),
            pltpu.SemaphoreType.DMA((2 * pieces, n - 1)),
            pltpu.SemaphoreType.DMA((2 * pieces, n - 1)),
        ]
    size = sum(math.prod(part[0].shape) for part in parts)
    operands = [part[0] for part in parts]
    if produce:
        scratch.append(pltpu.VMEM(parts[0][0].shape, jnp.float32))
        operands = list(factors[0]) + list(factors[1]) + operands[1:]
    return pl.pallas_call(
        functools.partial(ring_scatter_kernel, jobs, produce),
        out_shape=tuple(
            jax.ShapeDtypeStruct(part[0].shape[1:], part[2]) for part in parts
        ),
        in_specs=[pl.BlockSpec(memory_space=pltpu.VMEM)] * len(operands),
        out_specs=tuple(pl.BlockSpec(memory_space=pltpu.VMEM) for _ in parts),
        scratch_shapes=scratch,
        compiler_params=pltpu.CompilerParams(
            collective_id=channel, has_side_effects=True, vmem_limit_bytes=48 * 1024 * 1024
        ),
        cost_estimate=pl.CostEstimate(flops=2 * size, bytes_accessed=8 * size, transcendentals=0),
    )(*operands)


def exchange_kernel(n, axis, kv_ref, qg_ref, prefix_ref, suffix_ref,
                    pair_in, chip_sum, kv_in, qg_in, pair_sem, send_sem, recv_sem):
    me = lax.axis_index(axis)
    chips = n // 2
    chip, core = me // 2, lax.rem(me, 2)
    partner = me + 1 - 2 * core
    barrier = pltpu.get_barrier_semaphore()
    pl.semaphore_signal(barrier, inc=1, device_id={axis: partner}, device_id_type=MESH)
    for offset in range(1, chips):
        peer = lax.rem(chip + offset, chips) * 2 + core
        pl.semaphore_signal(barrier, inc=1, device_id={axis: peer}, device_id_type=MESH)
    pl.semaphore_wait(barrier, chips)

    swaps = []
    for kind, ref in enumerate((kv_ref, qg_ref)):
        swap = pltpu.make_async_remote_copy(
            src_ref=ref, dst_ref=pair_in.at[kind], send_sem=pair_sem.at[0, kind],
            recv_sem=pair_sem.at[1, kind], device_id={axis: partner}, device_id_type=MESH,
        )
        swap.start()
        swaps.append(swap)
    for swap in swaps:
        swap.wait_recv()
    chip_sum[0] = kv_ref[...] + pair_in[0]
    chip_sum[1] = qg_ref[...] + pair_in[1]

    def route(offset, later):
        peer = lax.rem(chip + offset, chips) * 2 + core
        kind = 0 if later else 1
        return pltpu.make_async_remote_copy(
            src_ref=chip_sum.at[kind],
            dst_ref=(kv_in if later else qg_in).at[chip],
            send_sem=send_sem.at[kind, offset],
            recv_sem=recv_sem.at[kind, chip],
            device_id={axis: peer},
            device_id_type=MESH,
        )

    for offset in range(1, chips):
        for later in (True, False):
            @pl.when((chip + offset < chips) == later)
            def _():
                route(offset, later).start()

    prefix_ref[...] = jnp.where(core == 1, pair_in[0], 0.0)
    suffix_ref[...] = jnp.where(core == 0, pair_in[1], 0.0)
    for sender in range(chips):
        @pl.when(sender < chip)
        def _():
            pltpu.make_async_remote_copy(
                src_ref=chip_sum.at[0], dst_ref=kv_in.at[sender], send_sem=send_sem.at[0, 0],
                recv_sem=recv_sem.at[0, sender], device_id={axis: sender * 2 + core},
                device_id_type=MESH,
            ).wait_recv()
            prefix_ref[...] += kv_in[sender]

        @pl.when(sender > chip)
        def _():
            pltpu.make_async_remote_copy(
                src_ref=chip_sum.at[1], dst_ref=qg_in.at[sender], send_sem=send_sem.at[1, 0],
                recv_sem=recv_sem.at[1, sender], device_id={axis: sender * 2 + core},
                device_id_type=MESH,
            ).wait_recv()
            suffix_ref[...] += qg_in[sender]

    for swap in swaps:
        swap.wait_send()
    for offset in range(1, chips):
        for later in (True, False):
            @pl.when((chip + offset < chips) == later)
            def _():
                route(offset, later).wait_send()


def exchange_states(kv_state, qg_state, axis):
    n = lax.axis_size(axis)
    chips = n // 2
    shape = kv_state.shape
    return pl.pallas_call(
        functools.partial(exchange_kernel, n, axis),
        out_shape=(jax.ShapeDtypeStruct(shape, jnp.float32),) * 2,
        in_specs=[pl.BlockSpec(memory_space=pltpu.VMEM)] * 2,
        out_specs=(pl.BlockSpec(memory_space=pltpu.VMEM),) * 2,
        scratch_shapes=[
            pltpu.VMEM((2,) + shape, jnp.float32),
            pltpu.VMEM((2,) + shape, jnp.float32),
            pltpu.VMEM((chips,) + shape, jnp.float32),
            pltpu.VMEM((chips,) + shape, jnp.float32),
            pltpu.SemaphoreType.DMA((2, 2)),
            pltpu.SemaphoreType.DMA((2, chips)),
            pltpu.SemaphoreType.DMA((2, chips)),
        ],
        compiler_params=pltpu.CompilerParams(collective_id=2, has_side_effects=True),
    )(kv_state, qg_state)


def local(layer_input, w_query, w_key, w_value, w_out, out_grad):
    num_rows = layer_input.shape[1]
    local_heads = w_query.shape[1] // HEAD_DIM
    width = local_heads * HEAD_DIM
    in_rows = layer_input[0]
    grad_rows = out_grad[0]

    def project(weight):
        result = jnp.dot(in_rows, weight, preferred_element_type=jnp.float32).astype(jnp.bfloat16)
        return result.reshape(num_rows, local_heads, HEAD_DIM)

    queries = project(w_query)
    key_rows = project(w_key)
    value_rows = project(w_value)
    row_start = lax.axis_index("seq") * num_rows
    positions = (row_start + jnp.arange(num_rows, dtype=jnp.int32)).astype(jnp.float32)
    pos_scale = 1.0 / jnp.sqrt(HEAD_DIM * (positions + 1.0))
    backward = jnp.einsum("td,kd->tk", grad_rows, w_out, preferred_element_type=jnp.float32)
    grad_in = (
        (backward * pos_scale[:, None])
        .astype(jnp.bfloat16)
        .reshape(num_rows, local_heads, HEAD_DIM)
    )
    kv_state = jnp.einsum("thd,the->hde", key_rows, value_rows, preferred_element_type=jnp.float32)
    qg_state = jnp.einsum("thd,the->hde", queries, grad_in, preferred_element_type=jnp.float32)
    prefix, suffix = exchange_states(kv_state, qg_state, "seq")
    prefix = prefix.astype(jnp.bfloat16)
    suffix = suffix.astype(jnp.bfloat16)
    causal = (jnp.arange(num_rows)[:, None] >= jnp.arange(num_rows)[None, :])[None]
    scores = jnp.einsum("thd,shd->hts", queries, key_rows, preferred_element_type=jnp.float32)
    scores_qk = jnp.where(causal, scores, 0.0).astype(jnp.bfloat16)
    scores_g = jnp.einsum("thd,shd->hts", grad_in, value_rows, preferred_element_type=jnp.float32)
    scores_gv = jnp.where(causal, scores_g, 0.0).astype(jnp.bfloat16)
    inner_sum = jnp.einsum(
        "hts,she->the", scores_qk, value_rows, preferred_element_type=jnp.float32
    )
    cross_sum = jnp.einsum("thd,hde->the", queries, prefix, preferred_element_type=jnp.float32)
    attention = (
        ((inner_sum + cross_sum) * pos_scale[:, None, None])
        .astype(jnp.bfloat16)
        .reshape(num_rows, width)
    )
    d_query = jnp.einsum("hts,shd->thd", scores_gv, key_rows, preferred_element_type=jnp.float32)
    d_query = d_query + jnp.einsum(
        "the,hde->thd", grad_in, prefix, preferred_element_type=jnp.float32
    )
    d_keys = jnp.einsum("hts,thd->shd", scores_gv, queries, preferred_element_type=jnp.float32)
    d_keys = d_keys + jnp.einsum(
        "she,hde->shd", value_rows, suffix, preferred_element_type=jnp.float32
    )
    d_values = jnp.einsum("hts,the->she", scores_qk, grad_in, preferred_element_type=jnp.float32)
    d_values = d_values + jnp.einsum(
        "shd,hde->she", key_rows, suffix, preferred_element_type=jnp.float32
    )
    d_query = d_query.astype(jnp.bfloat16).reshape(num_rows, width)
    d_keys = d_keys.astype(jnp.bfloat16).reshape(num_rows, width)
    d_values = d_values.astype(jnp.bfloat16).reshape(num_rows, width)
    groups = lax.axis_size("head")
    head_terms = jax.ShapeDtypeStruct((groups, num_rows, w_query.shape[0] // groups), jnp.float32)
    total_rows = lax.axis_size("seq") * lax.axis_size("dp") * num_rows
    grad_scale = jnp.float32(1.0) / jnp.sqrt(jnp.float32(total_rows))
    seqs, shares = lax.axis_size("seq"), lax.axis_size("dp")
    grads = jnp.concatenate([d_query, d_keys, d_values], axis=1)
    term_qkv = jnp.einsum("td,tk->dk", in_rows, grads, preferred_element_type=jnp.float32) * grad_scale
    grad_blocks = grad_rows.reshape(num_rows, seqs, shares, -1)
    term_out = jnp.einsum(
        "tspr,tk->psrk", grad_blocks, attention, preferred_element_type=jnp.float32
    ) * grad_scale
    term_out = term_out.reshape(shares, -1, width)
    factors = ((d_query, d_keys, d_values), (w_query, w_key, w_value))
    term_qkv, factors, term_out = lax.optimization_barrier((term_qkv, factors, term_out))
    summed = lax.psum_scatter(term_qkv, "seq", scatter_dimension=0, tiled=True)
    input_grad, out_shared = ring_scatter(
        [(head_terms, "head", jnp.float32, 4, False), (term_out, "dp", jnp.float32, 1, False)], 0,
        factors,
    )
    input_grad = input_grad.astype(jnp.bfloat16)[None]
    summed, input_grad, out_shared = lax.optimization_barrier((summed, input_grad, out_shared))
    summed, out_summed = ring_scatter(
        [
            (summed.reshape(shares, -1, summed.shape[1]), "dp", jnp.float32, 2, False),
            (out_shared.reshape(seqs, -1, width), "seq", jnp.float32, 1, True),
        ],
        1,
    )
    grad_query = summed[:, :width]
    grad_key = summed[:, width:2 * width]
    grad_value = summed[:, 2 * width:]
    grad_out = out_summed.T
    return (input_grad, grad_query, grad_key, grad_value, grad_out)


def solution(mesh):
    return jax.shard_map(
        local,
        mesh=mesh,
        in_specs=(
            P("dp", "seq", None),
            P(None, "head"),
            P(None, "head"),
            P(None, "head"),
            P("head", None),
            P("dp", "seq", None),
        ),
        out_specs=(
            P("dp", "seq", "head"),
            P(("seq", "dp"), "head"),
            P(("seq", "dp"), "head"),
            P(("seq", "dp"), "head"),
            P("head", ("seq", "dp")),
        ),
        check_vma=False,
    )
```
